32 devices in a mesh: dp: 8 (over z, y), tensor: 4 (over x, core).
Axes of the slice: x: 2, y: 2, z: 4, core: 2. Of those that a mesh axis runs over, the one named last changes fastest.
Arguments:
- hidden_in: bfloat16 [8, 1024, 1536], P('dp'), may hold values from -6 to 6
- conditioning: bfloat16 [8, 130, 768], P('dp'), may hold values from -6 to 6
- valid_mask: int32 [8, 1024], P('dp'), may hold values from 0 to 1, as said below
- teacher: bfloat16 [8, 1024, 1536], P('dp'), may hold values from -6 to 6
- gain_one: bfloat16 [1536], P('dp'), may hold values from 0.25 to 1.75
- gain_two: bfloat16 [1536], P('dp'), may hold values from 0.25 to 1.75
- gain_three: bfloat16 [1536], P('dp'), may hold values from 0.25 to 1.75
- self_in_weight: bfloat16 [1536, 3, 1536], P('dp', None, 'tensor'), may hold values from -0.15625 to 0.15625
- self_out_weight: bfloat16 [1536, 1536], P('tensor', 'dp'), may hold values from -1.25 to 1.25
- cross_query_weight: bfloat16 [1536, 1536], P('dp', 'tensor'), may hold values from -0.15625 to 0.15625
- cross_memory_weight: bfloat16 [768, 2, 1536], P('dp', None, 'tensor'), may hold values from -0.21875 to 0.21875
- cross_out_weight: bfloat16 [1536, 1536], P('tensor', 'dp'), may hold values from -0.625 to 0.625
- gate_up_weight: bfloat16 [1536, 2, 6144], P('dp', None, 'tensor'), may hold values from -0.15625 to 0.15625
- down_weight: bfloat16 [6144, 1536], P('tensor', 'dp'), may hold values from -0.078125 to 0.078125
Outputs:
- mean_loss: float32 [], replicated
- block_output: bfloat16 [8, 1024, 1536], P('dp')
- grad_hidden: float32 [8, 1024, 1536], P('dp')
- grad_conditioning: float32 [8, 130, 768], P('dp')
- grad_gain_one: float32 [1536], P('dp')
- grad_gain_two: float32 [1536], P('dp')
- grad_gain_three: float32 [1536], P('dp')
- grad_self_in: float32 [1536, 3, 1536], P('dp', None, 'tensor')
- grad_self_out: float32 [1536, 1536], P('tensor', 'dp')
- grad_cross_query: float32 [1536, 1536], P('dp', 'tensor')
- grad_cross_memory: float32 [768, 2, 1536], P('dp', None, 'tensor')
- grad_cross_out: float32 [1536, 1536], P('tensor', 'dp')
- grad_gate_up: float32 [1536, 2, 6144], P('dp', None, 'tensor')
- grad_down: float32 [6144, 1536], P('tensor', 'dp')
The draws below stay inside these ranges and needn't reach their ends.
Inputs may be any that keep to these rules, and one draw needn't show every extreme that they name: `valid_mask`: the valid tokens of each sequence form a prefix of it with at least one token.
All inputs are finite; a program needn't handle non-finite values.
Results may differ from the reference program's by a relative error of at most 0.018.
Values may be sent and summed in bfloat16 or wider, within the bound.
No kernel may reach another device: no remote copies, remote signals or barrier semaphores. Data moves between devices by JAX's collectives and lax.ppermute only.
A program may use at most 320 MiB of HBM per device.

```python
import math
import jax
import jax.numpy as jnp
from jax import lax

D = 1536
HEADS = 24
HEAD_DIM = 64
FF = 6144
COND_DIM = 768
COND_TOK = 130
ROT = 32
LENGTH = 1024
SEQS = 8


def draw_valid_mask(key, part):
    seq_index = jnp.arange(SEQS, dtype=jnp.int32)
    base_length = LENGTH // 3 + 2 * LENGTH // 3 * seq_index // max(SEQS - 1, 1)
    jitter = jax.random.randint(key, (SEQS,), 0, LENGTH // 16 + 1, dtype=jnp.int32)
    lengths = jnp.clip(base_length - jitter, 1, LENGTH)
    positions = jnp.arange(LENGTH, dtype=jnp.int32)
    return (positions[None, :] < lengths[:, None]).astype(jnp.int32)


def shard_levels(rng, extent, split, least, largest):
    def one(axis_at, shards_of):
        steps = jax.random.uniform(jax.random.fold_in(jax.random.fold_in(rng, 6), axis_at), (shards_of,), jnp.float32, least / len(split), largest / len(split))
        return jnp.repeat(jnp.exp(steps), extent[axis_at] // shards_of).reshape((-1,) + (1,) * (len(extent) - axis_at - 1))

    factor_of = one(*split[0])
    for cut in split[1:]:
        factor_of = factor_of * one(*cut)
    return factor_of


def gaussian(stream_key, dims, spread, bound, pieces=(), kind=jnp.bfloat16):
    values = spread * jax.random.normal(stream_key, dims, jnp.float32)
    if pieces:
        values = values * shard_levels(stream_key, dims, pieces, -0.22, 0.18)
    return jnp.clip(values, -bound, bound).astype(kind)


def setup_inputs(seed: int = 0) -> dict:
    key_list = jax.random.split(jax.random.key(seed), 15)
    hidden_in = gaussian(key_list[0], (SEQS, LENGTH, D), 1.0, 6.0, ((0, 8),))
    conditioning = gaussian(key_list[1], (SEQS, COND_TOK, COND_DIM), 1.0, 6.0, ((0, 8),))
    valid_mask = draw_valid_mask(jax.random.fold_in(key_list[14], 71), 0)
    teacher = gaussian(key_list[3], (SEQS, LENGTH, D), 1.0, 6.0, ((0, 8),))
    gain_one = jnp.clip(1.0 + 0.15 * jax.random.normal(key_list[4], (D,), jnp.float32), 0.25, 1.75).astype(jnp.bfloat16)
    gain_two = jnp.clip(1.0 + 0.15 * jax.random.normal(key_list[5], (D,), jnp.float32), 0.25, 1.75).astype(jnp.bfloat16)
    gain_three = jnp.clip(1.0 + 0.15 * jax.random.normal(key_list[6], (D,), jnp.float32), 0.25, 1.75).astype(jnp.bfloat16)
    self_in_weight = gaussian(key_list[7], (D, 3, D), D ** -0.5, 0.15625, ((0, 8), (2, 4)))
    self_out_weight = gaussian(key_list[8], (D, D), (D // 64) ** -0.5, 1.25, ((0, 4), (1, 8)))
    cross_query_weight = gaussian(key_list[9], (D, D), D ** -0.5, 0.15625, ((0, 8), (1, 4)))
    cross_memory_weight = gaussian(key_list[10], (COND_DIM, 2, D), COND_DIM ** -0.5, 0.21875, ((0, 8), (2, 4)))
    cross_out_weight = gaussian(key_list[11], (D, D), (D // 16) ** -0.5, 0.625, ((0, 4), (1, 8)))
    gate_up_weight = gaussian(key_list[12], (D, 2, FF), D ** -0.5, 0.15625, ((0, 8), (2, 4)))
    down_weight = gaussian(key_list[13], (FF, D), FF ** -0.5, 0.078125, ((0, 4), (1, 8)))
    return {"hidden_in": hidden_in, "conditioning": conditioning, "valid_mask": valid_mask, "teacher": teacher, "gain_one": gain_one, "gain_two": gain_two, "gain_three": gain_three, "self_in_weight": self_in_weight, "self_out_weight": self_out_weight, "cross_query_weight": cross_query_weight, "cross_memory_weight": cross_memory_weight, "cross_out_weight": cross_out_weight, "gate_up_weight": gate_up_weight, "down_weight": down_weight}


@jax.custom_vjp
def low(v):
    return lax.optimization_barrier(v.astype(jnp.bfloat16)).astype(jnp.float32)

@jax.custom_vjp
def low_back(v):
    return v

def low_keep(v):
    return (low(v), None)

def low_pass(kept, grad):
    return (grad,)

def back_keep(v):
    return (v, None)

def back_low(kept, grad):
    return (low(grad),)
low.defvjp(low_keep, low_pass)
low_back.defvjp(back_keep, back_low)
highest = lax.Precision.HIGHEST
masked_score = -1e+30

def layer_norm(inputs, norm_gain):
    centered = inputs - lax.optimization_barrier(jnp.mean(inputs, axis=-1, keepdims=True))
    inverse = lax.rsqrt(lax.optimization_barrier(jnp.mean(centered * centered, axis=-1, keepdims=True)) + 1e-05)
    return centered * inverse * norm_gain

def rotary_tables(length, rot_width):
    half_rot = rot_width // 2
    position = jnp.arange(length, dtype=jnp.float32)[:, None]
    frequency = jnp.exp(jnp.arange(half_rot, dtype=jnp.float32) * (-2.0 * math.log(10000.0) / rot_width))
    angles = position * frequency[None, :]
    return (jnp.cos(angles), jnp.sin(angles))

def rotate_heads(vectors, cos_table, sin_table):
    half_rot = cos_table.shape[-1]
    cos_wide = cos_table[:, None, :]
    sin_wide = sin_table[:, None, :]
    first_half = vectors[..., :half_rot]
    second_half = vectors[..., half_rot:2 * half_rot]
    return jnp.concatenate([first_half * cos_wide - second_half * sin_wide, second_half * cos_wide + first_half * sin_wide, vectors[..., 2 * half_rot:]], axis=-1)

def attention(queries, key_heads, values, key_valid):
    score_scale = 1.0 / math.sqrt(queries.shape[-1])
    scores = low_back(jnp.einsum('qhe,khe->hqk', queries, key_heads, precision=highest) * score_scale)
    if key_valid is not None:
        scores = jnp.where(key_valid[None, None, :], scores, masked_score)
    maxima = lax.optimization_barrier(jnp.max(scores, axis=-1, keepdims=True))
    exponent = jnp.exp(scores - maxima)
    weights_low = low(exponent / lax.optimization_barrier(jnp.sum(exponent, axis=-1, keepdims=True)))
    return low_back(low(jnp.einsum('hqk,khe->qhe', weights_low, values, precision=highest)))

def block_forward(hidden, cond_seq, key_valid, params, cos_table, sin_table):
    gain_first, gain_second, gain_third, self_in, self_out, cross_query, cross_mem, cross_out, gate_up_w, down_w = params
    length = hidden.shape[0]
    cond_tokens = cond_seq.shape[0]
    head_shape = (length, HEADS, HEAD_DIM)
    memory_shape = (cond_tokens, HEADS, HEAD_DIM)
    normed_one = low(layer_norm(hidden, gain_first))
    mixed_heads = jnp.einsum('td,dcf->tcf', normed_one, self_in, precision=highest)
    queries = low(rotate_heads(low_back(mixed_heads[:, 0]).reshape(head_shape), cos_table, sin_table))
    key_heads = low(rotate_heads(low_back(mixed_heads[:, 1]).reshape(head_shape), cos_table, sin_table))
    values = low(low_back(mixed_heads[:, 2])).reshape(head_shape)
    attended = attention(queries, key_heads, values, key_valid).reshape(length, D)
    after_self = hidden + low_back(jnp.dot(attended, self_out, precision=highest))
    normed_two = low(layer_norm(after_self, gain_second))
    cross_queries = low(low_back(jnp.dot(normed_two, cross_query, precision=highest))).reshape(head_shape)
    cross_memory = jnp.einsum('cd,dsf->csf', cond_seq, cross_mem, precision=highest)
    cross_keys = low(low_back(cross_memory[:, 0])).reshape(memory_shape)
    cross_values = low(low_back(cross_memory[:, 1])).reshape(memory_shape)
    cross_attended = attention(cross_queries, cross_keys, cross_values, None).reshape(length, D)
    after_cross = after_self + low_back(jnp.dot(cross_attended, cross_out, precision=highest))
    normed_three = low(layer_norm(after_cross, gain_third))
    gate_up = jnp.einsum('td,dsf->tsf', normed_three, gate_up_w, precision=highest)
    gate_value = low_back(gate_up[:, 0])
    upward = low_back(gate_up[:, 1])
    hidden_units = low(gate_value * jax.nn.sigmoid(gate_value) * upward)
    return after_cross + low_back(jnp.dot(hidden_units, down_w, precision=highest))

def reference(hidden_in, conditioning, valid_mask, teacher, gain_one, gain_two, gain_three, self_in_weight, self_out_weight, cross_query_weight, cross_memory_weight, cross_out_weight, gate_up_weight, down_weight):
    params = tuple((weight.astype(jnp.float32) for weight in (gain_one, gain_two, gain_three, self_in_weight, self_out_weight, cross_query_weight, cross_memory_weight, cross_out_weight, gate_up_weight, down_weight)))
    token_count = jnp.sum(valid_mask.astype(jnp.float32))
    cos_table, sin_table = rotary_tables(LENGTH, ROT)

    def one_sequence(running, packed):
        loss_sum, grad_sums = running
        hidden, cond_seq, mask_row, target = packed
        mask_float = mask_row.astype(jnp.float32)
        target_float = target.astype(jnp.float32)
        key_valid = mask_row > 0

        def scaled_error(hidden_float, cond_float, weights):
            final_state = block_forward(hidden_float, cond_float, key_valid, weights, cos_table, sin_table)
            difference = final_state - target_float
            return (final_state, jnp.sum(mask_float * lax.optimization_barrier(jnp.sum(difference * difference, axis=-1))))
        (final_state, error_sum), pullback = jax.vjp(scaled_error, hidden.astype(jnp.float32), cond_seq.astype(jnp.float32), params)
        grad_input, grad_cond, grad_weights = pullback((jnp.zeros_like(final_state), LENGTH / token_count))
        grad_sums = jax.tree.map(lambda summed, addend: summed + addend, grad_sums, grad_weights)
        return ((loss_sum + error_sum, grad_sums), (final_state.astype(jnp.bfloat16), grad_input, grad_cond))
    zero_grads = tuple((jnp.zeros(weight.shape, jnp.float32) for weight in params))
    (loss_sum, grad_sums), (block_output, grad_hidden, grad_conditioning) = lax.scan(one_sequence, (jnp.zeros((), jnp.float32), zero_grads), (hidden_in, conditioning, valid_mask, teacher))
    mean_loss = loss_sum / (token_count * D)
    return (mean_loss, block_output, grad_hidden, grad_conditioning, grad_sums[0], grad_sums[1], grad_sums[2], grad_sums[3], grad_sums[4], grad_sums[5], grad_sums[6], grad_sums[7], grad_sums[8], grad_sums[9])
```

```python
import math

import jax
import jax.numpy as jnp
from jax import lax
from jax.sharding import PartitionSpec as P

HEAD_DIM = 64
ROT = 32
CHUNKS = 1

epsilon = 1e-05
masked_score = -1e30
F32 = jnp.float32
BF16 = jnp.bfloat16


def low(x):
    return x.astype(BF16)


def wide(x):
    return x.astype(F32)


def dot(a, b):
    return lax.dot_general(a, b, (((1,), (0,)), ((), ())), preferred_element_type=F32)


def dot_nt(a, b):
    return lax.dot_general(a, b, (((1,), (1,)), ((), ())), preferred_element_type=F32)


def dot_tn(a, b):
    return lax.dot_general(a, b, (((0,), (0,)), ((), ())), preferred_element_type=F32)


def norm_forward(inputs, norm_gain):
    centered = inputs - jnp.mean(inputs, axis=-1, keepdims=True)
    inverse = lax.rsqrt(jnp.mean(centered * centered, axis=-1, keepdims=True) + epsilon)
    scaled = centered * inverse
    return (low(scaled * norm_gain), scaled, inverse)


def norm_backward(upstream, scaled, inverse, norm_gain):
    gain_grad = jnp.sum(upstream * scaled, axis=0)
    weighted = upstream * norm_gain
    centered_grad = weighted - jnp.mean(weighted, axis=-1, keepdims=True)
    input_grad = inverse * (
        centered_grad - scaled * jnp.mean(weighted * scaled, axis=-1, keepdims=True)
    )
    return (input_grad, gain_grad)


def rotate_heads(vectors, cos_table, sin_table):
    half_rot = cos_table.shape[-1]
    cos_wide = cos_table[:, None, :]
    sin_wide = sin_table[:, None, :]
    first_half = vectors[..., :half_rot]
    second_half = vectors[..., half_rot : 2 * half_rot]
    return jnp.concatenate(
        [
            first_half * cos_wide - second_half * sin_wide,
            second_half * cos_wide + first_half * sin_wide,
            vectors[..., 2 * half_rot :],
        ],
        axis=-1,
    )


def masked_scores(query_block, key_heads, key_valid):
    score_scale = 1.0 / math.sqrt(query_block.shape[-1])
    scores = jnp.einsum("qhe,khe->hqk", query_block, key_heads, preferred_element_type=F32)
    scores = scores * score_scale
    if key_valid is not None:
        scores = jnp.where(key_valid[None, None, :], scores, masked_score)
    return scores


def attend_forward(queries, key_heads, values, key_valid):
    scores = masked_scores(queries, key_heads, key_valid)
    maxima = jnp.max(scores, axis=-1, keepdims=True)
    exponent = jnp.exp(scores - maxima)
    denominator = jnp.sum(exponent, axis=-1, keepdims=True)
    weights_low = low(exponent / denominator)
    out = jnp.einsum("hqk,khe->qhe", weights_low, values, preferred_element_type=F32)
    return low(out), maxima + jnp.log(denominator)


def attend_backward(queries, key_heads, values, key_valid, log_totals, grad_out):
    score_scale = 1.0 / math.sqrt(queries.shape[-1])
    scores = masked_scores(queries, key_heads, key_valid)
    weights_full = jnp.exp(scores - log_totals)
    weights_low = low(weights_full)
    grad_values = jnp.einsum("hqk,qhe->khe", weights_low, grad_out, preferred_element_type=F32)
    grad_weights = jnp.einsum("qhe,khe->hqk", grad_out, values, preferred_element_type=F32)
    inner_sum = jnp.sum(weights_full * grad_weights, axis=-1, keepdims=True)
    grad_scores = low(weights_full * (grad_weights - inner_sum))
    grad_queries = (
        jnp.einsum("hqk,khe->qhe", grad_scores, key_heads, preferred_element_type=F32)
        * score_scale
    )
    grad_keys = (
        jnp.einsum("hqk,qhe->khe", grad_scores, queries, preferred_element_type=F32) * score_scale
    )
    return grad_queries, grad_keys, grad_values


def after(value, *tokens):
    return lax.optimization_barrier((value,) + tokens)[0]


def build(n_dp, n_tensor):
    n_ring = n_dp // 2
    tensor_bits = []
    bit = 1
    while bit < n_tensor:
        tensor_bits.append(bit)
        bit *= 2
    dp_bits = []
    bit = 1
    while bit < n_dp:
        dp_bits.append(bit)
        bit *= 2
    order = [0]
    for bit in reversed(tensor_bits):
        order = order + [o ^ bit for o in order]

    def swap(x, bit):
        return lax.ppermute(x, "tensor", [(i, i ^ bit) for i in range(n_tensor)])

    def swap_dp(x, bit):
        return lax.ppermute(x, "dp", [(i, i ^ bit) for i in range(n_dp)])

    def pair(x):
        return swap_dp(x, 1)

    def ring(x):
        return lax.ppermute(x, "dp", [(i, (i - 2) % n_dp) for i in range(n_dp)])

    def gather_rows(own):
        for bit in reversed(tensor_bits):
            own = jnp.concatenate([own, swap(own, bit)], axis=0)
        return own

    def scatter_rows(make, rows):
        half = rows // 2
        sent = low(make(half, rows))
        got = swap(sent, tensor_bits[0])
        total = make(0, half) + wide(got)
        for bit in tensor_bits[1:]:
            half = half // 2
            total = total[:half] + wide(swap(low(total[half:]), bit))
        return total

    def sum_tensor(x):
        for bit in tensor_bits:
            x = x + swap(x, bit)
        return x

    def sum_dp(x):
        for bit in dp_bits:
            x = x + swap_dp(x, bit)
        return x

    def body(
        hidden_in,
        conditioning,
        valid_mask,
        teacher,
        gain_one,
        gain_two,
        gain_three,
        self_in_weight,
        self_out_weight,
        cross_query_weight,
        cross_memory_weight,
        cross_out_weight,
        gate_up_weight,
        down_weight,
    ):
        _, length, width = hidden_in.shape
        cond_tokens, cond_width = conditioning.shape[1:]
        me = lax.axis_index("tensor")
        dp_me = lax.axis_index("dp")
        ring_me = dp_me // 2
        pair_me = dp_me % 2
        shard = width // n_dp
        chunk_rows = length // CHUNKS
        own_rows = chunk_rows // n_tensor

        def gather_dp(own, token):
            rows = own.shape[0]
            full = jnp.zeros((n_dp * rows,) + own.shape[1:], own.dtype)
            own = after(own, token)
            block = own
            for step in range(n_ring):
                other = pair(block)
                at = ((ring_me + step) % n_ring) * 2
                nxt = ring(block) if step < n_ring - 1 else None
                full = lax.dynamic_update_slice_in_dim(full, block, (at + pair_me) * rows, 0)
                full = lax.dynamic_update_slice_in_dim(full, other, (at + 1 - pair_me) * rows, 0)
                if step == n_ring - 2:
                    token = block
                if nxt is not None:
                    block = nxt
            return full, token

        def reduce_dp(grad, token=None):
            rows = grad.shape[0] // n_dp

            def part(ring_at, pair_at):
                return lax.dynamic_slice_in_dim(grad, (ring_at * 2 + pair_at) * rows, rows, 0)

            total = None
            for step in range(n_ring):
                at = (ring_me + step + 1) % n_ring
                other = pair(part(at, 1 - pair_me))
                here = wide(part(at, pair_me)) + wide(other)
                total = here if total is None else here + wide(total)
                if step < n_ring - 1:
                    total = ring(low(total))
            return total

        gains = jnp.zeros((3, n_dp, shard), BF16)
        gains_own = jnp.stack([gain_one, gain_two, gain_three])[:, None, :]
        gains = lax.dynamic_update_slice_in_dim(gains, gains_own, dp_me, 1)
        gains = sum_dp(gains).reshape(3, width)
        gain_first, gain_second, gain_third = wide(gains[0]), wide(gains[1]), wide(gains[2])

        local = self_in_weight.shape[2]
        heads = local // HEAD_DIM
        ff = down_weight.shape[0]
        token = gain_one
        full_self_in, token = gather_dp(self_in_weight.reshape(shard, 3 * local), token)
        small = jnp.stack(
            [
                self_out_weight.T,
                cross_query_weight,
                cross_out_weight.T,
                cross_memory_weight.reshape(shard, local),
            ],
            axis=1,
        ).reshape(shard, 4 * local)
        full_small, token = gather_dp(small, token)
        full_self_out = full_small[:, :local]
        full_cross_query = full_small[:, local : 2 * local]
        full_cross_out = full_small[:, 2 * local : 3 * local]
        full_memory = full_small[:, 3 * local :].reshape(cond_width, 2 * local)
        full_gate_up, token = gather_dp(gate_up_weight.reshape(shard, 2 * ff), token)
        full_down, token = gather_dp(down_weight.T, token)

        token_count = sum_dp(jnp.sum(wide(valid_mask)).reshape(1, 1))[0, 0]

        def take(x, chunk, owner):
            at = chunk * chunk_rows + owner * own_rows
            return lax.dynamic_slice_in_dim(x, at, own_rows, 0)

        def relative(x):
            return jnp.concatenate(
                [take(x, c, me ^ o) for c in range(CHUNKS) for o in order], axis=0
            )

        position = relative(jnp.arange(length, dtype=F32)[:, None])
        frequency = jnp.exp(
            jnp.arange(ROT // 2, dtype=F32) * (-2.0 * math.log(10000.0) / ROT)
        )
        angles = position * frequency[None, :]
        cos_table, sin_table = jnp.cos(angles), jnp.sin(angles)
        key_valid = relative(valid_mask[0][:, None])[:, 0] > 0

        residual = wide(relative(hidden_in[0]))
        normed_one, scaled_all, inverse_all = norm_forward(residual, gain_first)
        mixed = dot(normed_one, full_self_in)
        head_shape = (length, heads, HEAD_DIM)
        queries = low(rotate_heads(mixed[:, :local].reshape(head_shape), cos_table, sin_table))
        key_heads = low(
            rotate_heads(mixed[:, local : 2 * local].reshape(head_shape), cos_table, sin_table)
        )
        values = low(mixed[:, 2 * local :].reshape(head_shape))

        memory_input = conditioning[0]
        cross_memory = low(dot(memory_input, full_memory))
        memory_shape = (cond_tokens, heads, HEAD_DIM)
        cross_keys = cross_memory[:, :local].reshape(memory_shape)
        cross_values = cross_memory[:, local:].reshape(memory_shape)

        chunks = []
        for c in range(CHUNKS):
            rows = slice(c * chunk_rows, (c + 1) * chunk_rows)
            mine = slice(c * chunk_rows, c * chunk_rows + own_rows)
            attended, self_totals = attend_forward(queries[rows], key_heads, values, key_valid)
            attended = attended.reshape(chunk_rows, local)
            after_self = residual[mine] + scatter_rows(
                lambda a, b: dot_nt(attended[a:b], full_self_out), chunk_rows
            )
            normed_share, scaled_two, inverse_two = norm_forward(after_self, gain_second)
            normed_two = gather_rows(normed_share)
            cross_queries = low(dot(normed_two, full_cross_query)).reshape(-1, heads, HEAD_DIM)
            cross_attended, cross_totals = attend_forward(
                cross_queries, cross_keys, cross_values, None
            )
            cross_attended = cross_attended.reshape(chunk_rows, local)
            after_cross = after_self + scatter_rows(
                lambda a, b: dot_nt(cross_attended[a:b], full_cross_out), chunk_rows
            )
            normed_share, scaled_three, inverse_three = norm_forward(after_cross, gain_third)
            normed_three = gather_rows(normed_share)
            gate_up = dot(normed_three, full_gate_up)
            gate_value = gate_up[:, :ff]
            upward = gate_up[:, ff:]
            sigmoid_gate = jax.nn.sigmoid(gate_value)
            hidden_units = low(gate_value * sigmoid_gate * upward)
            final_state = after_cross + scatter_rows(
                lambda a, b: dot_nt(hidden_units[a:b], full_down), chunk_rows
            )
            chunks.append(
                dict(
                    attended=attended,
                    self_totals=self_totals,
                    scaled_two=scaled_two,
                    inverse_two=inverse_two,
                    normed_two=normed_two,
                    cross_queries=cross_queries,
                    cross_attended=cross_attended,
                    cross_totals=cross_totals,
                    scaled_three=scaled_three,
                    inverse_three=inverse_three,
                    normed_three=normed_three,
                    gate_value=gate_value,
                    upward=upward,
                    sigmoid_gate=sigmoid_gate,
                    hidden_units=hidden_units,
                    final_state=final_state,
                )
            )

        losses = 0.0
        gain_three_sum = 0.0
        gain_two_sum = 0.0
        for c, k in enumerate(chunks):
            target = wide(take(teacher[0], c, me))
            valid_rows = wide(take(valid_mask[0][:, None], c, me))
            difference = k["final_state"] - target
            losses += jnp.sum(valid_rows[:, 0] * jnp.sum(difference * difference, axis=-1))
            grad_final = 2.0 * length / token_count * valid_rows * difference
            grad_final_low = gather_rows(low(grad_final))
            k["grad_final_low"] = grad_final_low
            grad_hidden_units = dot(grad_final_low, full_down)
            gate_value, upward, s = k["gate_value"], k["upward"], k["sigmoid_gate"]
            grad_gate = grad_hidden_units * upward * s * (1.0 + gate_value * (1.0 - s))
            grad_upward = grad_hidden_units * gate_value * s
            grad_gate_low = jnp.concatenate([low(grad_gate), low(grad_upward)], axis=1)
            k["grad_gate_low"] = grad_gate_low
            grad_normed = scatter_rows(
                lambda a, b: dot_nt(grad_gate_low[a:b], full_gate_up), chunk_rows
            )
            grad_part, gain_part = norm_backward(
                grad_normed, k["scaled_three"], k["inverse_three"], gain_third
            )
            gain_three_sum += gain_part
            k["grad_after_cross"] = grad_final + grad_part

        def whole(name):
            if CHUNKS == 1:
                return chunks[0][name]
            return jnp.concatenate([k[name] for k in chunks], axis=0)

        grad_down = reduce_dp(low(dot_tn(whole("grad_final_low"), whole("hidden_units"))))
        grad_gate_up = reduce_dp(low(dot_tn(whole("normed_three"), whole("grad_gate_low"))))

        grad_keys_sum = 0.0
        grad_values_sum = 0.0
        for c, k in enumerate(chunks):
            grad_cross_low = gather_rows(low(k["grad_after_cross"]))
            k["grad_cross_low"] = grad_cross_low
            grad_cross_attended = low(dot(grad_cross_low, full_cross_out)).reshape(
                -1, heads, HEAD_DIM
            )
            grad_cross_queries, grad_keys, grad_values = attend_backward(
                k["cross_queries"],
                cross_keys,
                cross_values,
                None,
                k["cross_totals"],
                grad_cross_attended,
            )
            grad_keys_sum += grad_keys
            grad_values_sum += grad_values
            grad_cross_queries = low(grad_cross_queries.reshape(chunk_rows, local))
            k["grad_cross_queries"] = grad_cross_queries
            grad_normed = scatter_rows(
                lambda a, b: dot_nt(grad_cross_queries[a:b], full_cross_query), chunk_rows
            )
            grad_part, gain_part = norm_backward(
                grad_normed, k["scaled_two"], k["inverse_two"], gain_second
            )
            gain_two_sum += gain_part
            k["grad_after_self"] = k["grad_after_cross"] + grad_part

        grad_memory_low = jnp.concatenate(
            [
                low(grad_keys_sum.reshape(cond_tokens, local)),
                low(grad_values_sum.reshape(cond_tokens, local)),
            ],
            axis=1,
        )
        grad_memory_full = low(dot_tn(memory_input, grad_memory_low)).reshape(width, local)
        grad_conditioning = sum_tensor(dot_nt(grad_memory_low, full_memory))
        cross_out_full = low(dot_tn(whole("grad_cross_low"), whole("cross_attended")))
        cross_query_full = low(dot_tn(whole("normed_two"), whole("grad_cross_queries")))
        grad_cross = reduce_dp(
            jnp.concatenate([cross_out_full, cross_query_full, grad_memory_full], axis=1)
        )

        grad_query_parts = []
        grad_keys_sum = 0.0
        grad_values_sum = 0.0
        for c, k in enumerate(chunks):
            rows = slice(c * chunk_rows, (c + 1) * chunk_rows)
            grad_self_low = gather_rows(low(k["grad_after_self"]))
            k["grad_self_low"] = grad_self_low
            grad_attended = low(dot(grad_self_low, full_self_out)).reshape(-1, heads, HEAD_DIM)
            grad_queries, grad_keys, grad_values = attend_backward(
                queries[rows], key_heads, values, key_valid, k["self_totals"], grad_attended
            )
            grad_query_parts.append(grad_queries)
            grad_keys_sum += grad_keys
            grad_values_sum += grad_values
        grad_self_out = reduce_dp(low(dot_tn(whole("grad_self_low"), whole("attended"))))
        grad_queries = jnp.concatenate(grad_query_parts, axis=0)
        grad_queries = rotate_heads(grad_queries, cos_table, -sin_table)
        grad_keys = rotate_heads(grad_keys_sum, cos_table, -sin_table)
        grad_mixed_low = jnp.concatenate(
            [
                low(grad_queries.reshape(length, local)),
                low(grad_keys.reshape(length, local)),
                low(grad_values_sum.reshape(length, local)),
            ],
            axis=1,
        )
        grad_self_in = reduce_dp(low(dot_tn(normed_one, grad_mixed_low)))
        gain_one_sum = 0.0
        grad_hidden = jnp.zeros((length, width), F32)
        block_output = jnp.zeros((length, width), BF16)
        for c, k in enumerate(chunks):
            base = c * chunk_rows
            mine = slice(base, base + own_rows)
            grad_normed = scatter_rows(
                lambda a, b: dot_nt(grad_mixed_low[base + a : base + b], full_self_in), chunk_rows
            )
            grad_part, gain_part = norm_backward(
                grad_normed, scaled_all[mine], inverse_all[mine], gain_first
            )
            gain_one_sum += gain_part
            rows_hidden = gather_rows(low(k["grad_after_self"] + grad_part))
            rows_output = gather_rows(low(k["final_state"]))
            for place, owner in enumerate(order):
                at = base + (me ^ owner) * own_rows
                piece = slice(place * own_rows, (place + 1) * own_rows)
                grad_hidden = lax.dynamic_update_slice_in_dim(
                    grad_hidden, wide(rows_hidden[piece]), at, 0
                )
                block_output = lax.dynamic_update_slice_in_dim(
                    block_output, rows_output[piece], at, 0
                )

        lossrow = jnp.zeros((width,), F32).at[0].set(losses)
        sums = sum_dp(
            sum_tensor(jnp.stack([gain_one_sum, gain_two_sum, gain_three_sum, lossrow]))
        )
        mean_loss = sums[3, 0] / (token_count * width)

        def mine_dp(row):
            return lax.dynamic_slice_in_dim(row, dp_me * shard, shard, 0)

        return (
            mean_loss,
            block_output[None],
            grad_hidden[None],
            grad_conditioning[None],
            mine_dp(sums[0]),
            mine_dp(sums[1]),
            mine_dp(sums[2]),
            grad_self_in.reshape(shard, 3, local),
            grad_self_out.T,
            grad_cross[:, local : 2 * local],
            grad_cross[:, 2 * local :].reshape(cond_width // n_dp, 2, local),
            grad_cross[:, :local].T,
            grad_gate_up.reshape(shard, 2, ff),
            grad_down.T,
        )

    return body


def solution(mesh):
    return jax.shard_map(
        build(mesh.shape["dp"], mesh.shape["tensor"]),
        mesh=mesh,
        in_specs=(
            P("dp", None, None),
            P("dp", None, None),
            P("dp", None),
            P("dp", None, None),
            P("dp"),
            P("dp"),
            P("dp"),
            P("dp", None, "tensor"),
            P("tensor", "dp"),
            P("dp", "tensor"),
            P("dp", None, "tensor"),
            P("tensor", "dp"),
            P("dp", None, "tensor"),
            P("tensor", "dp"),
        ),
        out_specs=(
            P(),
            P("dp", None, None),
            P("dp", None, None),
            P("dp", None, None),
            P("dp"),
            P("dp"),
            P("dp"),
            P("dp", None, "tensor"),
            P("tensor", "dp"),
            P("dp", "tensor"),
            P("dp", None, "tensor"),
            P("tensor", "dp"),
            P("dp", None, "tensor"),
            P("tensor", "dp"),
        ),
        check_vma=False,
    )
```

```python
import functools
import math

import jax
import jax.numpy as jnp
from jax import lax
from jax.experimental import pallas as pl
from jax.experimental.pallas import tpu as pltpu
from jax.sharding import PartitionSpec as P

HEAD_DIM = 64
ROT = 32
CHUNKS = 1

epsilon = 1e-05
masked_score = -1e30
F32 = jnp.float32
BF16 = jnp.bfloat16


def low(x):
    return x.astype(BF16)


def wide(x):
    return x.astype(F32)


def dot(a, b):
    return lax.dot_general(a, b, (((1,), (0,)), ((), ())), preferred_element_type=F32)


def dot_nt(a, b):
    return lax.dot_general(a, b, (((1,), (1,)), ((), ())), preferred_element_type=F32)


def dot_tn(a, b):
    return lax.dot_general(a, b, (((0,), (0,)), ((), ())), preferred_element_type=F32)


PAIR=128
SCALE=1.0/math.sqrt(HEAD_DIM)
SCALE2=SCALE*math.log2(math.e)

def mm(a,b): return lax.dot_general(a,b,(((1,),(0,)),((),())),preferred_element_type=F32)
def mm_nt(a,b): return lax.dot_general(a,b,(((1,),(1,)),((),())),preferred_element_type=F32)

def head_lanes(shape, axis, head):
    at = lax.broadcasted_iota(jnp.int32, shape, axis)
    return (at >= head*HEAD_DIM) & (at < (head+1)*HEAD_DIM)

def keep_head(x, axis, head):
    return jnp.where(head_lanes(x.shape, axis, head), x, jnp.zeros_like(x))

def with_lane(x, head, lane_value):
    at = lax.broadcasted_iota(jnp.int32, x.shape, 1)
    other = (1-head)*HEAD_DIM
    return jnp.where(at == other, lane_value, keep_head(x, 1, head))

def fwd_kernel(q_ref, k_ref, v_ref, bias_ref, o_ref, lse_ref, k_sc, vt_sc):
    @pl.when(pl.program_id(1) == 0)
    def _():
        k = k_ref[...].astype(F32)
        vt = v_ref[...].astype(F32).T
        for h in range(2):
            k_sc[h] = with_lane(k, h, bias_ref[...]).astype(BF16)
            vt_sc[h] = keep_head(vt, 0, h).astype(BF16)
    q = q_ref[...].astype(F32)
    out = None
    for h in range(2):
        qh = with_lane(q, h, 1.0).astype(BF16)
        s = mm_nt(k_sc[h], qh)
        m = jnp.max(s, axis=0, keepdims=True)
        e = jnp.exp2((s - m) * SCALE2)
        l = jnp.sum(e, axis=0, keepdims=True)
        o = mm(vt_sc[h], e.astype(BF16)) * (1.0 / l)
        out = o if out is None else out + o
        lse_ref[0, h:h+1, :] = m * SCALE2 + jnp.log2(l)
    o_ref[...] = out.T.astype(BF16)

def bwd_kernel(q_ref, k_ref, v_ref, bias_ref, lse_ref, g_ref, *rest, rotary):
    if rotary:
        cosq_ref, sinq_ref, cosk_ref, sink_ref, dq_ref, dk_ref, dv_ref, k_sc, kt_sc, v_sc, dk_sc, dv_sc = rest
    else:
        dq_ref, dk_ref, dv_ref, k_sc, kt_sc, v_sc, dk_sc, dv_sc = rest
    i = pl.program_id(1)
    @pl.when(i == 0)
    def _():
        k = k_ref[...].astype(F32)
        kt = k.T
        for h in range(2):
            k_sc[h] = with_lane(k, h, bias_ref[...]).astype(BF16)
            kt_sc[h] = keep_head(kt, 0, h).astype(BF16)
            v_sc[h] = keep_head(v_ref[...].astype(F32), 1, h).astype(BF16)
        dk_sc[...] = jnp.zeros_like(dk_sc)
        dv_sc[...] = jnp.zeros_like(dv_sc)
    q = q_ref[...].astype(F32)
    g32 = g_ref[...].astype(F32)
    g = g_ref[...]
    dqt = None
    dk = dk_sc[...]
    dv = dv_sc[...]
    for h in range(2):
        qa = with_lane(q, h, 1.0).astype(BF16)
        qh = keep_head(q, 1, h).astype(BF16)
        gh = keep_head(g32, 1, h).astype(BF16)
        s = mm_nt(k_sc[h], qa)
        p = jnp.exp2(s * SCALE2 - lse_ref[0, h:h+1, :])
        dp = mm_nt(v_sc[h], g)
        t = p * dp
        delta = jnp.sum(t, axis=0, keepdims=True)
        ds = (t - p * delta).astype(BF16)
        dv = dv + mm(p.astype(BF16), gh)
        dk = dk + mm(ds, qh)
        d = mm(kt_sc[h], ds)
        dqt = d if dqt is None else dqt + d
    dk_sc[...] = dk
    dv_sc[...] = dv
    dq = dqt.T * SCALE
    if rotary:
        dq = turn_back(dq, cosq_ref[...], sinq_ref[...])
    dq_ref[...] = dq.astype(BF16)
    @pl.when(i == pl.num_programs(1) - 1)
    def _():
        dk = dk_sc[...] * SCALE
        if rotary:
            dk = turn_back(dk, cosk_ref[...], sink_ref[...])
        dk_ref[...] = dk.astype(BF16)
        dv_ref[...] = dv_sc[...].astype(BF16)

def swap_halves(x):
    n = x.shape[1]
    at = lax.broadcasted_iota(jnp.int32, x.shape, 1) % HEAD_DIM
    return jnp.where(at < 16, pltpu.roll(x, n - 16, 1), pltpu.roll(x, 16, 1))

def turn(x, cos, sin):
    return x * cos + swap_halves(x) * sin

def turn_back(x, cos, sin):
    return x * cos - swap_halves(x) * sin

def attend_forward(q, k, v, qcol, kcol, vcol, bias, pairs, block):
    rows = q.shape[0]; keys = k.shape[0]
    return pl.pallas_call(
        fwd_kernel,
        grid=(pairs, rows//block),
        in_specs=[
            pl.BlockSpec((block,PAIR), lambda p,i:(i,qcol+p)),
            pl.BlockSpec((keys,PAIR), lambda p,i:(0,kcol+p)),
            pl.BlockSpec((keys,PAIR), lambda p,i:(0,vcol+p)),
            pl.BlockSpec((keys,1), lambda p,i:(0,0)),
        ],
        out_specs=[
            pl.BlockSpec((block,PAIR), lambda p,i:(i,p)),
            pl.BlockSpec((1,8,block), lambda p,i:(p,0,i)),
        ],
        out_shape=[jax.ShapeDtypeStruct((rows,pairs*PAIR),BF16), jax.ShapeDtypeStruct((pairs,8,rows),F32)],
        scratch_shapes=[pltpu.VMEM((2,keys,PAIR),BF16), pltpu.VMEM((2,PAIR,keys),BF16)],
        compiler_params=pltpu.CompilerParams(vmem_limit_bytes=48<<20),
        cost_estimate=pl.CostEstimate(flops=4*rows*keys*PAIR*pairs*2, bytes_accessed=2*(2*rows+2*keys)*PAIR*pairs, transcendentals=rows*keys*2*pairs),
    )(q,k,v,bias)

def attend_backward(q, k, v, qcol, kcol, vcol, bias, lse, g, tables, pairs, block):
    rows = q.shape[0]; keys = k.shape[0]
    rotary = tables is not None
    in_specs=[
        pl.BlockSpec((block,PAIR), lambda p,i:(i,qcol+p)),
        pl.BlockSpec((keys,PAIR), lambda p,i:(0,kcol+p)),
        pl.BlockSpec((keys,PAIR), lambda p,i:(0,vcol+p)),
        pl.BlockSpec((keys,1), lambda p,i:(0,0)),
        pl.BlockSpec((1,8,block), lambda p,i:(p,0,i)),
        pl.BlockSpec((block,PAIR), lambda p,i:(i,p)),
    ]
    args=[q,k,v,bias,lse,g]
    if rotary:
        in_specs += [pl.BlockSpec((block,PAIR), lambda p,i:(i,0))]*2 + [pl.BlockSpec((keys,PAIR), lambda p,i:(0,0))]*2
        args += [tables[0],tables[1],tables[0],tables[1]]
    return pl.pallas_call(
        functools.partial(bwd_kernel, rotary=rotary),
        grid=(pairs, rows//block),
        in_specs=in_specs,
        out_specs=[
            pl.BlockSpec((block,PAIR), lambda p,i:(i,p)),
            pl.BlockSpec((keys,PAIR), lambda p,i:(0,p)),
            pl.BlockSpec((keys,PAIR), lambda p,i:(0,p)),
        ],
        out_shape=[jax.ShapeDtypeStruct((rows,pairs*PAIR),BF16)]+[jax.ShapeDtypeStruct((keys,pairs*PAIR),BF16)]*2,
        scratch_shapes=[pltpu.VMEM((2,keys,PAIR),BF16), pltpu.VMEM((2,PAIR,keys),BF16), pltpu.VMEM((2,keys,PAIR),BF16), pltpu.VMEM((keys,PAIR),F32), pltpu.VMEM((keys,PAIR),F32)],
        compiler_params=pltpu.CompilerParams(vmem_limit_bytes=48<<20),
        cost_estimate=pl.CostEstimate(flops=10*rows*keys*PAIR*pairs*2, bytes_accessed=2*(4*rows+4*keys)*PAIR*pairs, transcendentals=rows*keys*2*pairs),
    )(*args)


def whole_rows(ref):
    x = ref[...]
    return x.reshape(-1, x.shape[-1]) if x.ndim == 3 else x


def rows_spec(block, cols, start=0):
    return pl.BlockSpec((block, cols), lambda i: (start + i, 0))


def weight_spec(w, rows, cols, at):
    if w.ndim == 3:
        return pl.BlockSpec((w.shape[0], rows, cols), lambda i: (0, 0, at))
    return pl.BlockSpec((w.shape[0], cols), lambda i: (0, at))


def call_rows(kernel, rows, block, in_specs, outs, args, flops):
    return pl.pallas_call(
        kernel,
        grid=(rows // block,),
        in_specs=in_specs,
        out_specs=[rows_spec(block, cols) for cols, _ in outs],
        out_shape=[jax.ShapeDtypeStruct((rows, cols), kind) for cols, kind in outs],
        compiler_params=pltpu.CompilerParams(vmem_limit_bytes=52 << 20),
        cost_estimate=pl.CostEstimate(
            flops=flops, bytes_accessed=sum(2 * x.size for x in args), transcendentals=0
        ),
    )(*args)


def project_kernel(x_ref, near_ref, far_ref, o_ref):
    near, far = whole_rows(near_ref), whole_rows(far_ref)
    half = near.shape[0]
    o_ref[...] = (mm(x_ref[:, :half], near) + mm(x_ref[:, half:], far)).astype(o_ref.dtype)


def project(x, near, far, rows_each, cols, at, block=256):
    rows, width = x.shape
    spec = weight_spec(near, rows_each, cols, at)
    return call_rows(
        project_kernel,
        rows,
        block,
        [rows_spec(block, width), spec, spec],
        [(cols, BF16)],
        (x, near, far),
        2 * rows * width * cols,
    )[0]


def branch_kernel(*refs):
    out_ref = refs[-1]
    near_sum = far_sum = None
    for i in range(0, len(refs) - 1, 3):
        x, near, far = refs[i][...], whole_rows(refs[i + 1]), whole_rows(refs[i + 2])
        a, b = mm_nt(x, near), mm_nt(x, far)
        near_sum = a if near_sum is None else near_sum + a
        far_sum = b if far_sum is None else far_sum + b
    half = near_sum.shape[1]
    out_ref[:, :half] = near_sum.astype(out_ref.dtype)
    out_ref[:, half:] = far_sum.astype(out_ref.dtype)


def branch_rows(terms, start, rows, kind, rows_each, width, block=256):
    specs, args, flops = [], [], 0
    for x, near, far, at in terms:
        cols = x.shape[1]
        spec = weight_spec(near, rows_each, cols, at)
        specs += [rows_spec(block, cols, start // block), spec, spec]
        args += [x, near, far]
        flops += 2 * rows * cols * width
    return call_rows(branch_kernel, rows, block, specs, [(width, kind)], args, flops)[0]


def hidden_kernel(x_ref, gate_near, gate_far, up_near, up_far, gate_ref, up_ref, hidden_ref):
    half = gate_near.shape[0]
    near, far = x_ref[:, :half], x_ref[:, half:]
    gate = mm(near, gate_near[...]) + mm(far, gate_far[...])
    up = mm(near, up_near[...]) + mm(far, up_far[...])
    gate_ref[...] = gate
    up_ref[...] = up
    hidden_ref[...] = (gate * jax.nn.sigmoid(gate) * up).astype(BF16)


def hidden_forward(x, gate_w, up_w, block=128):
    rows, width = x.shape
    ff = gate_w[0].shape[1]
    spec = pl.BlockSpec((width // 2, ff), lambda i: (0, 0))
    return call_rows(
        hidden_kernel,
        rows,
        block,
        [rows_spec(block, width)] + [spec] * 4,
        [(ff, F32), (ff, F32), (ff, BF16)],
        (x, *gate_w, *up_w),
        4 * rows * width * ff,
    )


def hidden_back_kernel(g_ref, near_ref, far_ref, gate_ref, up_ref, grad_gate_ref, grad_up_ref):
    half = near_ref.shape[0]
    grad = mm(g_ref[:, :half], near_ref[...]) + mm(g_ref[:, half:], far_ref[...])
    gate, up = gate_ref[...], up_ref[...]
    s = jax.nn.sigmoid(gate)
    grad_gate_ref[...] = (grad * up * s * (1.0 + gate * (1.0 - s))).astype(BF16)
    grad_up_ref[...] = (grad * gate * s).astype(BF16)


def hidden_backward(g, down_w, gate, up, block=128):
    rows, width = g.shape
    ff = gate.shape[1]
    spec = pl.BlockSpec((width // 2, ff), lambda i: (0, 0))
    return call_rows(
        hidden_back_kernel,
        rows,
        block,
        [rows_spec(block, width), spec, spec, rows_spec(block, ff), rows_spec(block, ff)],
        [(ff, BF16), (ff, BF16)],
        (g, *down_w, gate, up),
        2 * rows * width * ff,
    )


def centered_rows(x):
    centered = x - jnp.mean(x, axis=-1, keepdims=True)
    inverse = lax.rsqrt(jnp.mean(centered * centered, axis=-1, keepdims=True) + epsilon)
    return centered * inverse, inverse


def add_norm_kernel(stream_ref, kept_ref, got_ref, far_ref, gain_ref, sum_ref, normed_ref):
    total = stream_ref[...].astype(F32) + (
        kept_ref[...] + got_ref[...].astype(F32) + far_ref[...].astype(F32)
    )
    sum_ref[...] = total
    normed_ref[...] = (centered_rows(total)[0] * gain_ref[...]).astype(BF16)


def add_norm(stream, kept, got, far, gain, block=128):
    rows, width = stream.shape
    spec = rows_spec(block, width)
    return call_rows(
        add_norm_kernel,
        rows,
        block,
        [spec] * 4 + [pl.BlockSpec((1, width), lambda i: (0, 0))],
        [(width, F32), (width, BF16)],
        (stream, kept, got, far, gain.reshape(1, width)),
        0,
    )


def norm_back_kernel(
    upper_ref, kept_ref, got_ref, far_ref, stream_ref, gain_ref, total_ref, low_ref, gain_grad_ref
):
    upstream = kept_ref[...] + got_ref[...].astype(F32) + far_ref[...].astype(F32)
    scaled, inverse = centered_rows(stream_ref[...].astype(F32))
    weighted = upstream * gain_ref[...]
    grad = inverse * (
        weighted
        - jnp.mean(weighted, axis=-1, keepdims=True)
        - scaled * jnp.mean(weighted * scaled, axis=-1, keepdims=True)
    )
    total = upper_ref[...] + grad
    total_ref[...] = total
    low_ref[...] = total.astype(BF16)

    @pl.when(pl.program_id(0) == 0)
    def _():
        gain_grad_ref[...] = jnp.zeros_like(gain_grad_ref)

    gain_grad_ref[...] += jnp.sum(upstream * scaled, axis=0, keepdims=True)


def norm_back(upper, kept, got, far, stream, gain, block=128):
    rows, width = stream.shape
    spec = rows_spec(block, width)
    row = pl.BlockSpec((1, width), lambda i: (0, 0))
    total, small, gain_grad = pl.pallas_call(
        norm_back_kernel,
        grid=(rows // block,),
        in_specs=[spec] * 5 + [row],
        out_specs=[spec, spec, row],
        out_shape=[
            jax.ShapeDtypeStruct((rows, width), F32),
            jax.ShapeDtypeStruct((rows, width), BF16),
            jax.ShapeDtypeStruct((1, width), F32),
        ],
        compiler_params=pltpu.CompilerParams(vmem_limit_bytes=32 << 20),
        cost_estimate=pl.CostEstimate(flops=0, bytes_accessed=20 * rows * width, transcendentals=0),
    )(upper, kept, got, far, stream, gain.reshape(1, width))
    return total, small, gain_grad[0]


def qkv_kernel(x_ref, near_ref, far_ref, cos_ref, sin_ref, o_ref):
    half = near_ref.shape[0]
    y = mm(x_ref[:, :half], near_ref[...]) + mm(x_ref[:, half:], far_ref[...])
    cos, sin = cos_ref[...], sin_ref[...]
    turned = 2 * (y.shape[1] // 3)
    for at in range(0, turned, PAIR):
        o_ref[:, at : at + PAIR] = turn(y[:, at : at + PAIR], cos, sin).astype(BF16)
    o_ref[:, turned:] = y[:, turned:].astype(BF16)


def project_heads(x, near, far, cols, tables, block):
    rows, width = x.shape
    return pl.pallas_call(
        qkv_kernel,
        grid=(rows // block,),
        in_specs=[
            pl.BlockSpec((block, width), lambda i: (i, 0)),
            pl.BlockSpec((width // 2, cols), lambda i: (0, 0)),
            pl.BlockSpec((width // 2, cols), lambda i: (0, 0)),
            pl.BlockSpec((block, PAIR), lambda i: (i, 0)),
            pl.BlockSpec((block, PAIR), lambda i: (i, 0)),
        ],
        out_specs=pl.BlockSpec((block, cols), lambda i: (i, 0)),
        out_shape=jax.ShapeDtypeStruct((rows, cols), BF16),
        compiler_params=pltpu.CompilerParams(vmem_limit_bytes=48 << 20),
        cost_estimate=pl.CostEstimate(
            flops=2 * rows * width * cols, bytes_accessed=2 * (rows + cols) * width, transcendentals=0
        ),
    )(x, near, far, *tables)


class Links:
    def __init__(self, move):
        self.move = move
        self.flying = {}

    def tick(self, values, advance="", start=()):
        values = list(values) if isinstance(values, (tuple, list)) else [values]
        count = len(values)
        names = [name for name in advance.split() if name in self.flying]
        chains = [self.flying.pop(name) for name in names]
        operands = list(values)
        for _, got in chains:
            operands += got
        for _, _, arrays in start:
            operands += arrays
        tied = list(lax.optimization_barrier(tuple(operands)))
        values, tied = tied[:count], tied[count:]
        moving = []
        for name, (chain, got) in zip(names, chains):
            got, tied = tied[: len(got)], tied[len(got) :]
            try:
                moving.append((name, chain, chain.send(got)))
            except StopIteration:
                pass
        for name, make, arrays in start:
            arrays, tied = tied[: len(arrays)], tied[len(arrays) :]
            chain = make(*arrays)
            moving.append((name, chain, next(chain)))
        operands = values + [x for _, _, moves in moving for _, x in moves]
        tied = list(lax.optimization_barrier(tuple(operands)))
        values, tied = tied[:count], tied[count:]
        for name, chain, moves in moving:
            self.flying[name] = (chain, [self.move(kind, tied.pop(0)) for kind, _ in moves])
        return values[0] if count == 1 else tuple(values)

    def finish(self, *names):
        for name in names:
            while name in self.flying:
                self.tick((), name)


def arrange_in_kernel(row_ref, col_ref, side_ref, x_ref, out_ref):
    count = out_ref.shape[1] // PAIR // 3
    width = 3 * HEAD_DIM
    side = side_ref[0]
    at = lax.broadcasted_iota(jnp.int32, (out_ref.shape[0], 2 * width), 1)
    for j in range(count):
        other = j >= count // 2
        pieces = []
        for i in range(2):
            source = col_ref[(2 * j + i) % count]
            piece = x_ref[:, pl.ds(pl.multiple_of(source * 2 * width, 2 * width), 2 * width)]
            pieces.append(piece.astype(F32))
        first, second = pieces
        own_first = jnp.where(at < width, first, pltpu.roll(second, width, 1))
        own_second = jnp.where(at < width, pltpu.roll(first, width, 1), second)
        want_first = (side == 1) if other else (side == 0)
        out = jnp.where(want_first, own_first, own_second)
        out_ref[:, j * 2 * width : (j + 1) * 2 * width] = out.astype(out_ref.dtype)


def arrange_out_kernel(row_ref, col_ref, side_ref, x_ref, out_ref):
    count = out_ref.shape[1] // PAIR // 3
    width = 3 * HEAD_DIM
    side = side_ref[0]
    half = count // 2
    at = lax.broadcasted_iota(jnp.int32, (out_ref.shape[0], 2 * width), 1)
    for j in range(half):
        own = x_ref[:, j * 2 * width : (j + 1) * 2 * width].astype(F32)
        other = x_ref[:, (half + j) * 2 * width : (half + j + 1) * 2 * width].astype(F32)
        first = jnp.where(side == 0, own, other)
        second = jnp.where(side == 0, other, own)
        made = (
            jnp.where(at < width, first, pltpu.roll(second, width, 1)),
            jnp.where(at < width, pltpu.roll(first, width, 1), second),
        )
        for i in range(2):
            place = col_ref[2 * j + i]
            out_ref[:, pl.ds(pl.multiple_of(place * 2 * width, 2 * width), 2 * width)] = made[
                i
            ].astype(out_ref.dtype)


def arrange(x, row_at, col_at, side, rows, shard, out_type, back):
    count, total = row_at.shape[0], x.shape[1]
    pairs = col_at.shape[0]
    if shard != 3 * HEAD_DIM or pairs % 2:
        shard_at = jnp.concatenate([col_at * 2 + side, col_at * 2 + 1 - side])
        blocks = x.reshape(-1, rows, 2 * pairs, shard)
        if back:
            blocks = jnp.zeros_like(blocks).at[row_at].set(blocks)
            blocks = jnp.zeros_like(blocks).at[:, :, shard_at].set(blocks)
        else:
            blocks = blocks[row_at][:, :, shard_at]
        return blocks.reshape(-1, total).astype(out_type)

    def here(i, row_at, col_at, side):
        return i, 0

    def there(i, row_at, col_at, side):
        return row_at[i], 0

    return pl.pallas_call(
        arrange_out_kernel if back else arrange_in_kernel,
        grid_spec=pltpu.PrefetchScalarGridSpec(
            num_scalar_prefetch=3,
            grid=(count,),
            in_specs=[pl.BlockSpec((rows, total), here if back else there)],
            out_specs=pl.BlockSpec((rows, total), there if back else here),
        ),
        out_shape=jax.ShapeDtypeStruct((count * rows, total), out_type),
        compiler_params=pltpu.CompilerParams(vmem_limit_bytes=32 << 20),
        cost_estimate=pl.CostEstimate(
            flops=0, bytes_accessed=6 * count * rows * total, transcendentals=0
        ),
    )(row_at, col_at, side.reshape(1), x)


def build(n_dp, n_tensor):
    tensor_bits = []
    bit = 1
    while bit < n_tensor:
        tensor_bits.append(bit)
        bit *= 2
    dp_bits = []
    bit = 1
    while bit < n_dp:
        dp_bits.append(bit)
        bit *= 2
    far_first = list(reversed(dp_bits))
    pair_first = [1] + far_first[:-1]
    near_first = dp_bits
    pair_last = dp_bits[1:] + [1]
    offsets = [0]
    for bit in far_first:
        offsets = offsets + [o ^ bit for o in offsets]
    order = [0]
    for bit in reversed(tensor_bits):
        order = order + [o ^ bit for o in order]

    def swap(x, bit):
        return lax.ppermute(x, "tensor", [(i, i ^ bit) for i in range(n_tensor)])

    def swap_dp(x, bit):
        return lax.ppermute(x, "dp", [(i, i ^ bit) for i in range(n_dp)])

    def gather_rows(own):
        for bit in reversed(tensor_bits):
            own = jnp.concatenate([own, swap(own, bit)], axis=0)
        return own

    def scatter_near(make, rows):
        half = rows // 2
        got = swap(make(half, half, BF16), tensor_bits[0])
        return make(0, half, F32), got

    def scatter_far(kept, got):
        for bit in tensor_bits[1:]:
            half = kept.shape[0] // 2
            far = swap(low(kept[half:] + wide(got[half:])), bit)
            if bit != tensor_bits[-1]:
                kept, got = kept[:half] + wide(got[:half]), far
        return kept, got, far

    def sum_tensor(x):
        for bit in tensor_bits:
            x = x + swap(x, bit)
        return x

    def sum_dp(x):
        for bit in dp_bits:
            x = x + swap_dp(x, bit)
        return x

    def body(
        hidden_in,
        conditioning,
        valid_mask,
        teacher,
        gain_one,
        gain_two,
        gain_three,
        self_in_weight,
        self_out_weight,
        cross_query_weight,
        cross_memory_weight,
        cross_out_weight,
        gate_up_weight,
        down_weight,
    ):
        _, length, width = hidden_in.shape
        cond_tokens, cond_width = conditioning.shape[1:]
        me = lax.axis_index("tensor")
        dp_me = lax.axis_index("dp")
        shard = width // n_dp
        own_rows = length // n_tensor

        running = valid_mask[0, 0] > 0

        def stage(work, *args):
            def skipped(*args):
                return jax.tree.map(
                    lambda x: jnp.zeros(x.shape, x.dtype), jax.eval_shape(work, *args)
                )

            return lax.cond(running, work, skipped, *args)

        def move(kind, x):
            axis, bit = kind
            return swap(x, bit) if axis == "tensor" else swap_dp(x, bit)

        links = Links(move)
        tick = links.tick

        def gather_double(own, out, name, bits):
            rows = own.shape[0]
            near, far, order_got = own, own[:0], [0]
            for bit in bits:
                near = jnp.concatenate([near, far], axis=0) if far.shape[0] else near
                (far,) = yield [(("dp", bit), near)]
                order_got = order_got + [o ^ bit for o in order_got]
            if order_got != offsets:
                half = len(order_got) // 2
                pieces = [
                    (near if order_got.index(o) < half else far)[
                        order_got.index(o) % half * rows : (order_got.index(o) % half + 1) * rows
                    ]
                    for o in offsets
                ]
                near = jnp.concatenate(pieces[:half], axis=0)
                far = jnp.concatenate(pieces[half:], axis=0)
            out[name] = (near, far)

        def gather_direct(own, out, name):
            two, four, one = yield [(("dp", 2), own), (("dp", 4), own), (("dp", 1), own)]
            six, three, five = yield [(("dp", 6), own), (("dp", 1), two), (("dp", 1), four)]
            (seven,) = yield [(("dp", 1), six)]
            shards = [own, one, two, three, four, five, six, seven]
            half = len(offsets) // 2
            out[name] = tuple(
                jnp.concatenate([shards[o] for o in part], axis=0)
                for part in (offsets[:half], offsets[half:])
            )

        def reduce_halve(near, far, out, name, narrow=low):
            (got,) = yield [(("dp", 1), narrow(far))]
            terms = [near, got]
            for bit in near_first[1:]:
                half = near.shape[0] // 2
                near = near[:half]
                (got,) = yield [(("dp", bit), narrow(sum(wide(t[half:]) for t in terms)))]
                terms = [t[:half] for t in terms] + [got]
            out[name] = sum(wide(t) for t in terms)

        def reduce_direct(near, far, out, name):
            rows = near.shape[0] // 4

            def block(offset):
                at = offsets.index(offset)
                return (near if at < 4 else far)[at % 4 * rows : (at % 4 + 1) * rows]

            def add(*xs):
                return sum(wide(x) for x in xs)

            (got,) = yield [(("dp", 1), block(7))]
            six = low(add(block(6), got))
            six, five, three = yield [(("dp", 6), six), (("dp", 1), block(5)), (("dp", 1), block(3))]
            four, two = low(add(block(4), five)), low(add(block(2), three))
            four, two, one = yield [(("dp", 4), four), (("dp", 2), two), (("dp", 1), block(1))]
            out[name] = add(block(0), six, four, two, one)

        if n_dp != 8:
            gather_direct = functools.partial(gather_double, bits=far_first)
            reduce_direct = reduce_halve

        def output_chain(own, part, out, name):
            for bit in reversed(tensor_bits):
                (got,) = yield [(("tensor", bit), jnp.concatenate([own, low(part)], axis=0))]
                part = wide(part) + wide(got[own.shape[0] :])
                own = jnp.concatenate([own, got[: own.shape[0]]], axis=0)
            out[name] = (own, part)

        local = self_in_weight.shape[2]
        ff = down_weight.shape[0]
        first = jnp.concatenate([self_in_weight.reshape(shard, 3 * local), self_out_weight.T], axis=1)
        gate_up_own = gate_up_weight.reshape(shard, 2 * ff)
        full = {}

        def gathering(name, own, bits):
            return name, functools.partial(gather_double, out=full, name=name, bits=bits), [own]

        cross_rows = shard + cond_width // n_dp
        start_cross = gathering(
            "cross",
            jnp.concatenate(
                [
                    jnp.concatenate([cross_query_weight, cross_out_weight.T], axis=1),
                    cross_memory_weight.reshape(cond_width // n_dp, 2 * local),
                ],
                axis=0,
            ),
            far_first,
        )
        start_up_a = gathering("up_a", gate_up_own[:, :ff], far_first)
        start_up_b = gathering("up_b", gate_up_own[:, ff:], far_first)
        start_down = gathering("down", down_weight.T, far_first)
        count = jnp.sum(valid_mask)
        count_row = jnp.zeros((shard,), F32).at[0].set(wide(count // 32)).at[1].set(wide(count % 32))
        gains_own = jnp.concatenate([gain_one, gain_two, gain_three, low(count_row)])[None]
        hidden_raw = tick(
            hidden_in[0],
            "",
            [
                gathering("gains", gains_own, far_first),
                ("first", functools.partial(gather_direct, out=full, name="first"), [first]),
            ],
        )

        pairs = local // PAIR
        rows = length
        mine = slice(0, own_rows)
        row_at = me ^ jnp.array(order, jnp.int32)
        col_at = (dp_me // 2) ^ jnp.array([o // 2 for o in offsets[: n_dp // 2]], jnp.int32)
        side = dp_me % 2

        def arrange_in(x, row_at):
            return arrange(x, row_at, col_at, side, own_rows, shard, BF16, False)

        def take(x, owner):
            return lax.dynamic_slice_in_dim(x, owner * own_rows, own_rows, 0)

        def center(x):
            return wide(x) - jnp.mean(wide(x), axis=-1, keepdims=True)

        def join(halves):
            return jnp.concatenate(halves, axis=0)

        hidden_raw, teacher_raw = tick((hidden_raw, teacher[0]), "gains")
        hidden = arrange_in(hidden_raw, row_at)
        hidden, me_late = tick((hidden, me), "first gains")
        centered = center(hidden)
        inverse_all = lax.rsqrt(jnp.mean(centered * centered, axis=-1, keepdims=True) + epsilon)

        def relative_late(x):
            return jnp.concatenate([take(x, me_late ^ o) for o in order], axis=0)

        position = relative_late(jnp.arange(length, dtype=F32)[:, None])
        lane = jnp.arange(PAIR) % HEAD_DIM
        frequency = jnp.exp((lane % (ROT // 2)).astype(F32) * (-2.0 * math.log(10000.0) / ROT))
        angles = position * frequency[None, :]
        cosine, sine = jnp.cos(angles), jnp.sin(angles)
        tables = (
            jnp.where(lane < ROT, cosine, 1.0),
            jnp.where(lane < ROT // 2, -sine, jnp.where(lane < ROT, sine, 0.0)),
        )
        bias = jnp.where(relative_late(valid_mask[0][:, None]) > 0, 0.0, masked_score)
        cosine, sine, hidden, inverse_all, teacher_raw = tick(
            (*tables, hidden, inverse_all, teacher_raw), "first gains", [start_cross]
        )
        tables = (cosine, sine)
        links.finish("gains")
        gains = jnp.concatenate(full["gains"], axis=0).reshape(n_dp, 4, shard)
        counts = wide(gains[:, 3])
        token_count = jnp.sum(32.0 * counts[:, 0] + counts[:, 1])
        gain_first, gain_second, gain_third = (wide(gains[:, i]).reshape(width) for i in range(3))
        normed_one = low(center(hidden) * inverse_all * gain_first)
        target_low = arrange_in(teacher_raw, me.reshape(1))
        residual = wide(hidden[mine])
        normed_one, target_low = tick((normed_one, target_low), "first", [start_up_a])
        links.finish("first")
        first_near, first_far = full["first"]
        cond_shard = cond_width // n_dp
        place = jnp.arange(cond_width)
        source = (dp_me ^ jnp.array(offsets, jnp.int32))[place // cond_shard] * cond_shard
        source = source + place % cond_shard
        cond_place = place[:, None] == source[None, :]
        memory_input = low(dot(conditioning[0], low(cond_place)))
        pad_tokens = -cond_tokens % 16
        cond_rows = cond_tokens + pad_tokens
        cond_bias = jnp.where(jnp.arange(cond_rows)[:, None] < cond_tokens, 0.0, masked_score)

        def self_attention(normed_one, first_near, first_far, tables, bias):
            mixed = project_heads(normed_one, first_near, first_far, 3 * local, tables, 256)
            attended, self_totals = attend_forward(
                mixed, mixed, mixed, 0, pairs, 2 * pairs, bias, pairs, rows
            )
            return mixed, attended, self_totals

        mixed, attended, self_totals = stage(
            self_attention, normed_one, first_near, first_far, tables, bias
        )
        attended = tick(attended, "cross")

        def branch(rows_each, *terms):
            return scatter_near(
                lambda start, count, kind: branch_rows(
                    terms, start, count, kind, rows_each, width
                ),
                rows,
            )

        near = stage(
            lambda x, a, b: branch(0, (x, a, b, 3 * local // local)), attended, *full["first"]
        )
        near = tick(near, "cross up_a", [start_up_b])

        def add_and_norm(stream, near, gain):
            return add_norm(stream, *scatter_far(*near), gain)

        after_self, normed_share = stage(add_and_norm, residual, near, gain_second)
        normed_share = tick(normed_share, "cross up_a up_b", [start_down])

        def unpack_memory(cross_near, cross_far):
            return [x[:, shard:].reshape(-1, 2 * local) for x in (cross_near, cross_far)]

        links.finish("cross")
        cross_w = [x.reshape(n_dp // 2, cross_rows, 2 * local) for x in full["cross"]]

        def gather_and_unpack(normed_share, *cross_w):
            halves = unpack_memory(*cross_w)
            memory = sum(
                dot(memory_input[:, i * cond_width // 2 : (i + 1) * cond_width // 2], halves[i])
                for i in range(2)
            )
            return gather_rows(normed_share), join(halves), jnp.pad(
                low(memory), ((0, pad_tokens), (0, 0))
            )

        normed_two, full_memory, cross_memory = stage(gather_and_unpack, normed_share, *cross_w)
        normed_two = tick(normed_two, "up_b")

        def cross_attention(normed_two, cross_near, cross_far, cross_memory):
            cross_queries = project(normed_two, cross_near, cross_far, shard, local, 0)
            cross_attended, cross_totals = attend_forward(
                cross_queries, cross_memory, cross_memory, 0, 0, pairs, cond_bias, pairs, rows
            )
            near = branch(shard, (cross_attended, cross_near, cross_far, 1))
            return cross_queries, cross_attended, cross_totals, near

        cross_queries, cross_attended, cross_totals, near = stage(
            cross_attention, normed_two, *cross_w, cross_memory
        )
        near = tick(near, "up_a down")
        after_cross, normed_share = stage(add_and_norm, after_self, near, gain_third)
        normed_share = tick(normed_share, "up_b down")
        normed_three = stage(gather_rows, normed_share)
        normed_three = tick(normed_three, "up_a up_b")
        links.finish("up_a", "up_b")
        gate_value, upward, hidden_units = stage(
            hidden_forward, normed_three, full["up_a"], full["up_b"]
        )
        hidden_units = tick(hidden_units, "down")
        links.finish("down")
        near = stage(
            lambda x, a, b: branch(0, (x, a, b, 0)), hidden_units, *full["down"]
        )

        def final_rows(stream, near, target_low, valid_rows):
            kept, got, far = scatter_far(*near)
            half = stream.shape[0]
            final_state = stream + (kept[:half] + wide(got[:half]) + wide(far))
            difference = final_state - wide(target_low)
            losses = jnp.sum(valid_rows[:, 0] * jnp.sum(difference * difference, axis=-1))
            grad_final = 2.0 * length / token_count * valid_rows * difference
            return final_state, losses, grad_final, gather_rows(low(grad_final))

        valid_rows = wide(take(valid_mask[0][:, None], me))
        final_state, losses, grad_final, grad_final_low = stage(
            final_rows, after_cross, near, target_low, valid_rows
        )
        grads = {}

        def halves_of(x, y):
            half = width // 2
            return low(dot_tn(x[:, :half], y)), low(dot_tn(x[:, half:], y))

        def reducing(name, halves):
            return name, functools.partial(reduce_halve, out=grads, name=name), list(halves)

        grad_down = halves_of(grad_final_low, hidden_units)
        grad_final_low = tick(grad_final_low, "", [reducing("down", grad_down)])

        def hidden_back(grad_final_low, gate_value, upward, down_w, up_a, up_b):
            grad_gate, grad_up = hidden_backward(grad_final_low, down_w, gate_value, upward)
            return grad_gate, grad_up, branch(0, (grad_gate, *up_a, 0), (grad_up, *up_b, 0))

        grad_gate, grad_up, near = stage(
            hidden_back,
            grad_final_low,
            gate_value,
            upward,
            full["down"],
            full["up_a"],
            full["up_b"],
        )

        def back_three(near, normed_three, grad_gate):
            return norm_back(
                grad_final, *scatter_far(*near), after_cross, gain_third
            ), halves_of(normed_three, grad_gate)

        (grad_after_cross, grad_share, gain_three_sum), grad_up_a = stage(
            back_three, near, normed_three, grad_gate
        )
        grad_share = tick(grad_share, "down", [reducing("up_a", grad_up_a)])

        def gather_three(grad_share, normed_three, grad_up):
            return gather_rows(grad_share), halves_of(normed_three, grad_up)

        grad_cross_low, grad_up_b = stage(gather_three, grad_share, normed_three, grad_up)
        grad_cross_low = tick(grad_cross_low, "down", [reducing("up_b", grad_up_b)])

        def cross_back(grad_cross_low, cross_near, cross_far):
            grad_cross_attended = project(grad_cross_low, cross_near, cross_far, shard, local, 1)
            grad_cross_queries, grad_keys, grad_values = attend_backward(
                cross_queries,
                cross_memory,
                cross_memory,
                0,
                0,
                pairs,
                cond_bias,
                cross_totals,
                grad_cross_attended,
                None,
                pairs,
                rows,
            )
            near = branch(shard, (grad_cross_queries, cross_near, cross_far, 0))
            return grad_cross_queries, grad_keys, grad_values, near

        grad_cross_queries, grad_keys, grad_values, near = stage(
            cross_back, grad_cross_low, *cross_w
        )

        def back_two(near, grad_cross_queries, grad_keys, grad_values):
            grad_memory_low = jnp.concatenate(
                [grad_keys[:cond_tokens], grad_values[:cond_tokens]], axis=1
            )
            cond_part = lax.dot_general(
                dot_nt(grad_memory_low, full_memory),
                wide(cond_place),
                (((1,), (1,)), ((), ())),
                precision=lax.Precision.HIGHEST,
            )
            return (
                norm_back(grad_after_cross, *scatter_far(*near), after_self, gain_second),
                halves_of(normed_two, grad_cross_queries),
                grad_memory_low,
                cond_part.reshape(-1, width),
            )

        (grad_after_self, grad_share, gain_two_sum), grad_cross_query, grad_memory_low, cond_part = (
            stage(back_two, near, grad_cross_queries, grad_keys, grad_values)
        )
        grad_share = tick(grad_share, "up_a down")

        def gather_two(grad_share, grad_cross_low, grad_cross_query, grad_memory_low):
            parts = zip(
                grad_cross_query,
                halves_of(grad_cross_low, cross_attended),
                (
                    low(dot_tn(memory_input[:, : cond_width // 2], grad_memory_low)),
                    low(dot_tn(memory_input[:, cond_width // 2 :], grad_memory_low)),
                ),
            )
            packed = tuple(
                jnp.concatenate(
                    [
                        jnp.concatenate([query, out], axis=1).reshape(n_dp // 2, shard, 2 * local),
                        memory.reshape(n_dp // 2, cond_shard, 2 * local),
                    ],
                    axis=1,
                ).reshape(-1, 2 * local)
                for query, out, memory in parts
            )
            return gather_rows(grad_share), packed

        grad_self_low, grad_cross = stage(
            gather_two, grad_share, grad_cross_low, grad_cross_query, grad_memory_low
        )
        others = {}
        grad_self_low = tick(
            grad_self_low,
            "up_b down",
            [
                (
                    "output",
                    functools.partial(output_chain, out=others, name="output"),
                    [low(final_state), cond_part],
                ),
                reducing("cross", grad_cross),
            ],
        )

        def self_back(grad_self_low, first_near, first_far):
            grad_attended = project(grad_self_low, first_near, first_far, 0, local, 3)
            grad_parts = attend_backward(
                mixed,
                mixed,
                mixed,
                0,
                pairs,
                2 * pairs,
                bias,
                self_totals,
                grad_attended,
                tables,
                pairs,
                rows,
            )
            grad_mixed_low = jnp.concatenate(grad_parts, axis=1)
            return grad_mixed_low, branch(0, (grad_mixed_low, first_near, first_far, 0))

        grad_mixed_low, near = stage(self_back, grad_self_low, *full["first"])
        near = tick(near, "up_a up_b output")

        def back_one(near, grad_mixed_low, grad_self_low):
            packed = tuple(
                jnp.concatenate([x, y], axis=1)
                for x, y in zip(
                    halves_of(normed_one, grad_mixed_low), halves_of(grad_self_low, attended)
                )
            )
            return norm_back(
                grad_after_self, *scatter_far(*near), hidden[mine], gain_first
            ), packed

        (_, grad_share, gain_one_sum), grad_first = stage(
            back_one, near, grad_mixed_low, grad_self_low
        )
        sums = jnp.stack([gain_one_sum, gain_two_sum, gain_three_sum]).reshape(3, n_dp, shard)
        sums = jnp.concatenate(
            [sums.transpose(1, 0, 2).reshape(n_dp, 3 * shard), jnp.full((n_dp, shard), losses)], axis=1
        )
        grad_share = tick(
            grad_share,
            "cross up_b output",
            [("first", functools.partial(reduce_direct, out=grads, name="first"), list(grad_first))],
        )

        def last_rows(grad_share, sums):
            got = {}
            sums = sum_tensor(sums)
            chain = reduce_halve(
                sums[: n_dp // 2], sums[n_dp // 2 :], out=got, name="sums", narrow=lambda x: x
            )
            moves = next(chain)
            while "sums" not in got:
                try:
                    moves = chain.send([move(kind, x) for kind, x in moves])
                except StopIteration:
                    pass
            return gather_rows(grad_share), got["sums"][0]

        rows_hidden, sums = stage(last_rows, grad_share, sums)
        rows_hidden = tick(rows_hidden, "first cross")
        links.finish(*list(links.flying))

        def arrange_out(x, out_type):
            return arrange(x, row_at, col_at, side, own_rows, shard, out_type, True)

        rows_output, cond_sum = others["output"]
        grad_conditioning = cond_sum.reshape(cond_tokens, cond_width)
        grad_hidden = arrange_out(rows_hidden, F32)
        block_output = arrange_out(rows_output, BF16)
        mean_loss = sums[3 * shard] / (token_count * width)

        return (
            mean_loss,
            block_output[None],
            grad_hidden[None],
            grad_conditioning[None],
            sums[:shard],
            sums[shard : 2 * shard],
            sums[2 * shard : 3 * shard],
            grads["first"][:, : 3 * local].reshape(shard, 3, local),
            grads["first"][:, 3 * local :].T,
            grads["cross"][:shard, :local],
            grads["cross"][shard:].reshape(cond_shard, 2, local),
            grads["cross"][:shard, local:].T,
            jnp.stack([grads["up_a"], grads["up_b"]], axis=1),
            grads["down"].T,
        )

    return body


def solution(mesh):
    return jax.shard_map(
        build(mesh.shape["dp"], mesh.shape["tensor"]),
        mesh=mesh,
        in_specs=(
            P("dp", None, None),
            P("dp", None, None),
            P("dp", None),
            P("dp", None, None),
            P("dp"),
            P("dp"),
            P("dp"),
            P("dp", None, "tensor"),
            P("tensor", "dp"),
            P("dp", "tensor"),
            P("dp", None, "tensor"),
            P("tensor", "dp"),
            P("dp", None, "tensor"),
            P("tensor", "dp"),
        ),
        out_specs=(
            P(),
            P("dp", None, None),
            P("dp", None, None),
            P("dp", None, None),
            P("dp"),
            P("dp"),
            P("dp"),
            P("dp", None, "tensor"),
            P("tensor", "dp"),
            P("dp", "tensor"),
            P("dp", None, "tensor"),
            P("tensor", "dp"),
            P("dp", None, "tensor"),
            P("tensor", "dp"),
        ),
        check_vma=False,
    )
```

```python
import functools
import math

import jax
import jax.numpy as jnp
from jax import lax
from jax.experimental import pallas as pl
from jax.experimental.pallas import tpu as pltpu
from jax.sharding import PartitionSpec as P

HEAD_DIM = 64
ROT = 32
CHUNKS = 1

epsilon = 1e-05
masked_score = -1e30
F32 = jnp.float32
BF16 = jnp.bfloat16


def low(x):
    return x.astype(BF16)


def wide(x):
    return x.astype(F32)


def dot(a, b):
    return lax.dot_general(a, b, (((1,), (0,)), ((), ())), preferred_element_type=F32)


def dot_nt(a, b):
    return lax.dot_general(a, b, (((1,), (1,)), ((), ())), preferred_element_type=F32)


def dot_tn(a, b):
    return lax.dot_general(a, b, (((0,), (0,)), ((), ())), preferred_element_type=F32)


PAIR=128
SCALE=1.0/math.sqrt(HEAD_DIM)
SCALE2=SCALE*math.log2(math.e)

def mm(a,b): return lax.dot_general(a,b,(((1,),(0,)),((),())),preferred_element_type=F32)
def mm_nt(a,b): return lax.dot_general(a,b,(((1,),(1,)),((),())),preferred_element_type=F32)

def mm_tn(a,b): return lax.dot_general(a,b,(((0,),(0,)),((),())),preferred_element_type=F32)


def head_lanes(shape, axis, head):
    at = lax.broadcasted_iota(jnp.int32, shape, axis)
    return (at >= head*HEAD_DIM) & (at < (head+1)*HEAD_DIM)

def keep_head(x, axis, head):
    return jnp.where(head_lanes(x.shape, axis, head), x, jnp.zeros_like(x))

def with_lane(x, head, lane_value):
    at = lax.broadcasted_iota(jnp.int32, x.shape, 1)
    other = (1-head)*HEAD_DIM
    return jnp.where(at == other, lane_value, keep_head(x, 1, head))

def fwd_kernel(q_ref, k_ref, v_ref, bias_ref, o_ref, lse_ref, k_sc, vt_sc):
    @pl.when(pl.program_id(1) == 0)
    def _():
        k = k_ref[...].astype(F32)
        vt = v_ref[...].astype(F32).T
        for h in range(2):
            k_sc[h] = with_lane(k, h, bias_ref[...]).astype(BF16)
            vt_sc[h] = keep_head(vt, 0, h).astype(BF16)
    q = q_ref[...].astype(F32)
    out = None
    for h in range(2):
        qh = with_lane(q, h, 1.0).astype(BF16)
        s = mm_nt(k_sc[h], qh)
        m = jnp.max(s, axis=0, keepdims=True)
        e = jnp.exp2((s - m) * SCALE2)
        l = jnp.sum(e, axis=0, keepdims=True)
        o = mm(vt_sc[h], e.astype(BF16)) * (1.0 / l)
        out = o if out is None else out + o
        lse_ref[0, h:h+1, :] = m * SCALE2 + jnp.log2(l)
    o_ref[...] = out.T.astype(BF16)

def bwd_kernel(q_ref, k_ref, v_ref, bias_ref, lse_ref, g_ref, *rest, rotary):
    if rotary:
        cosq_ref, sinq_ref, cosk_ref, sink_ref, dq_ref, dk_ref, dv_ref, k_sc, kt_sc, v_sc, dk_sc, dv_sc = rest
    else:
        dq_ref, dk_ref, dv_ref, k_sc, kt_sc, v_sc, dk_sc, dv_sc = rest
    i = pl.program_id(1)
    @pl.when(i == 0)
    def _():
        k = k_ref[...].astype(F32)
        kt = k.T
        for h in range(2):
            k_sc[h] = with_lane(k, h, bias_ref[...]).astype(BF16)
            kt_sc[h] = keep_head(kt, 0, h).astype(BF16)
            v_sc[h] = keep_head(v_ref[...].astype(F32), 1, h).astype(BF16)
        dk_sc[...] = jnp.zeros_like(dk_sc)
        dv_sc[...] = jnp.zeros_like(dv_sc)
    q = q_ref[...].astype(F32)
    g32 = g_ref[...].astype(F32)
    g = g_ref[...]
    dqt = None
    dk = dk_sc[...]
    dv = dv_sc[...]
    for h in range(2):
        qa = with_lane(q, h, 1.0).astype(BF16)
        qh = keep_head(q, 1, h).astype(BF16)
        gh = keep_head(g32, 1, h).astype(BF16)
        s = mm_nt(k_sc[h], qa)
        p = jnp.exp2(s * SCALE2 - lse_ref[0, h:h+1, :])
        dp = mm_nt(v_sc[h], g)
        t = p * dp
        delta = jnp.sum(t, axis=0, keepdims=True)
        ds = (t - p * delta).astype(BF16)
        dv = dv + mm(p.astype(BF16), gh)
        dk = dk + mm(ds, qh)
        d = mm(kt_sc[h], ds)
        dqt = d if dqt is None else dqt + d
    dk_sc[...] = dk
    dv_sc[...] = dv
    dq = dqt.T * SCALE
    if rotary:
        dq = turn_back(dq, cosq_ref[...], sinq_ref[...])
    dq_ref[...] = dq.astype(BF16)
    @pl.when(i == pl.num_programs(1) - 1)
    def _():
        dk = dk_sc[...] * SCALE
        if rotary:
            dk = turn_back(dk, cosk_ref[...], sink_ref[...])
        dk_ref[...] = dk.astype(BF16)
        dv_ref[...] = dv_sc[...].astype(BF16)

def swap_halves(x):
    n = x.shape[1]
    at = lax.broadcasted_iota(jnp.int32, x.shape, 1) % HEAD_DIM
    return jnp.where(at < 16, pltpu.roll(x, n - 16, 1), pltpu.roll(x, 16, 1))

def turn(x, cos, sin):
    return x * cos + swap_halves(x) * sin

def turn_back(x, cos, sin):
    return x * cos - swap_halves(x) * sin

def attend_forward(q, k, v, qcol, kcol, vcol, bias, pairs, block):
    rows = q.shape[0]; keys = k.shape[0]
    return pl.pallas_call(
        fwd_kernel,
        grid=(pairs, rows//block),
        in_specs=[
            pl.BlockSpec((block,PAIR), lambda p,i:(i,qcol+p)),
            pl.BlockSpec((keys,PAIR), lambda p,i:(0,kcol+p)),
            pl.BlockSpec((keys,PAIR), lambda p,i:(0,vcol+p)),
            pl.BlockSpec((keys,1), lambda p,i:(0,0)),
        ],
        out_specs=[
            pl.BlockSpec((block,PAIR), lambda p,i:(i,p)),
            pl.BlockSpec((1,8,block), lambda p,i:(p,0,i)),
        ],
        out_shape=[jax.ShapeDtypeStruct((rows,pairs*PAIR),BF16), jax.ShapeDtypeStruct((pairs,8,rows),F32)],
        scratch_shapes=[pltpu.VMEM((2,keys,PAIR),BF16), pltpu.VMEM((2,PAIR,keys),BF16)],
        compiler_params=pltpu.CompilerParams(vmem_limit_bytes=48<<20),
        cost_estimate=pl.CostEstimate(flops=4*rows*keys*PAIR*pairs*2, bytes_accessed=2*(2*rows+2*keys)*PAIR*pairs, transcendentals=rows*keys*2*pairs),
    )(q,k,v,bias)

def attend_backward(q, k, v, qcol, kcol, vcol, bias, lse, g, tables, pairs, block):
    rows = q.shape[0]; keys = k.shape[0]
    rotary = tables is not None
    in_specs=[
        pl.BlockSpec((block,PAIR), lambda p,i:(i,qcol+p)),
        pl.BlockSpec((keys,PAIR), lambda p,i:(0,kcol+p)),
        pl.BlockSpec((keys,PAIR), lambda p,i:(0,vcol+p)),
        pl.BlockSpec((keys,1), lambda p,i:(0,0)),
        pl.BlockSpec((1,8,block), lambda p,i:(p,0,i)),
        pl.BlockSpec((block,PAIR), lambda p,i:(i,p)),
    ]
    args=[q,k,v,bias,lse,g]
    if rotary:
        in_specs += [pl.BlockSpec((block,PAIR), lambda p,i:(i,0))]*2 + [pl.BlockSpec((keys,PAIR), lambda p,i:(0,0))]*2
        args += [tables[0],tables[1],tables[0],tables[1]]
    return pl.pallas_call(
        functools.partial(bwd_kernel, rotary=rotary),
        grid=(pairs, rows//block),
        in_specs=in_specs,
        out_specs=[
            pl.BlockSpec((block,PAIR), lambda p,i:(i,p)),
            pl.BlockSpec((keys,PAIR), lambda p,i:(0,p)),
            pl.BlockSpec((keys,PAIR), lambda p,i:(0,p)),
        ],
        out_shape=[jax.ShapeDtypeStruct((rows,pairs*PAIR),BF16)]+[jax.ShapeDtypeStruct((keys,pairs*PAIR),BF16)]*2,
        scratch_shapes=[pltpu.VMEM((2,keys,PAIR),BF16), pltpu.VMEM((2,PAIR,keys),BF16), pltpu.VMEM((2,keys,PAIR),BF16), pltpu.VMEM((keys,PAIR),F32), pltpu.VMEM((keys,PAIR),F32)],
        compiler_params=pltpu.CompilerParams(vmem_limit_bytes=48<<20),
        cost_estimate=pl.CostEstimate(flops=10*rows*keys*PAIR*pairs*2, bytes_accessed=2*(4*rows+4*keys)*PAIR*pairs, transcendentals=rows*keys*2*pairs),
    )(*args)


def whole_rows(ref):
    x = ref[...]
    return x.reshape(-1, x.shape[-1]) if x.ndim == 3 else x


def rows_spec(block, cols, start=0):
    return pl.BlockSpec((block, cols), lambda i: (start + i, 0))


def weight_spec(w, rows, cols, at):
    if w.ndim == 3:
        return pl.BlockSpec((w.shape[0], rows, cols), lambda i: (0, 0, at))
    return pl.BlockSpec((w.shape[0], cols), lambda i: (0, at))


def call_rows(kernel, rows, block, in_specs, outs, args, flops, scratch=()):
    return pl.pallas_call(
        kernel,
        grid=(rows // block,),
        in_specs=in_specs,
        out_specs=[rows_spec(block, cols) for cols, _ in outs],
        out_shape=[jax.ShapeDtypeStruct((rows, cols), kind) for cols, kind in outs],
        scratch_shapes=list(scratch),
        compiler_params=pltpu.CompilerParams(vmem_limit_bytes=52 << 20),
        cost_estimate=pl.CostEstimate(
            flops=flops, bytes_accessed=sum(2 * x.size for x in args), transcendentals=0
        ),
    )(*args)


def project_kernel(x_ref, near_ref, far_ref, o_ref):
    near, far = whole_rows(near_ref), whole_rows(far_ref)
    half = near.shape[0]
    o_ref[...] = (mm(x_ref[:, :half], near) + mm(x_ref[:, half:], far)).astype(o_ref.dtype)


def project(x, near, far, rows_each, cols, at, kind=BF16, block=512):
    rows, width = x.shape
    spec = weight_spec(near, rows_each, cols, at)
    return call_rows(
        project_kernel,
        rows,
        block,
        [rows_spec(block, width), spec, spec],
        [(cols, kind)],
        (x, near, far),
        2 * rows * width * cols,
    )[0]


def ordered(near, far, order, scratch_ref):
    if order is None:
        return near, far
    rows = 2 * near.shape[0] // len(order)

    @pl.when(pl.program_id(0) == 0)
    def _():
        half = len(order) // 2
        for i, place in enumerate(order):
            source = near if i < half else far
            scratch_ref[place * rows : (place + 1) * rows] = source[
                i % half * rows : (i % half + 1) * rows
            ]

    return scratch_ref[: near.shape[0]], scratch_ref[near.shape[0] :]


def branch_kernel(*refs, order):
    count = len(refs) - (1 if order is None else 2)
    out_ref = refs[count]
    near_sum = far_sum = None
    for i in range(0, count, 3):
        x, near, far = refs[i][...], whole_rows(refs[i + 1]), whole_rows(refs[i + 2])
        near, far = ordered(near, far, order, refs[-1])
        a, b = mm_nt(x, near), mm_nt(x, far)
        near_sum = a if near_sum is None else near_sum + a
        far_sum = b if far_sum is None else far_sum + b
    half = near_sum.shape[1]
    out_ref[:, :half] = near_sum.astype(out_ref.dtype)
    out_ref[:, half:] = far_sum.astype(out_ref.dtype)


def branch_rows(terms, start, rows, kind, rows_each, width, order=None, block=512):
    specs, args, flops = [], [], 0
    for x, near, far, at in terms:
        cols = x.shape[1]
        spec = weight_spec(near, rows_each, cols, at)
        specs += [rows_spec(block, cols, start // block), spec, spec]
        args += [x, near, far]
        flops += 2 * rows * cols * width
    scratch = [] if order is None else [pltpu.VMEM((width, terms[0][0].shape[1]), BF16)]
    return call_rows(
        functools.partial(branch_kernel, order=order),
        rows,
        block,
        specs,
        [(width, kind)],
        args,
        flops,
        scratch,
    )[0]


def weight_kernel(*refs, count, blocks):
    out_ref = refs[-1]
    at = 0
    for i in range(count):
        x_ref, y = refs[2 * i], refs[2 * i + 1][...]
        cols = y.shape[1]
        for j in range(0, x_ref.shape[1], 256):
            product = mm_tn(x_ref[:, j : j + 256], y)
            out_ref[j : j + 256, at : at + cols] = product.astype(BF16)
        at += cols
    if blocks:
        product = mm_tn(refs[2 * count][...], refs[2 * count + 1][...]).astype(BF16)
        rows, cols = product.shape[0] // blocks, product.shape[1] // 2
        for b in range(blocks):
            for i in range(2):
                out_ref[(2 * b + i) * rows : (2 * b + i + 1) * rows, at:] = product[
                    b * rows : (b + 1) * rows, i * cols : (i + 1) * cols
                ]


def weight_half(pairs, at, small=None, blocks=0):
    specs, args, cols = [], [], 0
    for x, y in pairs:
        specs.append(pl.BlockSpec((x.shape[0], x.shape[1] // 2), lambda i: (0, at)))
        specs.append(pl.BlockSpec(y.shape, lambda i: (0, 0)))
        args += [x, y]
        cols += y.shape[1]
    if small is not None:
        x, y = small
        specs.append(pl.BlockSpec((x.shape[0], x.shape[1] // 2), lambda i: (0, at)))
        specs.append(pl.BlockSpec(y.shape, lambda i: (0, 0)))
        args += [x, y]
        cols += y.shape[1] // 2
    rows = pairs[0][0].shape[1] // 2
    return call_rows(
        functools.partial(weight_kernel, count=len(pairs), blocks=blocks),
        rows,
        rows,
        specs,
        [(cols, BF16)],
        args,
        2 * rows * pairs[0][0].shape[0] * cols,
    )[0]


def hidden_kernel(x_ref, near_ref, far_ref, gate_ref, up_ref, hidden_ref):
    half = near_ref.shape[0]
    up = mm(x_ref[:, :half], near_ref[...]) + mm(x_ref[:, half:], far_ref[...])
    gate = gate_ref[...]
    up_ref[...] = up
    hidden_ref[...] = (gate * jax.nn.sigmoid(gate) * up).astype(BF16)


def hidden_forward(x, up_w, gate, block=512):
    rows, width = x.shape
    ff = gate.shape[1]
    spec = pl.BlockSpec((width // 2, ff), lambda i: (0, 0))
    return call_rows(
        hidden_kernel,
        rows,
        block,
        [rows_spec(block, width), spec, spec, rows_spec(block, ff)],
        [(ff, F32), (ff, BF16)],
        (x, *up_w, gate),
        2 * rows * width * ff,
    )


def hidden_back_kernel(
    g_ref, near_ref, far_ref, gate_ref, up_ref, grad_gate_ref, grad_up_ref, scratch_ref, *, order
):
    half = near_ref.shape[0]
    near, far = ordered(near_ref[...], far_ref[...], order, scratch_ref)
    grad = mm(g_ref[:, :half], near) + mm(g_ref[:, half:], far)
    gate, up = gate_ref[...], up_ref[...]
    s = jax.nn.sigmoid(gate)
    grad_gate_ref[...] = (grad * up * s * (1.0 + gate * (1.0 - s))).astype(BF16)
    grad_up_ref[...] = (grad * gate * s).astype(BF16)


def hidden_backward(g, down_w, gate, up, order, block=256):
    rows, width = g.shape
    ff = gate.shape[1]
    spec = pl.BlockSpec((width // 2, ff), lambda i: (0, 0))
    return call_rows(
        functools.partial(hidden_back_kernel, order=order),
        rows,
        block,
        [rows_spec(block, width), spec, spec, rows_spec(block, ff), rows_spec(block, ff)],
        [(ff, BF16), (ff, BF16)],
        (g, *down_w, gate, up),
        2 * rows * width * ff,
        [pltpu.VMEM((width, ff), BF16)],
    )


def centered_rows(x):
    centered = x - jnp.mean(x, axis=-1, keepdims=True)
    inverse = lax.rsqrt(jnp.mean(centered * centered, axis=-1, keepdims=True) + epsilon)
    return centered * inverse, inverse


def add_norm_kernel(stream_ref, kept_ref, got_ref, far_ref, gain_ref, sum_ref, normed_ref):
    total = stream_ref[...].astype(F32) + (
        kept_ref[...] + got_ref[...].astype(F32) + far_ref[...].astype(F32)
    )
    sum_ref[...] = total
    normed_ref[...] = (centered_rows(total)[0] * gain_ref[...]).astype(BF16)


def add_norm(stream, kept, got, far, gain, at):
    rows, width = far.shape
    own, part = rows_spec(rows, width), rows_spec(rows, width, at)
    return call_rows(
        add_norm_kernel,
        rows,
        rows,
        [part if stream.shape[0] > rows else own, part, part, own]
        + [pl.BlockSpec((1, width), lambda i: (0, 0))],
        [(width, F32), (width, BF16)],
        (stream, kept, got, far, gain.reshape(1, width)),
        0,
    )


def norm_back_kernel(
    upper_ref, kept_ref, got_ref, far_ref, stream_ref, gain_ref, total_ref, low_ref, gain_grad_ref
):
    upstream = kept_ref[...] + got_ref[...].astype(F32) + far_ref[...].astype(F32)
    scaled, inverse = centered_rows(stream_ref[...].astype(F32))
    weighted = upstream * gain_ref[...]
    grad = inverse * (
        weighted
        - jnp.mean(weighted, axis=-1, keepdims=True)
        - scaled * jnp.mean(weighted * scaled, axis=-1, keepdims=True)
    )
    total = upper_ref[...] + grad
    total_ref[...] = total
    low_ref[...] = total.astype(BF16)

    @pl.when(pl.program_id(0) == 0)
    def _():
        gain_grad_ref[...] = jnp.zeros_like(gain_grad_ref)

    gain_grad_ref[...] += jnp.sum(upstream * scaled, axis=0, keepdims=True)


def norm_back(upper, kept, got, far, stream, gain, at):
    rows, width = far.shape
    own, part = rows_spec(rows, width), rows_spec(rows, width, at)
    row = pl.BlockSpec((1, width), lambda i: (0, 0))
    total, small, gain_grad = pl.pallas_call(
        norm_back_kernel,
        grid=(1,),
        in_specs=[own, part, part, own, part if stream.shape[0] > rows else own, row],
        out_specs=[own, own, row],
        out_shape=[
            jax.ShapeDtypeStruct((rows, width), F32),
            jax.ShapeDtypeStruct((rows, width), BF16),
            jax.ShapeDtypeStruct((1, width), F32),
        ],
        compiler_params=pltpu.CompilerParams(vmem_limit_bytes=32 << 20),
        cost_estimate=pl.CostEstimate(flops=0, bytes_accessed=20 * rows * width, transcendentals=0),
    )(upper, kept, got, far, stream, gain.reshape(1, width))
    return total, small, gain_grad[0]


def qkv_kernel(x_ref, near_ref, far_ref, cos_ref, sin_ref, o_ref):
    half = near_ref.shape[0]
    y = mm(x_ref[:, :half], near_ref[...]) + mm(x_ref[:, half:], far_ref[...])
    cos, sin = cos_ref[...], sin_ref[...]
    turned = 2 * (y.shape[1] // 3)
    for at in range(0, turned, PAIR):
        o_ref[:, at : at + PAIR] = turn(y[:, at : at + PAIR], cos, sin).astype(BF16)
    o_ref[:, turned:] = y[:, turned:].astype(BF16)


def project_heads(x, near, far, cols, tables, block):
    rows, width = x.shape
    return pl.pallas_call(
        qkv_kernel,
        grid=(rows // block,),
        in_specs=[
            pl.BlockSpec((block, width), lambda i: (i, 0)),
            pl.BlockSpec((width // 2, cols), lambda i: (0, 0)),
            pl.BlockSpec((width // 2, cols), lambda i: (0, 0)),
            pl.BlockSpec((block, PAIR), lambda i: (i, 0)),
            pl.BlockSpec((block, PAIR), lambda i: (i, 0)),
        ],
        out_specs=pl.BlockSpec((block, cols), lambda i: (i, 0)),
        out_shape=jax.ShapeDtypeStruct((rows, cols), BF16),
        compiler_params=pltpu.CompilerParams(vmem_limit_bytes=48 << 20),
        cost_estimate=pl.CostEstimate(
            flops=2 * rows * width * cols, bytes_accessed=2 * (rows + cols) * width, transcendentals=0
        ),
    )(x, near, far, *tables)


class Links:
    def __init__(self, move):
        self.move = move
        self.flying = {}

    def tick(self, values, advance="", start=()):
        values = list(values) if isinstance(values, (tuple, list)) else [values]
        count = len(values)
        asked = advance.split()
        held_back = {name.strip("_") for name in asked if name.endswith("_")}
        names = [name.strip("_") for name in asked if name.strip("_") in self.flying]
        chains = [self.flying.pop(name) for name in names]
        operands = [values, [], []]
        for _, got, state in chains:
            operands[1].append((got, state))
        for _, _, arrays in start:
            operands[2].append(list(arrays))
        values, held, begun = lax.optimization_barrier(operands)
        moving, done = [], []
        for name, (chain, _, _), (got, state) in zip(names, chains, held):
            if name in held_back:
                self.flying[name] = (chain, got, state)
                continue
            try:
                moving.append((name, chain, *chain.send((got, state))))
            except StopIteration as end:
                done.append(end.value)
        for (name, make, _), arrays in zip(start, begun):
            chain = make(*arrays)
            moving.append((name, chain, *next(chain)))
        values, sent, results = lax.optimization_barrier(
            [
                values,
                [[x for _, x in moves] for _, _, moves, _ in moving],
                [result for _, _, result in done],
            ]
        )
        for (out, name, _), result in zip(done, results):
            out[name] = result
        for (name, chain, moves, state), xs in zip(moving, sent):
            got = [self.move(kind, x) for (kind, _), x in zip(moves, xs)]
            self.flying[name] = (chain, got, state)
        return values[0] if count == 1 else tuple(values)

    def finish(self, *names):
        for name in names:
            while name in self.flying:
                self.tick((), name)


def arrange_in_kernel(row_ref, col_ref, side_ref, x_ref, out_ref):
    count = out_ref.shape[1] // PAIR // 3
    width = 3 * HEAD_DIM
    side = side_ref[0]
    at = lax.broadcasted_iota(jnp.int32, (out_ref.shape[0], 2 * width), 1)
    for j in range(count):
        other = j >= count // 2
        pieces = []
        for i in range(2):
            source = col_ref[(2 * j + i) % count]
            piece = x_ref[:, pl.ds(pl.multiple_of(source * 2 * width, 2 * width), 2 * width)]
            pieces.append(piece.astype(F32))
        first, second = pieces
        own_first = jnp.where(at < width, first, pltpu.roll(second, width, 1))
        own_second = jnp.where(at < width, pltpu.roll(first, width, 1), second)
        want_first = (side == 1) if other else (side == 0)
        out = jnp.where(want_first, own_first, own_second)
        out_ref[:, j * 2 * width : (j + 1) * 2 * width] = out.astype(out_ref.dtype)


def arrange_out_kernel(row_ref, col_ref, side_ref, x_ref, out_ref):
    count = out_ref.shape[1] // PAIR // 3
    width = 3 * HEAD_DIM
    side = side_ref[0]
    half = count // 2
    at = lax.broadcasted_iota(jnp.int32, (out_ref.shape[0], 2 * width), 1)
    for j in range(half):
        own = x_ref[:, j * 2 * width : (j + 1) * 2 * width].astype(F32)
        other = x_ref[:, (half + j) * 2 * width : (half + j + 1) * 2 * width].astype(F32)
        first = jnp.where(side == 0, own, other)
        second = jnp.where(side == 0, other, own)
        made = (
            jnp.where(at < width, first, pltpu.roll(second, width, 1)),
            jnp.where(at < width, pltpu.roll(first, width, 1), second),
        )
        for i in range(2):
            place = col_ref[2 * j + i]
            out_ref[:, pl.ds(pl.multiple_of(place * 2 * width, 2 * width), 2 * width)] = made[
                i
            ].astype(out_ref.dtype)


def arrange(x, row_at, col_at, side, rows, shard, out_type, back):
    count, total = row_at.shape[0], x.shape[1]
    pairs = col_at.shape[0]
    if shard != 3 * HEAD_DIM or pairs % 2:
        shard_at = jnp.concatenate([col_at * 2 + side, col_at * 2 + 1 - side])
        blocks = x.reshape(-1, rows, 2 * pairs, shard)
        if back:
            blocks = jnp.zeros_like(blocks).at[row_at].set(blocks)
            blocks = jnp.zeros_like(blocks).at[:, :, shard_at].set(blocks)
        else:
            blocks = blocks[row_at][:, :, shard_at]
        return blocks.reshape(-1, total).astype(out_type)

    def here(i, row_at, col_at, side):
        return i, 0

    def there(i, row_at, col_at, side):
        return row_at[i], 0

    return pl.pallas_call(
        arrange_out_kernel if back else arrange_in_kernel,
        grid_spec=pltpu.PrefetchScalarGridSpec(
            num_scalar_prefetch=3,
            grid=(count,),
            in_specs=[pl.BlockSpec((rows, total), here if back else there)],
            out_specs=pl.BlockSpec((rows, total), there if back else here),
        ),
        out_shape=jax.ShapeDtypeStruct((count * rows, total), out_type),
        compiler_params=pltpu.CompilerParams(vmem_limit_bytes=32 << 20),
        cost_estimate=pl.CostEstimate(
            flops=0, bytes_accessed=6 * count * rows * total, transcendentals=0
        ),
    )(row_at, col_at, side.reshape(1), x)


def build(n_dp, n_tensor):
    tensor_bits = []
    bit = 1
    while bit < n_tensor:
        tensor_bits.append(bit)
        bit *= 2
    dp_bits = []
    bit = 1
    while bit < n_dp:
        dp_bits.append(bit)
        bit *= 2
    far_first = list(reversed(dp_bits))
    pair_first = [1] + far_first[:-1]
    near_first = dp_bits
    pair_last = dp_bits[1:] + [1]
    offsets = [0]
    for bit in far_first:
        offsets = offsets + [o ^ bit for o in offsets]
    order = [0]
    for bit in reversed(tensor_bits):
        order = order + [o ^ bit for o in order]

    def swap(x, bit):
        return lax.ppermute(x, "tensor", [(i, i ^ bit) for i in range(n_tensor)])

    def swap_dp(x, bit):
        return lax.ppermute(x, "dp", [(i, i ^ bit) for i in range(n_dp)])

    def gather_rows(own):
        for bit in reversed(tensor_bits):
            own = jnp.concatenate([own, swap(own, bit)], axis=0)
        return own

    def scatter_near(make, rows):
        half = rows // 2
        got = swap(make(half, half, BF16), tensor_bits[0])
        return make(0, half, F32), got

    def exchange(near, work, beside=(None, None)):
        kept, got = near
        rows = kept.shape[0] // 4
        far_bit, near_bit = tensor_bits[1], tensor_bits[0]
        fars = []
        for i in range(2):
            part = slice((2 + i) * rows, (3 + i) * rows)
            fars.append(swap(low(kept[part] + wide(got[part])), far_bit))
        first, second = beside
        if first is not None:
            fars, first = lax.optimization_barrier((fars, first))
        done = [work(i, kept, got, fars[i]) for i in range(2)]
        mine = [rows_low for _, rows_low in done]
        others = [swap(rows_low, far_bit) for rows_low in mine]
        if second is not None:
            others, second = lax.optimization_barrier((others, second))
        half = jnp.concatenate(mine + others, axis=0)
        everyone = jnp.concatenate([half, swap(half, near_bit)], axis=0)
        if first is None and second is None:
            return [out for out, _ in done], everyone
        return [out for out, _ in done], everyone, first, second

    def sum_tensor(x):
        for bit in tensor_bits:
            x = x + swap(x, bit)
        return x

    def sum_dp(x):
        for bit in dp_bits:
            x = x + swap_dp(x, bit)
        return x

    def body(
        hidden_in,
        conditioning,
        valid_mask,
        teacher,
        gain_one,
        gain_two,
        gain_three,
        self_in_weight,
        self_out_weight,
        cross_query_weight,
        cross_memory_weight,
        cross_out_weight,
        gate_up_weight,
        down_weight,
    ):
        _, length, width = hidden_in.shape
        cond_tokens, cond_width = conditioning.shape[1:]
        me = lax.axis_index("tensor")
        dp_me = lax.axis_index("dp")
        shard = width // n_dp
        own_rows = length // n_tensor

        running = valid_mask[0, 0] > 0

        def stage(work, *args):
            def skipped(*args):
                return jax.tree.map(
                    lambda x: jnp.zeros(x.shape, x.dtype), jax.eval_shape(work, *args)
                )

            return lax.cond(running, work, skipped, *args)

        def move(kind, x):
            axis, bit = kind
            return swap(x, bit) if axis == "tensor" else swap_dp(x, bit)

        later = {}
        links = Links(move)
        tick = links.tick

        def gather_double(own, out, name, bits):
            near, far = own, None
            for bit in bits:
                near = near if far is None else jnp.concatenate([near, far], axis=0)
                (far,), near = yield [(("dp", bit), near)], near
            return out, name, (near, far)

        def gather_direct(own, out, name):
            rows = own.shape[0]
            (two, four, one), own = (
                yield [(("dp", 2), own), (("dp", 4), own), (("dp", 1), own)],
                own,
            )
            both = jnp.concatenate([two, four], axis=0)
            (six, both), (own, one, two, four) = (
                yield [(("dp", 6), own), (("dp", 1), both)],
                (own, one, two, four),
            )
            three, five = both[:rows], both[rows:]
            (seven,), shards = (
                yield [(("dp", 1), six)],
                [own, one, two, three, four, five, six],
            )
            shards = shards + [seven]
            half = len(offsets) // 2
            return out, name, tuple(
                jnp.concatenate([shards[o] for o in part], axis=0)
                for part in (offsets[:half], offsets[half:])
            )

        def reduce_halve(*halves, out, name, own=None):
            rows = halves[-1].shape[0]

            def total(terms, at):
                return sum(wide(t[at : at + rows]) for t in terms)

            (got,), terms = yield [(("dp", 1), halves[-1])], list(halves[:-1])
            terms = (terms if own is None else [later[own]]) + [got]
            for bit in near_first[1:]:
                rows = rows // 2
                (got,), terms = yield [(("dp", bit), low(total(terms, rows)))], terms
                terms = terms + [got]
            return out, name, total(terms, 0)

        def reduce_direct(near, far, out, name):
            rows = near.shape[0] // 4

            def block(halves, offset):
                at = offsets.index(offset)
                return halves[at // 4][at % 4 * rows : (at % 4 + 1) * rows]

            def add(*xs):
                return sum(wide(x) for x in xs)

            halves = [near, far]
            (got,), halves = yield [(("dp", 1), block(halves, 7))], halves
            six = low(add(block(halves, 6), got))
            both = jnp.concatenate([block(halves, 5), block(halves, 3)], axis=0)
            (six, both), halves = yield [(("dp", 6), six), (("dp", 1), both)], halves
            four = low(add(block(halves, 4), both[:rows]))
            two = low(add(block(halves, 2), both[rows:]))
            (four, two, one), (halves, six) = (
                yield [(("dp", 4), four), (("dp", 2), two), (("dp", 1), block(halves, 1))],
                (halves, six),
            )
            return out, name, add(block(halves, 0), six, four, two, one)

        if n_dp != 8:
            gather_direct = functools.partial(gather_double, bits=far_first)
            reduce_direct = reduce_halve

        def output_chain(own, out, name):
            for bit in reversed(tensor_bits):
                (got,), own = yield [(("tensor", bit), own)], own
                own = jnp.concatenate([own, got], axis=0)
            return out, name, own

        local = self_in_weight.shape[2]
        ff = down_weight.shape[0]
        first = jnp.concatenate([self_in_weight.reshape(shard, 3 * local), self_out_weight.T], axis=1)
        gate_up_own = gate_up_weight.reshape(shard, 2 * ff)
        full = {}

        def gathering(name, own, bits):
            return name, functools.partial(gather_double, out=full, name=name, bits=bits), [own]

        cross_rows = shard + cond_width // n_dp
        start_cross = gathering(
            "cross",
            jnp.concatenate(
                [
                    jnp.concatenate([cross_query_weight, cross_out_weight.T], axis=1),
                    cross_memory_weight.reshape(cond_width // n_dp, 2 * local),
                ],
                axis=0,
            ),
            far_first,
        )
        start_up_a = gathering("up_a", gate_up_own[:, :ff], far_first)
        start_up_b = gathering("up_b", gate_up_own[:, ff:], far_first)
        start_down = gathering("down", down_weight.T, pair_first)
        count = jnp.sum(valid_mask)
        count_row = jnp.zeros((shard,), F32).at[0].set(wide(count // 32)).at[1].set(wide(count % 32))
        gains_own = jnp.concatenate([gain_one, gain_two, gain_three, low(count_row)])[None]
        hidden_raw = tick(
            hidden_in[0],
            "",
            [
                gathering("gains", gains_own, far_first),
                ("first", functools.partial(gather_direct, out=full, name="first"), [first]),
            ],
        )

        pairs = local // PAIR
        rows = length
        mine = slice(0, own_rows)
        row_at = me ^ jnp.array(order, jnp.int32)
        col_at = (dp_me // 2) ^ jnp.array([o // 2 for o in offsets[: n_dp // 2]], jnp.int32)
        side = dp_me % 2

        def arrange_in(x, row_at):
            return arrange(x, row_at, col_at, side, own_rows, shard, BF16, False)

        def take(x, owner):
            return lax.dynamic_slice_in_dim(x, owner * own_rows, own_rows, 0)

        def center(x):
            return wide(x) - jnp.mean(wide(x), axis=-1, keepdims=True)

        def join(halves):
            return jnp.concatenate(halves, axis=0)

        hidden_raw, teacher_raw = tick((hidden_raw, teacher[0]), "gains")
        hidden = arrange_in(hidden_raw, row_at)
        hidden, me_late = tick((hidden, me), "first gains")
        centered = center(hidden)
        inverse_all = lax.rsqrt(jnp.mean(centered * centered, axis=-1, keepdims=True) + epsilon)

        def relative_late(x):
            return jnp.concatenate([take(x, me_late ^ o) for o in order], axis=0)

        position = relative_late(jnp.arange(length, dtype=F32)[:, None])
        lane = jnp.arange(PAIR) % HEAD_DIM
        frequency = jnp.exp((lane % (ROT // 2)).astype(F32) * (-2.0 * math.log(10000.0) / ROT))
        angles = position * frequency[None, :]
        cosine, sine = jnp.cos(angles), jnp.sin(angles)
        tables = (
            jnp.where(lane < ROT, cosine, 1.0),
            jnp.where(lane < ROT // 2, -sine, jnp.where(lane < ROT, sine, 0.0)),
        )
        bias = jnp.where(relative_late(valid_mask[0][:, None]) > 0, 0.0, masked_score)
        cosine, sine, hidden, inverse_all, teacher_raw = tick(
            (*tables, hidden, inverse_all, teacher_raw), "first gains", [start_cross]
        )
        tables = (cosine, sine)
        links.finish("gains")
        gains = jnp.concatenate(full["gains"], axis=0).reshape(n_dp, 4, shard)
        counts = wide(gains[:, 3])
        token_count = jnp.sum(32.0 * counts[:, 0] + counts[:, 1])
        gain_first, gain_second, gain_third = (wide(gains[:, i]).reshape(width) for i in range(3))
        normed_one = low(center(hidden) * inverse_all * gain_first)
        target_low = arrange_in(teacher_raw, me.reshape(1))
        residual = wide(hidden[mine])
        normed_one, target_low, bias = tick(
            (normed_one, target_low, bias), "first cross", [start_up_a, start_down]
        )
        links.finish("first")
        first_near, first_far = full["first"]
        cond_shard = cond_width // n_dp
        place = jnp.arange(cond_width)
        offset = sum(
            ((place // cond_shard >> i) % 2) * bit for i, bit in enumerate(far_first)
        )
        source = (dp_me ^ offset) * cond_shard + place % cond_shard
        cond_place = place[:, None] == source[None, :]
        memory_input = low(dot(conditioning[0], low(cond_place)))
        pad_tokens = -cond_tokens % 16
        cond_rows = cond_tokens + pad_tokens
        cond_bias = jnp.where(jnp.arange(cond_rows)[:, None] < cond_tokens, 0.0, masked_score)

        def branch(rows_each, *terms, order=None):
            return scatter_near(
                lambda start, count, kind: branch_rows(
                    terms, start, count, kind, rows_each, width, order
                ),
                rows,
            )

        def self_attention(normed_one, first_near, first_far, cos, sin, bias):
            mixed = project_heads(normed_one, first_near, first_far, 3 * local, (cos, sin), 512)
            attended, self_totals = attend_forward(
                mixed, mixed, mixed, 0, pairs, 2 * pairs, bias, pairs, rows
            )
            near = branch(0, (attended, first_near, first_far, 3))
            return mixed, attended, self_totals, near

        mixed, attended, self_totals, near = stage(
            self_attention, normed_one, first_near, first_far, *tables, bias
        )
        near = tick(near, "cross up_a down_", [start_up_b])

        def add_and_norm(streams, near, gain):
            def work(i, kept, got, far):
                return add_norm(streams[i], kept, got, far, gain, i)

            return exchange(near, work)

        after_self, normed_two = stage(add_and_norm, (residual, residual), near, gain_second)
        normed_two = tick(normed_two, "cross up_a up_b down")

        def unpack_memory(cross_near, cross_far):
            return [x[:, shard:].reshape(-1, 2 * local) for x in (cross_near, cross_far)]

        links.finish("cross")
        cross_w = [x.reshape(n_dp // 2, cross_rows, 2 * local) for x in full["cross"]]

        def cross_attention(normed_two, cross_near, cross_far):
            halves = unpack_memory(cross_near, cross_far)
            memory = sum(
                dot(memory_input[:, i * cond_width // 2 : (i + 1) * cond_width // 2], halves[i])
                for i in range(2)
            )
            cross_memory = jnp.pad(low(memory), ((0, pad_tokens), (0, 0)))
            cross_queries = project(normed_two, cross_near, cross_far, shard, local, 0)
            cross_attended, cross_totals = attend_forward(
                cross_queries, cross_memory, cross_memory, 0, 0, pairs, cond_bias, pairs, rows
            )
            near = branch(shard, (cross_attended, cross_near, cross_far, 1))
            return cross_queries, cross_memory, cross_attended, cross_totals, near

        cross_queries, cross_memory, cross_attended, cross_totals, near = stage(
            cross_attention, normed_two, *cross_w
        )
        near = tick(near, "up_b down")
        after_cross, normed_three = stage(add_and_norm, after_self, near, gain_third)
        normed_three = tick(normed_three, "up_a")
        links.finish("up_a")
        gate_value = stage(
            lambda x, a, b: project(x, a, b, 0, ff, 0, kind=F32), normed_three, *full["up_a"]
        )
        gate_value = tick(gate_value, "up_b")
        links.finish("up_a", "up_b")
        upward, hidden_units = stage(hidden_forward, normed_three, full["up_b"], gate_value)
        hidden_units = tick(hidden_units, "down")
        links.finish("down")
        down_got = [0]
        for bit in pair_first:
            down_got = down_got + [o ^ bit for o in down_got]
        down_order = tuple(offsets.index(o) for o in down_got)
        near = stage(
            lambda x, a, b: branch(0, (x, a, b, 0), order=down_order), hidden_units, *full["down"]
        )

        def final_rows(streams, near, target_low, valid_rows):
            def work(i, kept, got, far):
                rows = far.shape[0]
                part = slice(i * rows, (i + 1) * rows)
                final_state = streams[i] + (kept[part] + wide(got[part]) + wide(far))
                difference = final_state - wide(target_low[part])
                valid = valid_rows[part]
                losses = jnp.sum(valid[:, 0] * jnp.sum(difference * difference, axis=-1))
                grad_final = 2.0 * length / token_count * valid * difference
                return (low(final_state), losses, grad_final), low(grad_final)

            return exchange(near, work)

        valid_rows = wide(take(valid_mask[0][:, None], me))
        finals, grad_final_low = stage(final_rows, after_cross, near, target_low, valid_rows)
        final_low = join([final for final, _, _ in finals])
        losses = sum(loss for _, loss, _ in finals)
        grad_final = [grad for _, _, grad in finals]
        grads = {}

        def half_of(x, y, at):
            return weight_half([(x, y)], at)

        def halves_of(x, y):
            return half_of(x, y, 0), half_of(x, y, 1)

        def reducing(name, halves):
            return name, functools.partial(reduce_halve, out=grads, name=name), list(halves)

        others = {}

        def reducing_far(name, far):
            return (
                name,
                functools.partial(reduce_halve, out=grads, name=name, own=name),
                [far],
            )

        grad_final_low = tick(
            grad_final_low,
            "",
            [
                reducing_far("down", half_of(grad_final_low, hidden_units, 1)),
                (
                    "output",
                    functools.partial(output_chain, out=others, name="output"),
                    [final_low],
                ),
            ],
        )

        def hidden_back(grad_final_low, gate_value, upward, down_w, up_a, up_b):
            grad_gate, grad_up = hidden_backward(
                grad_final_low, down_w, gate_value, upward, down_order
            )
            return grad_gate, grad_up, branch(0, (grad_gate, *up_a, 0), (grad_up, *up_b, 0))

        grad_gate, grad_up, near = stage(
            hidden_back,
            grad_final_low,
            gate_value,
            upward,
            full["down"],
            full["up_a"],
            full["up_b"],
        )

        def back_rows(near, uppers, streams, gain, beside):
            def work(i, kept, got, far):
                total, small, gain_sum = norm_back(uppers[i], kept, got, far, streams[i], gain, i)
                return (total, gain_sum), small

            outs, rows_low, first, second = exchange(near, work, beside)
            return [out for out, _ in outs], sum(x for _, x in outs), rows_low, first, second

        near = tick(
            near, "output", [reducing_far("up_a", half_of(normed_three, grad_gate, 1))]
        )

        def back_three(near, normed_three, grad_gate, grad_up):
            own = half_of(normed_three, grad_up, 0)
            return (
                *back_rows(
                    near,
                    grad_final,
                    after_cross,
                    gain_third,
                    (
                        (
                            half_of(grad_final_low, hidden_units, 0),
                            half_of(normed_three, grad_gate, 0),
                        ),
                        half_of(normed_three, grad_up, 1),
                    ),
                ),
                own,
            )

        grad_after_cross, gain_three_sum, grad_cross_low, owns, far, own = stage(
            back_three, near, normed_three, grad_gate, grad_up
        )
        later["down"], later["up_a"] = owns
        grad_up_b = (own, far)
        grad_cross_low = tick(grad_cross_low, "down output", [reducing("up_b", grad_up_b)])

        def cross_back(grad_cross_low, cross_near, cross_far):
            grad_cross_attended = project(grad_cross_low, cross_near, cross_far, shard, local, 1)
            grad_cross_queries, grad_keys, grad_values = attend_backward(
                cross_queries,
                cross_memory,
                cross_memory,
                0,
                0,
                pairs,
                cond_bias,
                cross_totals,
                grad_cross_attended,
                None,
                pairs,
                rows,
            )
            near = branch(shard, (grad_cross_queries, cross_near, cross_far, 0))
            return grad_cross_queries, grad_keys, grad_values, near

        grad_cross_queries, grad_keys, grad_values, near = stage(
            cross_back, grad_cross_low, *cross_w
        )

        near = tick(near, "up_a")

        def arrange_out(x, out_type):
            return arrange(x, row_at, col_at, side, own_rows, shard, out_type, True)

        def back_two(
            near, grad_cross_queries, grad_keys, grad_values, grad_cross_low, rows_output
        ):
            grad_memory_low = jnp.concatenate(
                [grad_keys[:cond_tokens], grad_values[:cond_tokens]], axis=1
            )
            cond_part = lax.dot_general(
                dot_nt(grad_memory_low, join(unpack_memory(*cross_w))),
                wide(cond_place),
                (((1,), (1,)), ((), ())),
                precision=lax.Precision.HIGHEST,
            )
            products = ((normed_two, grad_cross_queries), (grad_cross_low, cross_attended))
            if n_dp == 8:
                packed = tuple(
                    weight_half(products, at, (memory_input, grad_memory_low), n_dp // 2)
                    for at in range(2)
                )
            else:
                packed = []
                for at in range(2):
                    memory = half_of(memory_input, grad_memory_low, at)
                    memory = memory.reshape(n_dp // 2, cond_shard, 2, local)
                    memory = memory.transpose(0, 2, 1, 3).reshape(-1, local)
                    packed.append(
                        jnp.concatenate([half_of(x, y, at) for x, y in products] + [memory], axis=1)
                    )
                packed = tuple(packed)
            cond_part = cond_part.reshape(-1, width)
            block_output = arrange_out(rows_output, BF16)
            return back_rows(
                near,
                grad_after_cross,
                after_self,
                gain_second,
                ((packed[0], cond_part), (packed[1], block_output)),
            )

        grad_after_self, gain_two_sum, grad_self_low, (pack_near, cond_part), (pack_far, block_output) = (
            stage(
                back_two,
                near,
                grad_cross_queries,
                grad_keys,
                grad_values,
                grad_cross_low,
                others["output"],
            )
        )
        grad_cross = (pack_near, pack_far)
        grad_self_low = tick(grad_self_low, "up_a down up_b", [reducing("cross", grad_cross)])

        def self_back(grad_self_low, first_near, first_far, cond_part):
            grad_attended = project(grad_self_low, first_near, first_far, 0, local, 3)
            grad_parts = attend_backward(
                mixed,
                mixed,
                mixed,
                0,
                pairs,
                2 * pairs,
                bias,
                self_totals,
                grad_attended,
                tables,
                pairs,
                rows,
            )
            products = [(normed_one, part) for part in grad_parts]
            return (
                list(grad_parts),
                [weight_half(products, at) for at in range(2)],
                halves_of(grad_self_low, attended),
                sum_tensor(cond_part),
            )

        grad_mixed, grad_self_in, grad_self_out, cond_sum = stage(
            self_back, grad_self_low, *full["first"], cond_part
        )
        grad_mixed = tick(
            grad_mixed,
            "up_a down up_b cross",
            [
                (
                    "self_in",
                    functools.partial(reduce_direct, out=grads, name="self_in"),
                    list(grad_self_in),
                ),
                reducing("self_out", grad_self_out),
            ],
        )
        def self_branch(grad_mixed, first_near, first_far):
            terms = [(part, first_near, first_far, i) for i, part in enumerate(grad_mixed)]
            return branch(0, *terms)

        near = stage(self_branch, grad_mixed, *full["first"])
        near = tick(near, "self_in cross self_out up_b")

        def small_sums(gain_one_sum):
            sums = jnp.stack([gain_one_sum, gain_two_sum, gain_three_sum]).reshape(3, n_dp, shard)
            sums = jnp.concatenate(
                [sums.transpose(1, 0, 2).reshape(n_dp, 3 * shard), jnp.full((n_dp, shard), losses)],
                axis=1,
            )
            for bit in near_first:
                half = sums.shape[0] // 2
                sums = sums[:half] + swap_dp(sums[half:], bit)
            return sum_tensor(sums)[0]

        def back_one(near):
            _, gain_one_sum, rows_hidden, _, _ = back_rows(
                near, grad_after_self, (hidden, hidden), gain_first, (gain_two_sum, gain_three_sum)
            )
            return rows_hidden, gain_one_sum

        rows_hidden, gain_one_sum = stage(back_one, near)
        rows_hidden, gain_one_sum = tick(
            (rows_hidden, gain_one_sum), "self_in cross self_out"
        )

        def last(rows_hidden, gain_one_sum, up_a, up_b):
            return (
                small_sums(gain_one_sum),
                arrange_out(rows_hidden, F32),
                jnp.stack([up_a, up_b], axis=1),
            )

        links.finish("up_a", "up_b")
        sums, grad_hidden, grad_gate_up = stage(
            last, rows_hidden, gain_one_sum, grads["up_a"], grads["up_b"]
        )
        sums, grad_hidden, grad_gate_up = tick(
            (sums, grad_hidden, grad_gate_up), "self_in self_out"
        )
        links.finish(*list(links.flying))

        grad_conditioning = cond_sum.reshape(cond_tokens, cond_width)
        mean_loss = sums[3 * shard] / (token_count * width)

        return (
            mean_loss,
            block_output[None],
            grad_hidden[None],
            grad_conditioning[None],
            sums[:shard],
            sums[shard : 2 * shard],
            sums[2 * shard : 3 * shard],
            grads["self_in"].reshape(shard, 3, local),
            grads["self_out"].T,
            grads["cross"][:, :local],
            jnp.stack(
                [grads["cross"][:cond_shard, 2 * local :], grads["cross"][cond_shard:, 2 * local :]],
                axis=1,
            ),
            grads["cross"][:, local : 2 * local].T,
            grad_gate_up,
            grads["down"].T,
        )

    return body


def solution(mesh):
    return jax.shard_map(
        build(mesh.shape["dp"], mesh.shape["tensor"]),
        mesh=mesh,
        in_specs=(
            P("dp", None, None),
            P("dp", None, None),
            P("dp", None),
            P("dp", None, None),
            P("dp"),
            P("dp"),
            P("dp"),
            P("dp", None, "tensor"),
            P("tensor", "dp"),
            P("dp", "tensor"),
            P("dp", None, "tensor"),
            P("tensor", "dp"),
            P("dp", None, "tensor"),
            P("tensor", "dp"),
        ),
        out_specs=(
            P(),
            P("dp", None, None),
            P("dp", None, None),
            P("dp", None, None),
            P("dp"),
            P("dp"),
            P("dp"),
            P("dp", None, "tensor"),
            P("tensor", "dp"),
            P("dp", "tensor"),
            P("dp", None, "tensor"),
            P("tensor", "dp"),
            P("dp", None, "tensor"),
            P("tensor", "dp"),
        ),
        check_vma=False,
    )
```

```python
import functools
import math

import jax
import jax.numpy as jnp
from jax import lax
from jax.experimental import pallas as pl
from jax.experimental.pallas import tpu as pltpu
from jax.sharding import PartitionSpec as P

HEAD_DIM = 64
ROT = 32
CHUNKS = 1

epsilon = 1e-05
masked_score = -1e30
F32 = jnp.float32
BF16 = jnp.bfloat16


def low(x):
    return x.astype(BF16)


def wide(x):
    return x.astype(F32)


def dot(a, b):
    return lax.dot_general(a, b, (((1,), (0,)), ((), ())), preferred_element_type=F32)


def dot_nt(a, b):
    return lax.dot_general(a, b, (((1,), (1,)), ((), ())), preferred_element_type=F32)


def dot_tn(a, b):
    return lax.dot_general(a, b, (((0,), (0,)), ((), ())), preferred_element_type=F32)


PAIR=128
SCALE=1.0/math.sqrt(HEAD_DIM)
SCALE2=SCALE*math.log2(math.e)

def mm(a,b): return lax.dot_general(a,b,(((1,),(0,)),((),())),preferred_element_type=F32)
def mm_nt(a,b): return lax.dot_general(a,b,(((1,),(1,)),((),())),preferred_element_type=F32)

def mm_tn(a,b): return lax.dot_general(a,b,(((0,),(0,)),((),())),preferred_element_type=F32)


def head_lanes(shape, axis, head):
    at = lax.broadcasted_iota(jnp.int32, shape, axis)
    return (at >= head*HEAD_DIM) & (at < (head+1)*HEAD_DIM)

def keep_head(x, axis, head):
    return jnp.where(head_lanes(x.shape, axis, head), x, jnp.zeros_like(x))

def with_lane(x, head, lane_value):
    at = lax.broadcasted_iota(jnp.int32, x.shape, 1)
    other = (1-head)*HEAD_DIM
    return jnp.where(at == other, lane_value, keep_head(x, 1, head))

def fwd_kernel(q_ref, k_ref, v_ref, bias_ref, o_ref, lse_ref, k_sc, vt_sc):
    @pl.when(pl.program_id(1) == 0)
    def _():
        k = k_ref[...].astype(F32)
        vt = v_ref[...].astype(F32).T
        for h in range(2):
            k_sc[h] = with_lane(k, h, bias_ref[...]).astype(BF16)
            vt_sc[h] = keep_head(vt, 0, h).astype(BF16)
    q = q_ref[...].astype(F32)
    out = None
    for h in range(2):
        qh = with_lane(q, h, 1.0).astype(BF16)
        s = mm_nt(k_sc[h], qh)
        m = jnp.max(s, axis=0, keepdims=True)
        e = jnp.exp2((s - m) * SCALE2)
        l = jnp.sum(e, axis=0, keepdims=True)
        o = mm(vt_sc[h], e.astype(BF16)) * (1.0 / l)
        out = o if out is None else out + o
        lse_ref[0, h:h+1, :] = m * SCALE2 + jnp.log2(l)
    o_ref[...] = out.T.astype(BF16)

def bwd_kernel(q_ref, k_ref, v_ref, bias_ref, lse_ref, g_ref, *rest, rotary):
    if rotary:
        cosq_ref, sinq_ref, cosk_ref, sink_ref, dq_ref, dk_ref, dv_ref, k_sc, kt_sc, v_sc, dk_sc, dv_sc = rest
    else:
        dq_ref, dk_ref, dv_ref, k_sc, kt_sc, v_sc, dk_sc, dv_sc = rest
    i = pl.program_id(1)
    @pl.when(i == 0)
    def _():
        k = k_ref[...].astype(F32)
        kt = k.T
        for h in range(2):
            k_sc[h] = with_lane(k, h, bias_ref[...]).astype(BF16)
            kt_sc[h] = keep_head(kt, 0, h).astype(BF16)
            v_sc[h] = keep_head(v_ref[...].astype(F32), 1, h).astype(BF16)
        dk_sc[...] = jnp.zeros_like(dk_sc)
        dv_sc[...] = jnp.zeros_like(dv_sc)
    q = q_ref[...].astype(F32)
    g32 = g_ref[...].astype(F32)
    g = g_ref[...]
    dqt = None
    dk = dk_sc[...]
    dv = dv_sc[...]
    for h in range(2):
        qa = with_lane(q, h, 1.0).astype(BF16)
        qh = keep_head(q, 1, h).astype(BF16)
        gh = keep_head(g32, 1, h).astype(BF16)
        s = mm_nt(k_sc[h], qa)
        p = jnp.exp2(s * SCALE2 - lse_ref[0, h:h+1, :])
        dp = mm_nt(v_sc[h], g)
        t = p * dp
        delta = jnp.sum(t, axis=0, keepdims=True)
        ds = (t - p * delta).astype(BF16)
        dv = dv + mm(p.astype(BF16), gh)
        dk = dk + mm(ds, qh)
        d = mm(kt_sc[h], ds)
        dqt = d if dqt is None else dqt + d
    dk_sc[...] = dk
    dv_sc[...] = dv
    dq = dqt.T * SCALE
    if rotary:
        dq = turn_back(dq, cosq_ref[...], sinq_ref[...])
    dq_ref[...] = dq.astype(BF16)
    @pl.when(i == pl.num_programs(1) - 1)
    def _():
        dk = dk_sc[...] * SCALE
        if rotary:
            dk = turn_back(dk, cosk_ref[...], sink_ref[...])
        dk_ref[...] = dk.astype(BF16)
        dv_ref[...] = dv_sc[...].astype(BF16)

def swap_halves(x):
    n = x.shape[1]
    at = lax.broadcasted_iota(jnp.int32, x.shape, 1) % HEAD_DIM
    return jnp.where(at < 16, pltpu.roll(x, n - 16, 1), pltpu.roll(x, 16, 1))

def turn(x, cos, sin):
    return x * cos + swap_halves(x) * sin

def turn_back(x, cos, sin):
    return x * cos - swap_halves(x) * sin

def attend_forward(q, k, v, qcol, kcol, vcol, bias, pairs, block):
    rows = q.shape[0]; keys = k.shape[0]
    return pl.pallas_call(
        fwd_kernel,
        grid=(pairs, rows//block),
        in_specs=[
            pl.BlockSpec((block,PAIR), lambda p,i:(i,qcol+p)),
            pl.BlockSpec((keys,PAIR), lambda p,i:(0,kcol+p)),
            pl.BlockSpec((keys,PAIR), lambda p,i:(0,vcol+p)),
            pl.BlockSpec((keys,1), lambda p,i:(0,0)),
        ],
        out_specs=[
            pl.BlockSpec((block,PAIR), lambda p,i:(i,p)),
            pl.BlockSpec((1,8,block), lambda p,i:(p,0,i)),
        ],
        out_shape=[jax.ShapeDtypeStruct((rows,pairs*PAIR),BF16), jax.ShapeDtypeStruct((pairs,8,rows),F32)],
        scratch_shapes=[pltpu.VMEM((2,keys,PAIR),BF16), pltpu.VMEM((2,PAIR,keys),BF16)],
        compiler_params=pltpu.CompilerParams(vmem_limit_bytes=48<<20),
        cost_estimate=pl.CostEstimate(flops=4*rows*keys*PAIR*pairs*2, bytes_accessed=2*(2*rows+2*keys)*PAIR*pairs, transcendentals=rows*keys*2*pairs),
    )(q,k,v,bias)

def attend_backward(q, k, v, qcol, kcol, vcol, bias, lse, g, tables, pairs, block):
    rows = q.shape[0]; keys = k.shape[0]
    rotary = tables is not None
    in_specs=[
        pl.BlockSpec((block,PAIR), lambda p,i:(i,qcol+p)),
        pl.BlockSpec((keys,PAIR), lambda p,i:(0,kcol+p)),
        pl.BlockSpec((keys,PAIR), lambda p,i:(0,vcol+p)),
        pl.BlockSpec((keys,1), lambda p,i:(0,0)),
        pl.BlockSpec((1,8,block), lambda p,i:(p,0,i)),
        pl.BlockSpec((block,PAIR), lambda p,i:(i,p)),
    ]
    args=[q,k,v,bias,lse,g]
    if rotary:
        in_specs += [pl.BlockSpec((block,PAIR), lambda p,i:(i,0))]*2 + [pl.BlockSpec((keys,PAIR), lambda p,i:(0,0))]*2
        args += [tables[0],tables[1],tables[0],tables[1]]
    return pl.pallas_call(
        functools.partial(bwd_kernel, rotary=rotary),
        grid=(pairs, rows//block),
        in_specs=in_specs,
        out_specs=[
            pl.BlockSpec((block,PAIR), lambda p,i:(i,p)),
            pl.BlockSpec((keys,PAIR), lambda p,i:(0,p)),
            pl.BlockSpec((keys,PAIR), lambda p,i:(0,p)),
        ],
        out_shape=[jax.ShapeDtypeStruct((rows,pairs*PAIR),BF16)]+[jax.ShapeDtypeStruct((keys,pairs*PAIR),BF16)]*2,
        scratch_shapes=[pltpu.VMEM((2,keys,PAIR),BF16), pltpu.VMEM((2,PAIR,keys),BF16), pltpu.VMEM((2,keys,PAIR),BF16), pltpu.VMEM((keys,PAIR),F32), pltpu.VMEM((keys,PAIR),F32)],
        compiler_params=pltpu.CompilerParams(vmem_limit_bytes=48<<20),
        cost_estimate=pl.CostEstimate(flops=10*rows*keys*PAIR*pairs*2, bytes_accessed=2*(4*rows+4*keys)*PAIR*pairs, transcendentals=rows*keys*2*pairs),
    )(*args)


def rows_spec(block, cols, start=0):
    return pl.BlockSpec((block, cols), lambda i: (start + i, 0))


def call_rows(kernel, rows, block, in_specs, outs, args, flops, scratch=()):
    return pl.pallas_call(
        kernel,
        grid=(rows // block,),
        in_specs=in_specs,
        out_specs=[rows_spec(block, cols) for cols, _ in outs],
        out_shape=[jax.ShapeDtypeStruct((rows, cols), kind) for cols, kind in outs],
        scratch_shapes=list(scratch),
        compiler_params=pltpu.CompilerParams(vmem_limit_bytes=56 << 20),
        cost_estimate=pl.CostEstimate(
            flops=flops, bytes_accessed=sum(2 * x.size for x in args), transcendentals=0
        ),
    )(*args)


class Weight:
    def __init__(self, pieces, places, rows):
        self.pieces, self.places, self.rows = list(pieces), tuple(places), rows

    def specs(self, cols, at):
        return [
            pl.BlockSpec((x.shape[0], self.rows, cols), lambda i: (0, 0, at))
            if x.ndim == 3
            else pl.BlockSpec((x.shape[0], cols), lambda i: (0, at))
            for x in self.pieces
        ]

    def scratch(self, cols):
        return pltpu.VMEM((len(self.places) * self.rows, cols), BF16)

    def assemble(self, refs, scratch_ref):
        rows, places = self.rows, list(self.places)

        @pl.when(pl.program_id(0) == 0)
        def _():
            left = list(places)
            for ref in refs:
                packed = len(ref.shape) == 3
                count = ref.shape[0] if packed else ref.shape[0] // rows
                for i in range(count):
                    place = left.pop(0)
                    source = ref[i] if packed else ref[i * rows : (i + 1) * rows]
                    scratch_ref[place * rows : (place + 1) * rows] = source

        return scratch_ref


def project_kernel(*refs, weight):
    x_ref, o_ref, scratch_ref = refs[0], refs[-2], refs[-1]
    w_ref = weight.assemble(refs[1:-2], scratch_ref)
    o_ref[...] = mm(x_ref[...], w_ref[...]).astype(o_ref.dtype)


def project(x, weight, cols, at, kind=BF16, block=512):
    rows, width = x.shape
    return call_rows(
        functools.partial(project_kernel, weight=weight),
        rows,
        block,
        [rows_spec(block, width)] + weight.specs(cols, at),
        [(cols, kind)],
        (x, *weight.pieces),
        2 * rows * width * cols,
        [weight.scratch(cols)],
    )[0]


def branch_kernel(*refs, weights):
    count = sum(1 + len(w.pieces) for w in weights)
    out_ref, scratches = refs[count], refs[count + 1 :]
    total, at = None, 0
    for weight, scratch_ref in zip(weights, scratches):
        x_ref, pieces = refs[at], refs[at + 1 : at + 1 + len(weight.pieces)]
        at += 1 + len(pieces)
        w_ref = weight.assemble(pieces, scratch_ref)
        product = mm_nt(x_ref[...], w_ref[...])
        total = product if total is None else total + product
    out_ref[...] = total.astype(out_ref.dtype)


def branch_rows(terms, start, rows, kind, width, block=512):
    specs, args, flops = [], [], 0
    for x, weight, at in terms:
        cols = x.shape[1]
        specs += [rows_spec(block, cols, start // block)] + weight.specs(cols, at)
        args += [x, *weight.pieces]
        flops += 2 * rows * cols * width
    return call_rows(
        functools.partial(branch_kernel, weights=[w for _, w, _ in terms]),
        rows,
        block,
        specs,
        [(width, kind)],
        args,
        flops,
        [w.scratch(x.shape[1]) for x, w, _ in terms],
    )[0]


def weight_kernel(*refs, count, blocks):
    out_ref = refs[-1]
    at = 0
    for i in range(count):
        x_ref, y = refs[2 * i], refs[2 * i + 1][...]
        cols = y.shape[1]
        for j in range(0, x_ref.shape[1], 256):
            product = mm_tn(x_ref[:, j : j + 256], y)
            out_ref[j : j + 256, at : at + cols] = product.astype(BF16)
        at += cols
    if blocks:
        product = mm_tn(refs[2 * count][...], refs[2 * count + 1][...]).astype(BF16)
        rows, cols = product.shape[0] // blocks, product.shape[1] // 2
        for b in range(blocks):
            for i in range(2):
                out_ref[(2 * b + i) * rows : (2 * b + i + 1) * rows, at:] = product[
                    b * rows : (b + 1) * rows, i * cols : (i + 1) * cols
                ]


def weight_half(pairs, at, small=None, blocks=0):
    specs, args, cols = [], [], 0
    for x, y in pairs:
        specs.append(pl.BlockSpec((x.shape[0], x.shape[1] // 2), lambda i: (0, at)))
        specs.append(pl.BlockSpec(y.shape, lambda i: (0, 0)))
        args += [x, y]
        cols += y.shape[1]
    if small is not None:
        x, y = small
        specs.append(pl.BlockSpec((x.shape[0], x.shape[1] // 2), lambda i: (0, at)))
        specs.append(pl.BlockSpec(y.shape, lambda i: (0, 0)))
        args += [x, y]
        cols += y.shape[1] // 2
    rows = pairs[0][0].shape[1] // 2
    return call_rows(
        functools.partial(weight_kernel, count=len(pairs), blocks=blocks),
        rows,
        rows,
        specs,
        [(cols, BF16)],
        args,
        2 * rows * pairs[0][0].shape[0] * cols,
    )[0]


def hidden_kernel(*refs, weight):
    x_ref, gate_ref = refs[0], refs[1]
    up_ref, hidden_ref, scratch_ref = refs[-3:]
    w_ref = weight.assemble(refs[2:-3], scratch_ref)
    up = mm(x_ref[...], w_ref[...])
    gate = gate_ref[...]
    up_ref[...] = up
    hidden_ref[...] = (gate * jax.nn.sigmoid(gate) * up).astype(BF16)


def hidden_forward(x, weight, gate, block=512):
    rows, width = x.shape
    ff = gate.shape[1]
    return call_rows(
        functools.partial(hidden_kernel, weight=weight),
        rows,
        block,
        [rows_spec(block, width), rows_spec(block, ff)] + weight.specs(ff, 0),
        [(ff, F32), (ff, BF16)],
        (x, gate, *weight.pieces),
        2 * rows * width * ff,
        [weight.scratch(ff)],
    )


def hidden_back_kernel(*refs, weight):
    g_ref, gate_ref, up_ref = refs[:3]
    grad_gate_ref, grad_up_ref, scratch_ref = refs[-3:]
    w_ref = weight.assemble(refs[3:-3], scratch_ref)
    grad = mm(g_ref[...], w_ref[...])
    gate, up = gate_ref[...], up_ref[...]
    s = jax.nn.sigmoid(gate)
    grad_gate_ref[...] = (grad * up * s * (1.0 + gate * (1.0 - s))).astype(BF16)
    grad_up_ref[...] = (grad * gate * s).astype(BF16)


def hidden_backward(g, weight, gate, up, block=512):
    rows, width = g.shape
    ff = gate.shape[1]
    return call_rows(
        functools.partial(hidden_back_kernel, weight=weight),
        rows,
        block,
        [rows_spec(block, width), rows_spec(block, ff), rows_spec(block, ff)] + weight.specs(ff, 0),
        [(ff, BF16), (ff, BF16)],
        (g, gate, up, *weight.pieces),
        2 * rows * width * ff,
        [weight.scratch(ff)],
    )


def centered_rows(x):
    centered = x - jnp.mean(x, axis=-1, keepdims=True)
    inverse = lax.rsqrt(jnp.mean(centered * centered, axis=-1, keepdims=True) + epsilon)
    return centered * inverse, inverse


def add_norm_kernel(stream_ref, kept_ref, got_ref, far_ref, gain_ref, sum_ref, normed_ref):
    total = stream_ref[...].astype(F32) + (
        kept_ref[...] + got_ref[...].astype(F32) + far_ref[...].astype(F32)
    )
    sum_ref[...] = total
    normed_ref[...] = (centered_rows(total)[0] * gain_ref[...]).astype(BF16)


def add_norm(stream, kept, got, far, gain, at):
    rows, width = far.shape
    own, part = rows_spec(rows, width), rows_spec(rows, width, at)
    return call_rows(
        add_norm_kernel,
        rows,
        rows,
        [part if stream.shape[0] > rows else own, part, part, own]
        + [pl.BlockSpec((1, width), lambda i: (0, 0))],
        [(width, F32), (width, BF16)],
        (stream, kept, got, far, gain.reshape(1, width)),
        0,
    )


def final_kernel(
    stream_ref, kept_ref, got_ref, far_ref, target_ref, valid_ref, factor_ref,
    final_ref, grad_ref, low_ref, loss_ref,
):
    final = stream_ref[...] + (
        kept_ref[...] + got_ref[...].astype(F32) + far_ref[...].astype(F32)
    )
    difference = final - target_ref[...].astype(F32)
    grad = factor_ref[...] * difference
    final_ref[...] = final.astype(BF16)
    grad_ref[...] = grad
    low_ref[...] = grad.astype(BF16)
    loss_ref[...] = jnp.sum(valid_ref[...] * (difference * difference), axis=0, keepdims=True)


def final_part(stream, kept, got, far, target, valid, factor, at):
    rows, width = far.shape
    own, part = rows_spec(rows, width), rows_spec(rows, width, at)
    column = pl.BlockSpec((rows, 1), lambda i: (at, 0))
    return pl.pallas_call(
        final_kernel,
        grid=(1,),
        in_specs=[own, part, part, own, part, column, column],
        out_specs=[own, own, own, pl.BlockSpec((1, width), lambda i: (0, 0))],
        out_shape=[
            jax.ShapeDtypeStruct((rows, width), BF16),
            jax.ShapeDtypeStruct((rows, width), F32),
            jax.ShapeDtypeStruct((rows, width), BF16),
            jax.ShapeDtypeStruct((1, width), F32),
        ],
        compiler_params=pltpu.CompilerParams(vmem_limit_bytes=32 << 20),
        cost_estimate=pl.CostEstimate(flops=0, bytes_accessed=20 * rows * width, transcendentals=0),
    )(stream, kept, got, far, target, valid, factor)


def norm_back_kernel(
    upper_ref, kept_ref, got_ref, far_ref, stream_ref, gain_ref, total_ref, low_ref, gain_grad_ref
):
    upstream = kept_ref[...] + got_ref[...].astype(F32) + far_ref[...].astype(F32)
    scaled, inverse = centered_rows(stream_ref[...].astype(F32))
    weighted = upstream * gain_ref[...]
    grad = inverse * (
        weighted
        - jnp.mean(weighted, axis=-1, keepdims=True)
        - scaled * jnp.mean(weighted * scaled, axis=-1, keepdims=True)
    )
    total = upper_ref[...] + grad
    total_ref[...] = total
    low_ref[...] = total.astype(BF16)

    @pl.when(pl.program_id(0) == 0)
    def _():
        gain_grad_ref[...] = jnp.zeros_like(gain_grad_ref)

    gain_grad_ref[...] += jnp.sum(upstream * scaled, axis=0, keepdims=True)


def norm_back(upper, kept, got, far, stream, gain, at):
    rows, width = far.shape
    own, part = rows_spec(rows, width), rows_spec(rows, width, at)
    row = pl.BlockSpec((1, width), lambda i: (0, 0))
    total, small, gain_grad = pl.pallas_call(
        norm_back_kernel,
        grid=(1,),
        in_specs=[own, part, part, own, part if stream.shape[0] > rows else own, row],
        out_specs=[own, own, row],
        out_shape=[
            jax.ShapeDtypeStruct((rows, width), F32),
            jax.ShapeDtypeStruct((rows, width), BF16),
            jax.ShapeDtypeStruct((1, width), F32),
        ],
        compiler_params=pltpu.CompilerParams(vmem_limit_bytes=32 << 20),
        cost_estimate=pl.CostEstimate(flops=0, bytes_accessed=20 * rows * width, transcendentals=0),
    )(upper, kept, got, far, stream, gain.reshape(1, width))
    return total, small, gain_grad[0]


def qkv_kernel(*refs, weight):
    x_ref, cos_ref, sin_ref = refs[:3]
    o_ref, scratch_ref = refs[-2:]
    w_ref = weight.assemble(refs[3:-2], scratch_ref)
    y = mm(x_ref[...], w_ref[...])
    cos, sin = cos_ref[...], sin_ref[...]
    turned = 2 * (y.shape[1] // 3)
    for at in range(0, turned, PAIR):
        o_ref[:, at : at + PAIR] = turn(y[:, at : at + PAIR], cos, sin).astype(BF16)
    o_ref[:, turned:] = y[:, turned:].astype(BF16)


def project_heads(x, weight, cols, tables, block):
    rows, width = x.shape
    return call_rows(
        functools.partial(qkv_kernel, weight=weight),
        rows,
        block,
        [rows_spec(block, width), rows_spec(block, PAIR), rows_spec(block, PAIR)]
        + weight.specs(cols, 0),
        [(cols, BF16)],
        (x, *tables, *weight.pieces),
        2 * rows * width * cols,
        [weight.scratch(cols)],
    )[0]


class Links:
    def __init__(self, move):
        self.move = move
        self.flying = {}

    def tick(self, values, advance="", start=()):
        values = list(values) if isinstance(values, (tuple, list)) else [values]
        count = len(values)
        asked = advance.split()
        held_back = {name.strip("_") for name in asked if name.endswith("_")}
        names = [name.strip("_") for name in asked if name.strip("_") in self.flying]
        chains = [self.flying.pop(name) for name in names]
        operands = [values, [], []]
        for _, got, state in chains:
            operands[1].append((got, state))
        for _, _, arrays in start:
            operands[2].append(list(arrays))
        values, held, begun = lax.optimization_barrier(operands)
        moving, done = [], []
        for name, (chain, _, _), (got, state) in zip(names, chains, held):
            if name in held_back:
                self.flying[name] = (chain, got, state)
                continue
            try:
                moving.append((name, chain, *chain.send((got, state))))
            except StopIteration as end:
                done.append(end.value)
        for (name, make, _), arrays in zip(start, begun):
            chain = make(*arrays)
            moving.append((name, chain, *next(chain)))
        values, sent, results = lax.optimization_barrier(
            [
                values,
                [[x for _, x in moves] for _, _, moves, _ in moving],
                [result for _, _, result in done],
            ]
        )
        for (out, name, _), result in zip(done, results):
            out[name] = result
        for (name, chain, moves, state), xs in zip(moving, sent):
            got = [self.move(kind, x) for (kind, _), x in zip(moves, xs)]
            self.flying[name] = (chain, got, state)
        return values[0] if count == 1 else tuple(values)

    def finish(self, *names):
        for name in names:
            while name in self.flying:
                self.tick((), name)


def arrange_in_kernel(row_ref, col_ref, side_ref, x_ref, out_ref):
    count = out_ref.shape[1] // PAIR // 3
    width = 3 * HEAD_DIM
    side = side_ref[0]
    at = lax.broadcasted_iota(jnp.int32, (out_ref.shape[0], 2 * width), 1)
    for j in range(count):
        other = j >= count // 2
        pieces = []
        for i in range(2):
            source = col_ref[(2 * j + i) % count]
            piece = x_ref[:, pl.ds(pl.multiple_of(source * 2 * width, 2 * width), 2 * width)]
            pieces.append(piece.astype(F32))
        first, second = pieces
        own_first = jnp.where(at < width, first, pltpu.roll(second, width, 1))
        own_second = jnp.where(at < width, pltpu.roll(first, width, 1), second)
        want_first = (side == 1) if other else (side == 0)
        out = jnp.where(want_first, own_first, own_second)
        out_ref[:, j * 2 * width : (j + 1) * 2 * width] = out.astype(out_ref.dtype)


def arrange_out_kernel(row_ref, col_ref, side_ref, x_ref, out_ref):
    count = out_ref.shape[1] // PAIR // 3
    width = 3 * HEAD_DIM
    side = side_ref[0]
    half = count // 2
    at = lax.broadcasted_iota(jnp.int32, (out_ref.shape[0], 2 * width), 1)
    for j in range(half):
        own = x_ref[:, j * 2 * width : (j + 1) * 2 * width].astype(F32)
        other = x_ref[:, (half + j) * 2 * width : (half + j + 1) * 2 * width].astype(F32)
        first = jnp.where(side == 0, own, other)
        second = jnp.where(side == 0, other, own)
        made = (
            jnp.where(at < width, first, pltpu.roll(second, width, 1)),
            jnp.where(at < width, pltpu.roll(first, width, 1), second),
        )
        for i in range(2):
            place = col_ref[2 * j + i]
            out_ref[:, pl.ds(pl.multiple_of(place * 2 * width, 2 * width), 2 * width)] = made[
                i
            ].astype(out_ref.dtype)


def arrange(x, row_at, col_at, side, rows, shard, out_type, back):
    count, total = row_at.shape[0], x.shape[1]
    pairs = col_at.shape[0]
    if shard != 3 * HEAD_DIM or pairs % 2:
        shard_at = jnp.concatenate([col_at * 2 + side, col_at * 2 + 1 - side])
        blocks = x.reshape(-1, rows, 2 * pairs, shard)
        if back:
            blocks = jnp.zeros_like(blocks).at[row_at].set(blocks)
            blocks = jnp.zeros_like(blocks).at[:, :, shard_at].set(blocks)
        else:
            blocks = blocks[row_at][:, :, shard_at]
        return blocks.reshape(-1, total).astype(out_type)

    def here(i, row_at, col_at, side):
        return i, 0

    def there(i, row_at, col_at, side):
        return row_at[i], 0

    return pl.pallas_call(
        arrange_out_kernel if back else arrange_in_kernel,
        grid_spec=pltpu.PrefetchScalarGridSpec(
            num_scalar_prefetch=3,
            grid=(count,),
            in_specs=[pl.BlockSpec((rows, total), here if back else there)],
            out_specs=pl.BlockSpec((rows, total), there if back else here),
        ),
        out_shape=jax.ShapeDtypeStruct((count * rows, total), out_type),
        compiler_params=pltpu.CompilerParams(vmem_limit_bytes=32 << 20),
        cost_estimate=pl.CostEstimate(
            flops=0, bytes_accessed=6 * count * rows * total, transcendentals=0
        ),
    )(row_at, col_at, side.reshape(1), x)


def build(n_dp, n_tensor):
    tensor_bits = []
    bit = 1
    while bit < n_tensor:
        tensor_bits.append(bit)
        bit *= 2
    dp_bits = []
    bit = 1
    while bit < n_dp:
        dp_bits.append(bit)
        bit *= 2
    far_first = list(reversed(dp_bits))
    pair_first = [1] + far_first[:-1]
    near_first = dp_bits
    pair_last = dp_bits[1:] + [1]
    offsets = [0]
    for bit in far_first:
        offsets = offsets + [o ^ bit for o in offsets]
    order = [0]
    for bit in reversed(tensor_bits):
        order = order + [o ^ bit for o in order]

    def swap(x, bit):
        return lax.ppermute(x, "tensor", [(i, i ^ bit) for i in range(n_tensor)])

    def swap_dp(x, bit):
        return lax.ppermute(x, "dp", [(i, i ^ bit) for i in range(n_dp)])

    def gather_rows(own):
        for bit in reversed(tensor_bits):
            own = jnp.concatenate([own, swap(own, bit)], axis=0)
        return own

    def scatter_near(make, rows):
        half = rows // 2
        got = swap(make(half, half, BF16), tensor_bits[0])
        return make(0, half, F32), got

    def exchange(near, work, beside=(None, None)):
        kept, got = near
        rows = kept.shape[0] // 4
        far_bit, near_bit = tensor_bits[1], tensor_bits[0]
        fars = []
        for i in range(2):
            part = slice((2 + i) * rows, (3 + i) * rows)
            fars.append(swap(low(kept[part] + wide(got[part])), far_bit))
        first, second = beside
        if first is not None:
            fars, first = lax.optimization_barrier((fars, first))
        done = [work(i, kept, got, fars[i]) for i in range(2)]
        mine = [rows_low for _, rows_low in done]
        others = [swap(rows_low, far_bit) for rows_low in mine]
        if second is not None:
            others, second = lax.optimization_barrier((others, second))
        half = jnp.concatenate(mine + others, axis=0)
        everyone = jnp.concatenate([half, swap(half, near_bit)], axis=0)
        if first is None and second is None:
            return [out for out, _ in done], everyone
        return [out for out, _ in done], everyone, first, second

    def sum_tensor(x):
        for bit in tensor_bits:
            x = x + swap(x, bit)
        return x

    def sum_dp(x):
        for bit in dp_bits:
            x = x + swap_dp(x, bit)
        return x

    def body(
        hidden_in,
        conditioning,
        valid_mask,
        teacher,
        gain_one,
        gain_two,
        gain_three,
        self_in_weight,
        self_out_weight,
        cross_query_weight,
        cross_memory_weight,
        cross_out_weight,
        gate_up_weight,
        down_weight,
    ):
        _, length, width = hidden_in.shape
        cond_tokens, cond_width = conditioning.shape[1:]
        me = lax.axis_index("tensor")
        dp_me = lax.axis_index("dp")
        shard = width // n_dp
        own_rows = length // n_tensor

        running = valid_mask[0, 0] > 0

        def stage(work, *args):
            def skipped(*args):
                return jax.tree.map(
                    lambda x: jnp.zeros(x.shape, x.dtype), jax.eval_shape(work, *args)
                )

            return lax.cond(running, work, skipped, *args)

        def move(kind, x):
            axis, bit = kind
            return swap(x, bit) if axis == "tensor" else swap_dp(x, bit)

        later = {}
        links = Links(move)
        tick = links.tick

        def gather_double(own, out, name, bits):
            near, far = own, None
            for bit in bits:
                near = near if far is None else jnp.concatenate([near, far], axis=0)
                (far,), near = yield [(("dp", bit), near)], near
            return out, name, (near, far)

        def gather_direct(own, out, name):
            rows = own.shape[0]
            (two, four, one), own = (
                yield [(("dp", 2), own), (("dp", 4), own), (("dp", 1), own)],
                own,
            )
            both = jnp.concatenate([two, four], axis=0)
            (six, both), (own, one, four, two) = (
                yield [(("dp", 6), own), (("dp", 1), both)],
                (own, one, four, two),
            )
            (seven,), shards = yield [(("dp", 1), six)], (own, four, two, six, one, both)
            return out, name, (*shards, seven)

        def came(bits):
            got_order = [0]
            for bit in bits:
                got_order = got_order + [o ^ bit for o in got_order]
            return tuple(offsets.index(o) for o in got_order)

        direct = (0, 4, 2, 6, 1, 3, 5, 7) if n_dp == 8 else tuple(offsets)
        came_direct = tuple(offsets.index(o) for o in direct)

        def reduce_halve(*halves, out, name, own=None):
            rows = halves[-1].shape[0]

            def total(terms, at):
                return sum(wide(t[at : at + rows]) for t in terms)

            (got,), terms = yield [(("dp", 1), halves[-1])], list(halves[:-1])
            terms = (terms if own is None else [later[own]]) + [got]
            for bit in near_first[1:]:
                rows = rows // 2
                (got,), terms = yield [(("dp", bit), low(total(terms, rows)))], terms
                terms = terms + [got]
            return out, name, total(terms, 0)

        def reduce_direct(near, far, out, name):
            rows = near.shape[0] // 4

            def block(halves, offset):
                at = offsets.index(offset)
                return halves[at // 4][at % 4 * rows : (at % 4 + 1) * rows]

            def add(*xs):
                return sum(wide(x) for x in xs)

            halves = [near, far]
            (got,), halves = yield [(("dp", 1), block(halves, 7))], halves
            six = low(add(block(halves, 6), got))
            both = jnp.concatenate([block(halves, 5), block(halves, 3)], axis=0)
            (six, both), halves = yield [(("dp", 6), six), (("dp", 1), both)], halves
            four = low(add(block(halves, 4), both[:rows]))
            two = low(add(block(halves, 2), both[rows:]))
            (four, two, one), (halves, six) = (
                yield [(("dp", 4), four), (("dp", 2), two), (("dp", 1), block(halves, 1))],
                (halves, six),
            )
            return out, name, add(block(halves, 0), six, four, two, one)

        if n_dp != 8:
            gather_direct = functools.partial(gather_double, bits=far_first)
            reduce_direct = reduce_halve

        def output_chain(own, out, name):
            for bit in reversed(tensor_bits):
                (got,), own = yield [(("tensor", bit), own)], own
                own = jnp.concatenate([own, got], axis=0)
            return out, name, own

        local = self_in_weight.shape[2]
        ff = down_weight.shape[0]
        first = jnp.concatenate([self_in_weight.reshape(shard, 3 * local), self_out_weight.T], axis=1)
        gate_up_own = gate_up_weight.reshape(shard, 2 * ff)
        full = {}

        def gathering(name, own, bits):
            return name, functools.partial(gather_double, out=full, name=name, bits=bits), [own]

        cross_rows = shard + cond_width // n_dp
        start_cross = gathering(
            "cross",
            jnp.concatenate(
                [
                    jnp.concatenate([cross_query_weight, cross_out_weight.T], axis=1),
                    cross_memory_weight.reshape(cond_width // n_dp, 2 * local),
                ],
                axis=0,
            ),
            far_first,
        )
        start_up_a = gathering("up_a", gate_up_own[:, :ff], far_first)
        start_up_b = gathering("up_b", gate_up_own[:, ff:], far_first)
        start_down = gathering("down", down_weight.T, pair_first)
        count = jnp.sum(valid_mask)
        count_row = jnp.zeros((shard,), F32).at[0].set(wide(count // 32)).at[1].set(wide(count % 32))
        gains_own = jnp.concatenate([gain_one, gain_two, gain_three, low(count_row)])[None]
        hidden_raw = tick(
            hidden_in[0],
            "",
            [
                gathering("gains", gains_own, far_first),
                ("first", functools.partial(gather_direct, out=full, name="first"), [first]),
            ],
        )

        pairs = local // PAIR
        rows = length
        mine = slice(0, own_rows)
        row_at = me ^ jnp.array(order, jnp.int32)
        col_at = (dp_me // 2) ^ jnp.array([o // 2 for o in offsets[: n_dp // 2]], jnp.int32)
        side = dp_me % 2

        def arrange_in(x, row_at):
            return arrange(x, row_at, col_at, side, own_rows, shard, BF16, False)

        def take(x, owner):
            return lax.dynamic_slice_in_dim(x, owner * own_rows, own_rows, 0)

        def center(x):
            return wide(x) - jnp.mean(wide(x), axis=-1, keepdims=True)

        def join(halves):
            return jnp.concatenate(halves, axis=0)

        hidden_raw, teacher_raw = tick((hidden_raw, teacher[0]), "gains")
        hidden = arrange_in(hidden_raw, row_at)
        hidden, me_late = tick((hidden, me), "first gains")
        centered = center(hidden)
        inverse_all = lax.rsqrt(jnp.mean(centered * centered, axis=-1, keepdims=True) + epsilon)

        def relative_late(x):
            return jnp.concatenate([take(x, me_late ^ o) for o in order], axis=0)

        position = relative_late(jnp.arange(length, dtype=F32)[:, None])
        lane = jnp.arange(PAIR) % HEAD_DIM
        frequency = jnp.exp((lane % (ROT // 2)).astype(F32) * (-2.0 * math.log(10000.0) / ROT))
        angles = position * frequency[None, :]
        cosine, sine = jnp.cos(angles), jnp.sin(angles)
        tables = (
            jnp.where(lane < ROT, cosine, 1.0),
            jnp.where(lane < ROT // 2, -sine, jnp.where(lane < ROT, sine, 0.0)),
        )
        bias = jnp.where(relative_late(valid_mask[0][:, None]) > 0, 0.0, masked_score)
        cosine, sine, hidden, inverse_all, teacher_raw = tick(
            (*tables, hidden, inverse_all, teacher_raw), "first gains", [start_cross]
        )
        tables = (cosine, sine)
        links.finish("gains")
        gains = jnp.concatenate(full["gains"], axis=0).reshape(n_dp, 4, shard)
        counts = wide(gains[:, 3])
        token_count = jnp.sum(32.0 * counts[:, 0] + counts[:, 1])
        gain_first, gain_second, gain_third = (wide(gains[:, i]).reshape(width) for i in range(3))
        normed_one = low(center(hidden) * inverse_all * gain_first)
        target_low = arrange_in(teacher_raw, me.reshape(1))
        normed_one, target_low, bias = tick(
            (normed_one, target_low, bias), "first cross", [start_up_a, start_down]
        )
        links.finish("first")
        cond_shard = cond_width // n_dp
        place = jnp.arange(cond_width)
        offset = sum(
            ((place // cond_shard >> i) % 2) * bit for i, bit in enumerate(far_first)
        )
        source = (dp_me ^ offset) * cond_shard + place % cond_shard
        cond_place = place[:, None] == source[None, :]
        memory_input = low(dot(conditioning[0], low(cond_place)))
        pad_tokens = -cond_tokens % 16
        cond_rows = cond_tokens + pad_tokens
        cond_bias = jnp.where(jnp.arange(cond_rows)[:, None] < cond_tokens, 0.0, masked_score)

        def branch(*terms):
            return scatter_near(
                lambda start, count, kind: branch_rows(terms, start, count, kind, width), rows
            )

        def of(pieces, places, rows_each=shard):
            return Weight(pieces, places, rows_each)

        far_places, pair_places = came(far_first), came(pair_first)

        def self_attention(normed_one, first, cos, sin, bias):
            first = of(first, came_direct)
            mixed = project_heads(normed_one, first, 3 * local, (cos, sin), 512)
            attended, self_totals = attend_forward(
                mixed, mixed, mixed, 0, pairs, 2 * pairs, bias, pairs, rows
            )
            return mixed, attended, self_totals, branch((attended, first, 3))

        mixed, attended, self_totals, near = stage(
            self_attention, normed_one, full["first"], *tables, bias
        )
        near = tick(near, "cross up_a down_", [start_up_b])

        def add_and_norm(streams, near, gain):
            def work(i, kept, got, far):
                return add_norm(streams[i], kept, got, far, gain, i)

            return exchange(near, work)

        after_self, normed_two = stage(add_and_norm, (hidden, hidden), near, gain_second)
        normed_two = tick(normed_two, "cross up_a up_b")

        links.finish("cross")
        cross_w = [x.reshape(-1, cross_rows, 2 * local) for x in full["cross"]]

        def unpack_memory(cross_w):
            return join([x[:, shard:].reshape(-1, 2 * local) for x in cross_w])

        def cross_attention(normed_two, cross_w):
            memory = dot(memory_input, unpack_memory(cross_w))
            cross_memory = jnp.pad(low(memory), ((0, pad_tokens), (0, 0)))
            weight = of(cross_w, far_places)
            cross_queries = project(normed_two, weight, local, 0)
            cross_attended, cross_totals = attend_forward(
                cross_queries, cross_memory, cross_memory, 0, 0, pairs, cond_bias, pairs, rows
            )
            near = branch((cross_attended, weight, 1))
            return cross_queries, cross_memory, cross_attended, cross_totals, near

        cross_queries, cross_memory, cross_attended, cross_totals, near = stage(
            cross_attention, normed_two, cross_w
        )
        near = tick(near, "up_b down")
        after_cross, normed_three = stage(add_and_norm, after_self, near, gain_third)
        normed_three = tick(normed_three, "up_a down")
        links.finish("up_a")
        gate_value = stage(
            lambda x, w: project(x, of(w, far_places), ff, 0, kind=F32), normed_three, full["up_a"]
        )
        gate_value = tick(gate_value, "up_b")
        links.finish("up_b")
        upward, hidden_units = stage(
            lambda x, w, gate: hidden_forward(x, of(w, far_places), gate),
            normed_three,
            full["up_b"],
            gate_value,
        )
        hidden_units = tick(hidden_units, "down")
        links.finish("down")
        near = stage(lambda x, w: branch((x, of(w, pair_places), 0)), hidden_units, full["down"])

        def final_rows(streams, near, target_low, valid_rows):
            factor = valid_rows * (2.0 * length / token_count)

            def work(i, kept, got, far):
                final, grad, grad_low, loss = final_part(
                    streams[i], kept, got, far, target_low, valid_rows, factor, i
                )
                return (final, jnp.sum(loss), grad), grad_low

            return exchange(near, work)

        valid_rows = wide(take(valid_mask[0][:, None], me))
        finals, grad_final_low = stage(final_rows, after_cross, near, target_low, valid_rows)
        final_low = join([final for final, _, _ in finals])
        losses = sum(loss for _, loss, _ in finals)
        grad_final = [grad for _, _, grad in finals]
        grads = {}

        def half_of(x, y, at):
            return weight_half([(x, y)], at)

        def halves_of(x, y):
            return half_of(x, y, 0), half_of(x, y, 1)

        def reducing(name, halves):
            return name, functools.partial(reduce_halve, out=grads, name=name), list(halves)

        others = {}

        def reducing_far(name, far):
            return (
                name,
                functools.partial(reduce_halve, out=grads, name=name, own=name),
                [far],
            )

        grad_final_low = tick(
            grad_final_low,
            "",
            [
                reducing_far("down", half_of(grad_final_low, hidden_units, 1)),
                (
                    "output",
                    functools.partial(output_chain, out=others, name="output"),
                    [final_low],
                ),
            ],
        )

        def hidden_back(grad_final_low, gate_value, upward, down_w, up_a, up_b):
            grad_gate, grad_up = hidden_backward(
                grad_final_low, of(down_w, pair_places), gate_value, upward
            )
            near = branch(
                (grad_gate, of(up_a, far_places), 0), (grad_up, of(up_b, far_places), 0)
            )
            return grad_gate, grad_up, near

        grad_gate, grad_up, near = stage(
            hidden_back,
            grad_final_low,
            gate_value,
            upward,
            full["down"],
            full["up_a"],
            full["up_b"],
        )

        def back_rows(near, uppers, streams, gain, beside):
            def work(i, kept, got, far):
                total, small, gain_sum = norm_back(uppers[i], kept, got, far, streams[i], gain, i)
                return (total, gain_sum), small

            outs, rows_low, first, second = exchange(near, work, beside)
            return [out for out, _ in outs], sum(x for _, x in outs), rows_low, first, second

        near = tick(
            near, "output", [reducing_far("up_a", half_of(normed_three, grad_gate, 1))]
        )

        def back_three(near, normed_three, grad_gate, grad_up):
            own = half_of(normed_three, grad_up, 0)
            return (
                *back_rows(
                    near,
                    grad_final,
                    after_cross,
                    gain_third,
                    (
                        (
                            half_of(grad_final_low, hidden_units, 0),
                            half_of(normed_three, grad_gate, 0),
                        ),
                        half_of(normed_three, grad_up, 1),
                    ),
                ),
                own,
            )

        grad_after_cross, gain_three_sum, grad_cross_low, owns, far, own = stage(
            back_three, near, normed_three, grad_gate, grad_up
        )
        later["down"], later["up_a"] = owns
        grad_up_b = (own, far)
        grad_cross_low = tick(grad_cross_low, "down output", [reducing("up_b", grad_up_b)])

        def cross_back(grad_cross_low, cross_w):
            weight = of(cross_w, far_places)
            grad_cross_attended = project(grad_cross_low, weight, local, 1)
            grad_cross_queries, grad_keys, grad_values = attend_backward(
                cross_queries,
                cross_memory,
                cross_memory,
                0,
                0,
                pairs,
                cond_bias,
                cross_totals,
                grad_cross_attended,
                None,
                pairs,
                rows,
            )
            near = branch((grad_cross_queries, weight, 0))
            return grad_cross_queries, grad_keys, grad_values, near

        grad_cross_queries, grad_keys, grad_values, near = stage(
            cross_back, grad_cross_low, cross_w
        )

        near = tick(near, "up_a")

        def arrange_out(x, out_type):
            return arrange(x, row_at, col_at, side, own_rows, shard, out_type, True)

        def back_two(
            near, grad_cross_queries, grad_keys, grad_values, grad_cross_low, rows_output
        ):
            grad_memory_low = jnp.concatenate(
                [grad_keys[:cond_tokens], grad_values[:cond_tokens]], axis=1
            )
            cond_part = lax.dot_general(
                dot_nt(grad_memory_low, unpack_memory(cross_w)),
                wide(cond_place),
                (((1,), (1,)), ((), ())),
                precision=lax.Precision.HIGHEST,
            )
            products = ((normed_two, grad_cross_queries), (grad_cross_low, cross_attended))
            if n_dp == 8:
                packed = tuple(
                    weight_half(products, at, (memory_input, grad_memory_low), n_dp // 2)
                    for at in range(2)
                )
            else:
                packed = []
                for at in range(2):
                    memory = half_of(memory_input, grad_memory_low, at)
                    memory = memory.reshape(n_dp // 2, cond_shard, 2, local)
                    memory = memory.transpose(0, 2, 1, 3).reshape(-1, local)
                    packed.append(
                        jnp.concatenate([half_of(x, y, at) for x, y in products] + [memory], axis=1)
                    )
                packed = tuple(packed)
            cond_part = cond_part.reshape(-1, width)
            block_output = arrange_out(rows_output, BF16)
            return back_rows(
                near,
                grad_after_cross,
                after_self,
                gain_second,
                ((packed[0], cond_part), (packed[1], block_output)),
            )

        grad_after_self, gain_two_sum, grad_self_low, (pack_near, cond_part), (pack_far, block_output) = (
            stage(
                back_two,
                near,
                grad_cross_queries,
                grad_keys,
                grad_values,
                grad_cross_low,
                others["output"],
            )
        )
        grad_cross = (pack_near, pack_far)
        grad_self_low = tick(grad_self_low, "up_a down up_b", [reducing("cross", grad_cross)])

        def self_back(grad_self_low, first, cond_part):
            grad_attended = project(grad_self_low, of(first, came_direct), local, 3)
            grad_parts = attend_backward(
                mixed,
                mixed,
                mixed,
                0,
                pairs,
                2 * pairs,
                bias,
                self_totals,
                grad_attended,
                tables,
                pairs,
                rows,
            )
            products = [(normed_one, part) for part in grad_parts] + [(grad_self_low, attended)]
            return (
                list(grad_parts),
                [weight_half(products, at) for at in range(2)],
                sum_tensor(cond_part),
            )

        grad_mixed, grad_first, cond_sum = stage(
            self_back, grad_self_low, full["first"], cond_part
        )
        grad_mixed = tick(
            grad_mixed,
            "up_a down up_b cross",
            [("first", functools.partial(reduce_direct, out=grads, name="first"), list(grad_first))],
        )

        def self_branch(grad_mixed, first):
            return branch(*((part, of(first, came_direct), i) for i, part in enumerate(grad_mixed)))

        near = stage(self_branch, grad_mixed, full["first"])
        near = tick(near, "first cross up_b")

        def small_sums(gain_one_sum):
            sums = jnp.stack([gain_one_sum, gain_two_sum, gain_three_sum]).reshape(3, n_dp, shard)
            sums = jnp.concatenate(
                [sums.transpose(1, 0, 2).reshape(n_dp, 3 * shard), jnp.full((n_dp, shard), losses)],
                axis=1,
            )
            for bit in near_first:
                half = sums.shape[0] // 2
                sums = sums[:half] + swap_dp(sums[half:], bit)
            return sum_tensor(sums)[0]

        links.finish("up_a", "up_b")

        def back_one(near, up_a, up_b):
            _, gain_one_sum, rows_hidden, grad_gate_up, _ = back_rows(
                near,
                grad_after_self,
                (hidden, hidden),
                gain_first,
                (jnp.stack([up_a, up_b], axis=1), gain_two_sum),
            )
            return rows_hidden, gain_one_sum, grad_gate_up

        rows_hidden, gain_one_sum, grad_gate_up = stage(
            back_one, near, grads["up_a"], grads["up_b"]
        )
        rows_hidden, gain_one_sum = tick(
            (rows_hidden, gain_one_sum), "first cross"
        )

        def last(rows_hidden, gain_one_sum):
            return small_sums(gain_one_sum), arrange_out(rows_hidden, F32)

        sums, grad_hidden = stage(last, rows_hidden, gain_one_sum)
        sums, grad_hidden = tick((sums, grad_hidden), "first")
        links.finish(*list(links.flying))

        grad_conditioning = cond_sum.reshape(cond_tokens, cond_width)
        mean_loss = sums[3 * shard] / (token_count * width)

        return (
            mean_loss,
            block_output[None],
            grad_hidden[None],
            grad_conditioning[None],
            sums[:shard],
            sums[shard : 2 * shard],
            sums[2 * shard : 3 * shard],
            grads["first"][:, : 3 * local].reshape(shard, 3, local),
            grads["first"][:, 3 * local :].T,
            grads["cross"][:, :local],
            jnp.stack(
                [grads["cross"][:cond_shard, 2 * local :], grads["cross"][cond_shard:, 2 * local :]],
                axis=1,
            ),
            grads["cross"][:, local : 2 * local].T,
            grad_gate_up,
            grads["down"].T,
        )

    return body


def solution(mesh):
    return jax.shard_map(
        build(mesh.shape["dp"], mesh.shape["tensor"]),
        mesh=mesh,
        in_specs=(
            P("dp", None, None),
            P("dp", None, None),
            P("dp", None),
            P("dp", None, None),
            P("dp"),
            P("dp"),
            P("dp"),
            P("dp", None, "tensor"),
            P("tensor", "dp"),
            P("dp", "tensor"),
            P("dp", None, "tensor"),
            P("tensor", "dp"),
            P("dp", None, "tensor"),
            P("tensor", "dp"),
        ),
        out_specs=(
            P(),
            P("dp", None, None),
            P("dp", None, None),
            P("dp", None, None),
            P("dp"),
            P("dp"),
            P("dp"),
            P("dp", None, "tensor"),
            P("tensor", "dp"),
            P("dp", "tensor"),
            P("dp", None, "tensor"),
            P("tensor", "dp"),
            P("dp", None, "tensor"),
            P("tensor", "dp"),
        ),
        check_vma=False,
    )
```

```python
import functools
import math

import jax
import jax.numpy as jnp
from jax import lax
from jax.experimental import pallas as pl
from jax.experimental.pallas import tpu as pltpu
from jax.sharding import PartitionSpec as P

HEAD_DIM = 64
ROT = 32
CHUNKS = 1

epsilon = 1e-05
masked_score = -1e30
F32 = jnp.float32
BF16 = jnp.bfloat16


def low(x):
    return x.astype(BF16)


def wide(x):
    return x.astype(F32)


def dot(a, b):
    return lax.dot_general(a, b, (((1,), (0,)), ((), ())), preferred_element_type=F32)


def dot_nt(a, b):
    return lax.dot_general(a, b, (((1,), (1,)), ((), ())), preferred_element_type=F32)


def dot_tn(a, b):
    return lax.dot_general(a, b, (((0,), (0,)), ((), ())), preferred_element_type=F32)


PAIR=128
SCALE=1.0/math.sqrt(HEAD_DIM)
SCALE2=SCALE*math.log2(math.e)

def mm(a,b): return lax.dot_general(a,b,(((1,),(0,)),((),())),preferred_element_type=F32)
def mm_nt(a,b): return lax.dot_general(a,b,(((1,),(1,)),((),())),preferred_element_type=F32)

def mm_tn(a,b): return lax.dot_general(a,b,(((0,),(0,)),((),())),preferred_element_type=F32)


def head_lanes(shape, axis, head):
    at = lax.broadcasted_iota(jnp.int32, shape, axis)
    return (at >= head*HEAD_DIM) & (at < (head+1)*HEAD_DIM)

def keep_head(x, axis, head):
    return jnp.where(head_lanes(x.shape, axis, head), x, jnp.zeros_like(x))

def with_lane(x, head, lane_value):
    at = lax.broadcasted_iota(jnp.int32, x.shape, 1)
    other = (1-head)*HEAD_DIM
    return jnp.where(at == other, lane_value, keep_head(x, 1, head))

def fwd_kernel(q_ref, k_ref, v_ref, bias_ref, o_ref, lse_ref, k_sc, vt_sc):
    @pl.when(pl.program_id(1) == 0)
    def _():
        k = k_ref[...].astype(F32)
        vt = v_ref[...].astype(F32).T
        for h in range(2):
            k_sc[h] = with_lane(k, h, bias_ref[...]).astype(BF16)
            vt_sc[h] = keep_head(vt, 0, h).astype(BF16)
    q = q_ref[...].astype(F32)
    out = None
    for h in range(2):
        qh = with_lane(q, h, 1.0).astype(BF16)
        s = mm_nt(k_sc[h], qh)
        m = jnp.max(s, axis=0, keepdims=True)
        e = jnp.exp2((s - m) * SCALE2)
        l = jnp.sum(e, axis=0, keepdims=True)
        o = mm(vt_sc[h], e.astype(BF16)) * (1.0 / l)
        out = o if out is None else out + o
        lse_ref[0, h:h+1, :] = m * SCALE2 + jnp.log2(l)
    o_ref[...] = out.T.astype(BF16)

def bwd_kernel(q_ref, k_ref, v_ref, bias_ref, lse_ref, g_ref, *rest, rotary):
    if rotary:
        cosq_ref, sinq_ref, cosk_ref, sink_ref, dq_ref, dk_ref, dv_ref, k_sc, kt_sc, v_sc, dk_sc, dv_sc = rest
    else:
        dq_ref, dk_ref, dv_ref, k_sc, kt_sc, v_sc, dk_sc, dv_sc = rest
    i = pl.program_id(1)
    @pl.when(i == 0)
    def _():
        k = k_ref[...].astype(F32)
        kt = k.T
        for h in range(2):
            k_sc[h] = with_lane(k, h, bias_ref[...]).astype(BF16)
            kt_sc[h] = keep_head(kt, 0, h).astype(BF16)
            v_sc[h] = keep_head(v_ref[...].astype(F32), 1, h).astype(BF16)
        dk_sc[...] = jnp.zeros_like(dk_sc)
        dv_sc[...] = jnp.zeros_like(dv_sc)
    q = q_ref[...].astype(F32)
    g32 = g_ref[...].astype(F32)
    g = g_ref[...]
    dqt = None
    dk = dk_sc[...]
    dv = dv_sc[...]
    for h in range(2):
        qa = with_lane(q, h, 1.0).astype(BF16)
        qh = keep_head(q, 1, h).astype(BF16)
        gh = keep_head(g32, 1, h).astype(BF16)
        s = mm_nt(k_sc[h], qa)
        p = jnp.exp2(s * SCALE2 - lse_ref[0, h:h+1, :])
        dp = mm_nt(v_sc[h], g)
        t = p * dp
        delta = jnp.sum(t, axis=0, keepdims=True)
        ds = (t - p * delta).astype(BF16)
        dv = dv + mm(p.astype(BF16), gh)
        dk = dk + mm(ds, qh)
        d = mm(kt_sc[h], ds)
        dqt = d if dqt is None else dqt + d
    dk_sc[...] = dk
    dv_sc[...] = dv
    dq = dqt.T * SCALE
    if rotary:
        dq = turn_back(dq, cosq_ref[...], sinq_ref[...])
    dq_ref[...] = dq.astype(BF16)
    @pl.when(i == pl.num_programs(1) - 1)
    def _():
        dk = dk_sc[...] * SCALE
        if rotary:
            dk = turn_back(dk, cosk_ref[...], sink_ref[...])
        dk_ref[...] = dk.astype(BF16)
        dv_ref[...] = dv_sc[...].astype(BF16)

def swap_halves(x):
    n = x.shape[1]
    at = lax.broadcasted_iota(jnp.int32, x.shape, 1) % HEAD_DIM
    return jnp.where(at < 16, pltpu.roll(x, n - 16, 1), pltpu.roll(x, 16, 1))

def turn(x, cos, sin):
    return x * cos + swap_halves(x) * sin

def turn_back(x, cos, sin):
    return x * cos - swap_halves(x) * sin

def attend_forward(q, k, v, qcol, kcol, vcol, bias, pairs, block):
    rows = q.shape[0]; keys = k.shape[0]
    return pl.pallas_call(
        fwd_kernel,
        grid=(pairs, rows//block),
        in_specs=[
            pl.BlockSpec((block,PAIR), lambda p,i:(i,qcol+p)),
            pl.BlockSpec((keys,PAIR), lambda p,i:(0,kcol+p)),
            pl.BlockSpec((keys,PAIR), lambda p,i:(0,vcol+p)),
            pl.BlockSpec((keys,1), lambda p,i:(0,0)),
        ],
        out_specs=[
            pl.BlockSpec((block,PAIR), lambda p,i:(i,p)),
            pl.BlockSpec((1,8,block), lambda p,i:(p,0,i)),
        ],
        out_shape=[jax.ShapeDtypeStruct((rows,pairs*PAIR),BF16), jax.ShapeDtypeStruct((pairs,8,rows),F32)],
        scratch_shapes=[pltpu.VMEM((2,keys,PAIR),BF16), pltpu.VMEM((2,PAIR,keys),BF16)],
        compiler_params=pltpu.CompilerParams(vmem_limit_bytes=48<<20),
        cost_estimate=pl.CostEstimate(flops=4*rows*keys*PAIR*pairs*2, bytes_accessed=2*(2*rows+2*keys)*PAIR*pairs, transcendentals=rows*keys*2*pairs),
    )(q,k,v,bias)

def attend_backward(q, k, v, qcol, kcol, vcol, bias, lse, g, tables, pairs, block):
    rows = q.shape[0]; keys = k.shape[0]
    rotary = tables is not None
    in_specs=[
        pl.BlockSpec((block,PAIR), lambda p,i:(i,qcol+p)),
        pl.BlockSpec((keys,PAIR), lambda p,i:(0,kcol+p)),
        pl.BlockSpec((keys,PAIR), lambda p,i:(0,vcol+p)),
        pl.BlockSpec((keys,1), lambda p,i:(0,0)),
        pl.BlockSpec((1,8,block), lambda p,i:(p,0,i)),
        pl.BlockSpec((block,PAIR), lambda p,i:(i,p)),
    ]
    args=[q,k,v,bias,lse,g]
    if rotary:
        in_specs += [pl.BlockSpec((block,PAIR), lambda p,i:(i,0))]*2 + [pl.BlockSpec((keys,PAIR), lambda p,i:(0,0))]*2
        args += [tables[0],tables[1],tables[0],tables[1]]
    return pl.pallas_call(
        functools.partial(bwd_kernel, rotary=rotary),
        grid=(pairs, rows//block),
        in_specs=in_specs,
        out_specs=[
            pl.BlockSpec((block,PAIR), lambda p,i:(i,p)),
            pl.BlockSpec((keys,PAIR), lambda p,i:(0,p)),
            pl.BlockSpec((keys,PAIR), lambda p,i:(0,p)),
        ],
        out_shape=[jax.ShapeDtypeStruct((rows,pairs*PAIR),BF16)]+[jax.ShapeDtypeStruct((keys,pairs*PAIR),BF16)]*2,
        scratch_shapes=[pltpu.VMEM((2,keys,PAIR),BF16), pltpu.VMEM((2,PAIR,keys),BF16), pltpu.VMEM((2,keys,PAIR),BF16), pltpu.VMEM((keys,PAIR),F32), pltpu.VMEM((keys,PAIR),F32)],
        compiler_params=pltpu.CompilerParams(vmem_limit_bytes=48<<20),
        cost_estimate=pl.CostEstimate(flops=10*rows*keys*PAIR*pairs*2, bytes_accessed=2*(4*rows+4*keys)*PAIR*pairs, transcendentals=rows*keys*2*pairs),
    )(*args)


def rows_spec(block, cols, start=0):
    return pl.BlockSpec((block, cols), lambda i: (start + i, 0))


def call_rows(kernel, rows, block, in_specs, outs, args, flops, scratch=()):
    return pl.pallas_call(
        kernel,
        grid=(rows // block,),
        in_specs=in_specs,
        out_specs=[rows_spec(block, cols) for cols, _ in outs],
        out_shape=[jax.ShapeDtypeStruct((rows, cols), kind) for cols, kind in outs],
        scratch_shapes=list(scratch),
        compiler_params=pltpu.CompilerParams(vmem_limit_bytes=56 << 20),
        cost_estimate=pl.CostEstimate(
            flops=flops, bytes_accessed=sum(2 * x.size for x in args), transcendentals=0
        ),
    )(*args)


class Weight:
    def __init__(self, pieces, places, rows):
        self.pieces, self.places, self.rows = list(pieces), tuple(places), rows

    def specs(self, cols, at):
        return [
            pl.BlockSpec((x.shape[0], self.rows, cols), lambda i: (0, 0, at))
            if x.ndim == 3
            else pl.BlockSpec((x.shape[0], cols), lambda i: (0, at))
            for x in self.pieces
        ]

    def scratch(self, cols):
        return pltpu.VMEM((len(self.places) * self.rows, cols), BF16)

    def assemble(self, refs, scratch_ref):
        rows, places = self.rows, list(self.places)

        @pl.when(pl.program_id(0) == 0)
        def _():
            left = list(places)
            for ref in refs:
                packed = len(ref.shape) == 3
                count = ref.shape[0] if packed else ref.shape[0] // rows
                for i in range(count):
                    place = left.pop(0)
                    source = ref[i] if packed else ref[i * rows : (i + 1) * rows]
                    scratch_ref[place * rows : (place + 1) * rows] = source

        return scratch_ref


def project_kernel(*refs, weight):
    x_ref, o_ref, scratch_ref = refs[0], refs[-2], refs[-1]
    w_ref = weight.assemble(refs[1:-2], scratch_ref)
    o_ref[...] = mm(x_ref[...], w_ref[...]).astype(o_ref.dtype)


def project(x, weight, cols, at, kind=BF16, block=512):
    rows, width = x.shape
    return call_rows(
        functools.partial(project_kernel, weight=weight),
        rows,
        block,
        [rows_spec(block, width)] + weight.specs(cols, at),
        [(cols, kind)],
        (x, *weight.pieces),
        2 * rows * width * cols,
        [weight.scratch(cols)],
    )[0]


def branch_kernel(*refs, weights):
    count = sum(1 + len(w.pieces) for w in weights)
    out_ref, scratches = refs[count], refs[count + 1 :]
    total, at = None, 0
    for weight, scratch_ref in zip(weights, scratches):
        x_ref, pieces = refs[at], refs[at + 1 : at + 1 + len(weight.pieces)]
        at += 1 + len(pieces)
        w_ref = weight.assemble(pieces, scratch_ref)
        product = mm_nt(x_ref[...], w_ref[...])
        total = product if total is None else total + product
    out_ref[...] = total.astype(out_ref.dtype)


def branch_rows(terms, start, rows, kind, width, block=512):
    specs, args, flops = [], [], 0
    for x, weight, at in terms:
        cols = x.shape[1]
        specs += [rows_spec(block, cols, start // block)] + weight.specs(cols, at)
        args += [x, *weight.pieces]
        flops += 2 * rows * cols * width
    return call_rows(
        functools.partial(branch_kernel, weights=[w for _, w, _ in terms]),
        rows,
        block,
        specs,
        [(width, kind)],
        args,
        flops,
        [w.scratch(x.shape[1]) for x, w, _ in terms],
    )[0]


def weight_kernel(*refs, count, blocks):
    out_ref = refs[-1]
    at = 0
    for i in range(count):
        x_ref, y = refs[2 * i], refs[2 * i + 1][...]
        cols = y.shape[1]
        for j in range(0, x_ref.shape[1], 256):
            product = mm_tn(x_ref[:, j : j + 256], y)
            out_ref[j : j + 256, at : at + cols] = product.astype(BF16)
        at += cols
    if blocks:
        product = mm_tn(refs[2 * count][...], refs[2 * count + 1][...]).astype(BF16)
        rows, cols = product.shape[0] // blocks, product.shape[1] // 2
        for b in range(blocks):
            for i in range(2):
                out_ref[(2 * b + i) * rows : (2 * b + i + 1) * rows, at:] = product[
                    b * rows : (b + 1) * rows, i * cols : (i + 1) * cols
                ]


def weight_half(pairs, at, small=None, blocks=0):
    specs, args, cols = [], [], 0
    for x, y in pairs:
        specs.append(pl.BlockSpec((x.shape[0], x.shape[1] // 2), lambda i: (0, at)))
        specs.append(pl.BlockSpec(y.shape, lambda i: (0, 0)))
        args += [x, y]
        cols += y.shape[1]
    if small is not None:
        x, y = small
        specs.append(pl.BlockSpec((x.shape[0], x.shape[1] // 2), lambda i: (0, at)))
        specs.append(pl.BlockSpec(y.shape, lambda i: (0, 0)))
        args += [x, y]
        cols += y.shape[1] // 2
    rows = pairs[0][0].shape[1] // 2
    return call_rows(
        functools.partial(weight_kernel, count=len(pairs), blocks=blocks),
        rows,
        rows,
        specs,
        [(cols, BF16)],
        args,
        2 * rows * pairs[0][0].shape[0] * cols,
    )[0]


def hidden_kernel(*refs, weight):
    x_ref, gate_ref = refs[0], refs[1]
    up_ref, hidden_ref, scratch_ref = refs[-3:]
    w_ref = weight.assemble(refs[2:-3], scratch_ref)
    up = mm(x_ref[...], w_ref[...])
    gate = gate_ref[...]
    up_ref[...] = up
    hidden_ref[...] = (gate * jax.nn.sigmoid(gate) * up).astype(BF16)


def hidden_forward(x, weight, gate, block=512):
    rows, width = x.shape
    ff = gate.shape[1]
    return call_rows(
        functools.partial(hidden_kernel, weight=weight),
        rows,
        block,
        [rows_spec(block, width), rows_spec(block, ff)] + weight.specs(ff, 0),
        [(ff, F32), (ff, BF16)],
        (x, gate, *weight.pieces),
        2 * rows * width * ff,
        [weight.scratch(ff)],
    )


def hidden_back_kernel(*refs, weight):
    g_ref, gate_ref, up_ref = refs[:3]
    grad_gate_ref, grad_up_ref, scratch_ref = refs[-3:]
    w_ref = weight.assemble(refs[3:-3], scratch_ref)
    grad = mm(g_ref[...], w_ref[...])
    gate, up = gate_ref[...], up_ref[...]
    s = jax.nn.sigmoid(gate)
    grad_gate_ref[...] = (grad * up * s * (1.0 + gate * (1.0 - s))).astype(BF16)
    grad_up_ref[...] = (grad * gate * s).astype(BF16)


def hidden_backward(g, weight, gate, up, block=512):
    rows, width = g.shape
    ff = gate.shape[1]
    return call_rows(
        functools.partial(hidden_back_kernel, weight=weight),
        rows,
        block,
        [rows_spec(block, width), rows_spec(block, ff), rows_spec(block, ff)] + weight.specs(ff, 0),
        [(ff, BF16), (ff, BF16)],
        (g, gate, up, *weight.pieces),
        2 * rows * width * ff,
        [weight.scratch(ff)],
    )


def centered_rows(x):
    centered = x - jnp.mean(x, axis=-1, keepdims=True)
    inverse = lax.rsqrt(jnp.mean(centered * centered, axis=-1, keepdims=True) + epsilon)
    return centered * inverse, inverse


def add_norm_kernel(stream_ref, kept_ref, got_ref, far_ref, gain_ref, sum_ref, normed_ref):
    total = stream_ref[...].astype(F32) + (
        kept_ref[...] + got_ref[...].astype(F32) + far_ref[...].astype(F32)
    )
    sum_ref[...] = total
    normed_ref[...] = (centered_rows(total)[0] * gain_ref[...]).astype(BF16)


def add_norm(stream, kept, got, far, gain, at):
    rows, width = far.shape
    own, part = rows_spec(rows, width), rows_spec(rows, width, at)
    return call_rows(
        add_norm_kernel,
        rows,
        rows,
        [part if stream.shape[0] > rows else own, part, part, own]
        + [pl.BlockSpec((1, width), lambda i: (0, 0))],
        [(width, F32), (width, BF16)],
        (stream, kept, got, far, gain.reshape(1, width)),
        0,
    )


def final_kernel(
    stream_ref, kept_ref, got_ref, far_ref, target_ref, valid_ref, factor_ref,
    final_ref, grad_ref, low_ref, loss_ref,
):
    final = stream_ref[...] + (
        kept_ref[...] + got_ref[...].astype(F32) + far_ref[...].astype(F32)
    )
    difference = final - target_ref[...].astype(F32)
    grad = factor_ref[...] * difference
    final_ref[...] = final.astype(BF16)
    grad_ref[...] = grad
    low_ref[...] = grad.astype(BF16)
    loss_ref[...] = jnp.sum(valid_ref[...] * (difference * difference), axis=0, keepdims=True)


def final_part(stream, kept, got, far, target, valid, factor, at):
    rows, width = far.shape
    own, part = rows_spec(rows, width), rows_spec(rows, width, at)
    column = pl.BlockSpec((rows, 1), lambda i: (at, 0))
    return pl.pallas_call(
        final_kernel,
        grid=(1,),
        in_specs=[own, part, part, own, part, column, column],
        out_specs=[own, own, own, pl.BlockSpec((1, width), lambda i: (0, 0))],
        out_shape=[
            jax.ShapeDtypeStruct((rows, width), BF16),
            jax.ShapeDtypeStruct((rows, width), F32),
            jax.ShapeDtypeStruct((rows, width), BF16),
            jax.ShapeDtypeStruct((1, width), F32),
        ],
        compiler_params=pltpu.CompilerParams(vmem_limit_bytes=32 << 20),
        cost_estimate=pl.CostEstimate(flops=0, bytes_accessed=20 * rows * width, transcendentals=0),
    )(stream, kept, got, far, target, valid, factor)


def norm_back_kernel(
    upper_ref, kept_ref, got_ref, far_ref, stream_ref, gain_ref, total_ref, low_ref, gain_grad_ref
):
    upstream = kept_ref[...] + got_ref[...].astype(F32) + far_ref[...].astype(F32)
    scaled, inverse = centered_rows(stream_ref[...].astype(F32))
    weighted = upstream * gain_ref[...]
    grad = inverse * (
        weighted
        - jnp.mean(weighted, axis=-1, keepdims=True)
        - scaled * jnp.mean(weighted * scaled, axis=-1, keepdims=True)
    )
    total = upper_ref[...] + grad
    total_ref[...] = total
    low_ref[...] = total.astype(BF16)

    @pl.when(pl.program_id(0) == 0)
    def _():
        gain_grad_ref[...] = jnp.zeros_like(gain_grad_ref)

    gain_grad_ref[...] += jnp.sum(upstream * scaled, axis=0, keepdims=True)


def norm_back(upper, kept, got, far, stream, gain, at):
    rows, width = far.shape
    own, part = rows_spec(rows, width), rows_spec(rows, width, at)
    row = pl.BlockSpec((1, width), lambda i: (0, 0))
    total, small, gain_grad = pl.pallas_call(
        norm_back_kernel,
        grid=(1,),
        in_specs=[own, part, part, own, part if stream.shape[0] > rows else own, row],
        out_specs=[own, own, row],
        out_shape=[
            jax.ShapeDtypeStruct((rows, width), F32),
            jax.ShapeDtypeStruct((rows, width), BF16),
            jax.ShapeDtypeStruct((1, width), F32),
        ],
        compiler_params=pltpu.CompilerParams(vmem_limit_bytes=32 << 20),
        cost_estimate=pl.CostEstimate(flops=0, bytes_accessed=20 * rows * width, transcendentals=0),
    )(upper, kept, got, far, stream, gain.reshape(1, width))
    return total, small, gain_grad[0]


def qkv_kernel(*refs, weight):
    x_ref, cos_ref, sin_ref = refs[:3]
    o_ref, scratch_ref = refs[-2:]
    w_ref = weight.assemble(refs[3:-2], scratch_ref)
    y = mm(x_ref[...], w_ref[...])
    cos, sin = cos_ref[...], sin_ref[...]
    turned = 2 * (y.shape[1] // 3)
    for at in range(0, turned, PAIR):
        o_ref[:, at : at + PAIR] = turn(y[:, at : at + PAIR], cos, sin).astype(BF16)
    o_ref[:, turned:] = y[:, turned:].astype(BF16)


def project_heads(x, weight, cols, tables, block):
    rows, width = x.shape
    return call_rows(
        functools.partial(qkv_kernel, weight=weight),
        rows,
        block,
        [rows_spec(block, width), rows_spec(block, PAIR), rows_spec(block, PAIR)]
        + weight.specs(cols, 0),
        [(cols, BF16)],
        (x, *tables, *weight.pieces),
        2 * rows * width * cols,
        [weight.scratch(cols)],
    )[0]


class Links:
    def __init__(self, move):
        self.move = move
        self.flying = {}

    def tick(self, values, advance="", start=()):
        values = list(values) if isinstance(values, (tuple, list)) else [values]
        count = len(values)
        asked = advance.split()
        held_back = {name.strip("_") for name in asked if name.endswith("_")}
        names = [name.strip("_") for name in asked if name.strip("_") in self.flying]
        chains = [self.flying.pop(name) for name in names]
        operands = [values, [], []]
        for _, got, state in chains:
            operands[1].append((got, state))
        for _, _, arrays in start:
            operands[2].append(list(arrays))
        values, held, begun = lax.optimization_barrier(operands)
        moving, done = [], []
        for name, (chain, _, _), (got, state) in zip(names, chains, held):
            if name in held_back:
                self.flying[name] = (chain, got, state)
                continue
            try:
                moving.append((name, chain, *chain.send((got, state))))
            except StopIteration as end:
                done.append(end.value)
        for (name, make, _), arrays in zip(start, begun):
            chain = make(*arrays)
            moving.append((name, chain, *next(chain)))
        values, sent, results = lax.optimization_barrier(
            [
                values,
                [[x for _, x in moves] for _, _, moves, _ in moving],
                [result for _, _, result in done],
            ]
        )
        for (out, name, _), result in zip(done, results):
            out[name] = result
        for (name, chain, moves, state), xs in zip(moving, sent):
            got = [self.move(kind, x) for (kind, _), x in zip(moves, xs)]
            self.flying[name] = (chain, got, state)
        return values[0] if count == 1 else tuple(values)

    def finish(self, *names):
        for name in names:
            while name in self.flying:
                self.tick((), name)


def arrange_in_kernel(row_ref, col_ref, side_ref, x_ref, out_ref):
    count = out_ref.shape[1] // PAIR // 3
    width = 3 * HEAD_DIM
    side = side_ref[0]
    at = lax.broadcasted_iota(jnp.int32, (out_ref.shape[0], 2 * width), 1)
    for j in range(count):
        other = j >= count // 2
        pieces = []
        for i in range(2):
            source = col_ref[(2 * j + i) % count]
            piece = x_ref[:, pl.ds(pl.multiple_of(source * 2 * width, 2 * width), 2 * width)]
            pieces.append(piece.astype(F32))
        first, second = pieces
        own_first = jnp.where(at < width, first, pltpu.roll(second, width, 1))
        own_second = jnp.where(at < width, pltpu.roll(first, width, 1), second)
        want_first = (side == 1) if other else (side == 0)
        out = jnp.where(want_first, own_first, own_second)
        out_ref[:, j * 2 * width : (j + 1) * 2 * width] = out.astype(out_ref.dtype)


def arrange_out_kernel(row_ref, col_ref, side_ref, x_ref, out_ref):
    count = out_ref.shape[1] // PAIR // 3
    width = 3 * HEAD_DIM
    side = side_ref[0]
    half = count // 2
    at = lax.broadcasted_iota(jnp.int32, (out_ref.shape[0], 2 * width), 1)
    for j in range(half):
        own = x_ref[:, j * 2 * width : (j + 1) * 2 * width].astype(F32)
        other = x_ref[:, (half + j) * 2 * width : (half + j + 1) * 2 * width].astype(F32)
        first = jnp.where(side == 0, own, other)
        second = jnp.where(side == 0, other, own)
        made = (
            jnp.where(at < width, first, pltpu.roll(second, width, 1)),
            jnp.where(at < width, pltpu.roll(first, width, 1), second),
        )
        for i in range(2):
            place = col_ref[2 * j + i]
            out_ref[:, pl.ds(pl.multiple_of(place * 2 * width, 2 * width), 2 * width)] = made[
                i
            ].astype(out_ref.dtype)


def arrange(x, row_at, col_at, side, rows, shard, out_type, back):
    count, total = row_at.shape[0], x.shape[1]
    pairs = col_at.shape[0]
    if shard != 3 * HEAD_DIM or pairs % 2:
        shard_at = jnp.concatenate([col_at * 2 + side, col_at * 2 + 1 - side])
        blocks = x.reshape(-1, rows, 2 * pairs, shard)
        if back:
            blocks = jnp.zeros_like(blocks).at[row_at].set(blocks)
            blocks = jnp.zeros_like(blocks).at[:, :, shard_at].set(blocks)
        else:
            blocks = blocks[row_at][:, :, shard_at]
        return blocks.reshape(-1, total).astype(out_type)

    def here(i, row_at, col_at, side):
        return i, 0

    def there(i, row_at, col_at, side):
        return row_at[i], 0

    return pl.pallas_call(
        arrange_out_kernel if back else arrange_in_kernel,
        grid_spec=pltpu.PrefetchScalarGridSpec(
            num_scalar_prefetch=3,
            grid=(count,),
            in_specs=[pl.BlockSpec((rows, total), here if back else there)],
            out_specs=pl.BlockSpec((rows, total), there if back else here),
        ),
        out_shape=jax.ShapeDtypeStruct((count * rows, total), out_type),
        compiler_params=pltpu.CompilerParams(vmem_limit_bytes=32 << 20),
        cost_estimate=pl.CostEstimate(
            flops=0, bytes_accessed=6 * count * rows * total, transcendentals=0
        ),
    )(row_at, col_at, side.reshape(1), x)


def build(n_dp, n_tensor):
    tensor_bits = []
    bit = 1
    while bit < n_tensor:
        tensor_bits.append(bit)
        bit *= 2
    dp_bits = []
    bit = 1
    while bit < n_dp:
        dp_bits.append(bit)
        bit *= 2
    far_first = list(reversed(dp_bits))
    pair_first = [1] + far_first[:-1]
    near_first = dp_bits
    pair_last = dp_bits[1:] + [1]
    offsets = [0]
    for bit in far_first:
        offsets = offsets + [o ^ bit for o in offsets]
    order = [0]
    for bit in reversed(tensor_bits):
        order = order + [o ^ bit for o in order]

    def swap(x, bit):
        return lax.ppermute(x, "tensor", [(i, i ^ bit) for i in range(n_tensor)])

    def swap_dp(x, bit):
        return lax.ppermute(x, "dp", [(i, i ^ bit) for i in range(n_dp)])

    def gather_rows(own):
        for bit in reversed(tensor_bits):
            own = jnp.concatenate([own, swap(own, bit)], axis=0)
        return own

    def scatter_near(make, rows):
        half = rows // 2
        got = swap(make(half, half, BF16), tensor_bits[0])
        return make(0, half, F32), got

    def exchange(near, work, beside=(None, None)):
        kept, got = near
        rows = kept.shape[0] // 4
        far_bit, near_bit = tensor_bits[1], tensor_bits[0]
        fars = []
        for i in range(2):
            part = slice((2 + i) * rows, (3 + i) * rows)
            fars.append(swap(low(kept[part] + wide(got[part])), far_bit))
        first, second = beside
        if first is not None:
            fars, first = lax.optimization_barrier((fars, first))
        done = [work(i, kept, got, fars[i]) for i in range(2)]
        mine = [rows_low for _, rows_low in done]
        others = [swap(rows_low, far_bit) for rows_low in mine]
        if second is not None:
            others, second = lax.optimization_barrier((others, second))
        half = jnp.concatenate(mine + others, axis=0)
        everyone = jnp.concatenate([half, swap(half, near_bit)], axis=0)
        if first is None and second is None:
            return [out for out, _ in done], everyone
        return [out for out, _ in done], everyone, first, second

    def sum_tensor(x):
        for bit in tensor_bits:
            x = x + swap(x, bit)
        return x

    def sum_dp(x):
        for bit in dp_bits:
            x = x + swap_dp(x, bit)
        return x

    def body(
        hidden_in,
        conditioning,
        valid_mask,
        teacher,
        gain_one,
        gain_two,
        gain_three,
        self_in_weight,
        self_out_weight,
        cross_query_weight,
        cross_memory_weight,
        cross_out_weight,
        gate_up_weight,
        down_weight,
    ):
        _, length, width = hidden_in.shape
        cond_tokens, cond_width = conditioning.shape[1:]
        me = lax.axis_index("tensor")
        dp_me = lax.axis_index("dp")
        shard = width // n_dp
        own_rows = length // n_tensor

        running = valid_mask[0, 0] > 0

        def stage(work, *args):
            def skipped(*args):
                return jax.tree.map(
                    lambda x: jnp.zeros(x.shape, x.dtype), jax.eval_shape(work, *args)
                )

            return lax.cond(running, work, skipped, *args)

        def move(kind, x):
            axis, bit = kind
            return swap(x, bit) if axis == "tensor" else swap_dp(x, bit)

        later = {}
        links = Links(move)
        tick = links.tick

        def gather_double(own, out, name, bits):
            near, far = own, None
            for bit in bits:
                near = near if far is None else jnp.concatenate([near, far], axis=0)
                (far,), near = yield [(("dp", bit), near)], near
            return out, name, (near, far)

        def gather_direct(own, out, name):
            rows = own.shape[0]
            (two, four, one), own = (
                yield [(("dp", 2), own), (("dp", 4), own), (("dp", 1), own)],
                own,
            )
            both = jnp.concatenate([two, four], axis=0)
            (six, both), (own, one, four, two) = (
                yield [(("dp", 6), own), (("dp", 1), both)],
                (own, one, four, two),
            )
            (seven,), shards = yield [(("dp", 1), six)], (own, four, two, six, one, both)
            return out, name, (*shards, seven)

        def came(bits):
            got_order = [0]
            for bit in bits:
                got_order = got_order + [o ^ bit for o in got_order]
            return tuple(offsets.index(o) for o in got_order)

        direct = (0, 4, 2, 6, 1, 3, 5, 7) if n_dp == 8 else tuple(offsets)
        came_direct = tuple(offsets.index(o) for o in direct)

        def reduce_halve(*halves, out, name, own=None):
            rows = halves[-1].shape[0]

            def total(terms, at):
                return sum(wide(t[at : at + rows]) for t in terms)

            (got,), terms = yield [(("dp", 1), halves[-1])], list(halves[:-1])
            terms = (terms if own is None else [later[own]]) + [got]
            for bit in near_first[1:]:
                rows = rows // 2
                (got,), terms = yield [(("dp", bit), low(total(terms, rows)))], terms
                terms = terms + [got]
            return out, name, total(terms, 0)

        def reduce_direct(far, out, name):
            rows = far.shape[0] // 4

            def block(halves, offset):
                at = offsets.index(offset)
                return halves[at // 4][at % 4 * rows : (at % 4 + 1) * rows]

            def add(*xs):
                return sum(wide(x) for x in xs)

            (got,), far = yield [(("dp", 1), block((None, far), 7))], far
            halves = [later[name], far]
            six = low(add(block(halves, 6), got))
            both = jnp.concatenate([block(halves, 5), block(halves, 3)], axis=0)
            (six, both), halves = yield [(("dp", 6), six), (("dp", 1), both)], halves
            four = low(add(block(halves, 4), both[:rows]))
            two = low(add(block(halves, 2), both[rows:]))
            (four, two, one), (halves, six) = (
                yield [(("dp", 4), four), (("dp", 2), two), (("dp", 1), block(halves, 1))],
                (halves, six),
            )
            return out, name, add(block(halves, 0), six, four, two, one)

        if n_dp != 8:
            gather_direct = functools.partial(gather_double, bits=far_first)
            reduce_direct = functools.partial(reduce_halve, own="first")

        def output_chain(own, out, name):
            for bit in reversed(tensor_bits):
                (got,), own = yield [(("tensor", bit), own)], own
                own = jnp.concatenate([own, got], axis=0)
            return out, name, own

        local = self_in_weight.shape[2]
        ff = down_weight.shape[0]
        first = jnp.concatenate([self_in_weight.reshape(shard, 3 * local), self_out_weight.T], axis=1)
        gate_up_own = gate_up_weight.reshape(shard, 2 * ff)
        full = {}

        def gathering(name, own, bits):
            return name, functools.partial(gather_double, out=full, name=name, bits=bits), [own]

        cross_rows = shard + cond_width // n_dp
        start_cross = gathering(
            "cross",
            jnp.concatenate(
                [
                    jnp.concatenate([cross_query_weight, cross_out_weight.T], axis=1),
                    cross_memory_weight.reshape(cond_width // n_dp, 2 * local),
                ],
                axis=0,
            ),
            far_first,
        )
        start_up_a = gathering("up_a", gate_up_own[:, :ff], far_first)
        start_up_b = gathering("up_b", gate_up_own[:, ff:], far_first)
        start_down = gathering("down", down_weight.T, pair_first)
        count = jnp.sum(valid_mask)
        count_row = jnp.zeros((shard,), F32).at[0].set(wide(count // 32)).at[1].set(wide(count % 32))
        gains_own = jnp.concatenate([gain_one, gain_two, gain_three, low(count_row)])[None]
        hidden_raw = tick(
            hidden_in[0],
            "",
            [
                gathering("gains", gains_own, far_first),
                ("first", functools.partial(gather_direct, out=full, name="first"), [first]),
            ],
        )

        pairs = local // PAIR
        rows = length
        mine = slice(0, own_rows)
        row_at = me ^ jnp.array(order, jnp.int32)
        col_at = (dp_me // 2) ^ jnp.array([o // 2 for o in offsets[: n_dp // 2]], jnp.int32)
        side = dp_me % 2

        def arrange_in(x, row_at):
            return arrange(x, row_at, col_at, side, own_rows, shard, BF16, False)

        def take(x, owner):
            return lax.dynamic_slice_in_dim(x, owner * own_rows, own_rows, 0)

        def center(x):
            return wide(x) - jnp.mean(wide(x), axis=-1, keepdims=True)

        def join(halves):
            return jnp.concatenate(halves, axis=0)

        hidden_raw, teacher_raw = tick((hidden_raw, teacher[0]), "gains")
        hidden = arrange_in(hidden_raw, row_at)
        hidden, me_late = tick((hidden, me), "first gains")
        centered = center(hidden)
        inverse_all = lax.rsqrt(jnp.mean(centered * centered, axis=-1, keepdims=True) + epsilon)

        def relative_late(x):
            return jnp.concatenate([take(x, me_late ^ o) for o in order], axis=0)

        position = relative_late(jnp.arange(length, dtype=F32)[:, None])
        lane = jnp.arange(PAIR) % HEAD_DIM
        frequency = jnp.exp((lane % (ROT // 2)).astype(F32) * (-2.0 * math.log(10000.0) / ROT))
        angles = position * frequency[None, :]
        cosine, sine = jnp.cos(angles), jnp.sin(angles)
        tables = (
            jnp.where(lane < ROT, cosine, 1.0),
            jnp.where(lane < ROT // 2, -sine, jnp.where(lane < ROT, sine, 0.0)),
        )
        bias = jnp.where(relative_late(valid_mask[0][:, None]) > 0, 0.0, masked_score)
        cosine, sine, hidden, inverse_all, teacher_raw = tick(
            (*tables, hidden, inverse_all, teacher_raw), "first gains", [start_cross]
        )
        tables = (cosine, sine)
        links.finish("gains")
        gains = jnp.concatenate(full["gains"], axis=0).reshape(n_dp, 4, shard)
        counts = wide(gains[:, 3])
        token_count = jnp.sum(32.0 * counts[:, 0] + counts[:, 1])
        gain_first, gain_second, gain_third = (wide(gains[:, i]).reshape(width) for i in range(3))
        normed_one = low(center(hidden) * inverse_all * gain_first)
        target_low = arrange_in(teacher_raw, me.reshape(1))
        normed_one, target_low, bias = tick(
            (normed_one, target_low, bias), "first cross", [start_up_a, start_down]
        )
        links.finish("first")
        cond_shard = cond_width // n_dp
        place = jnp.arange(cond_width)
        offset = sum(
            ((place // cond_shard >> i) % 2) * bit for i, bit in enumerate(far_first)
        )
        source = (dp_me ^ offset) * cond_shard + place % cond_shard
        cond_place = place[:, None] == source[None, :]
        memory_input = low(dot(conditioning[0], low(cond_place)))
        pad_tokens = -cond_tokens % 16
        cond_rows = cond_tokens + pad_tokens
        cond_bias = jnp.where(jnp.arange(cond_rows)[:, None] < cond_tokens, 0.0, masked_score)

        def branch(*terms):
            return scatter_near(
                lambda start, count, kind: branch_rows(terms, start, count, kind, width), rows
            )

        def of(pieces, places, rows_each=shard):
            return Weight(pieces, places, rows_each)

        far_places, pair_places = came(far_first), came(pair_first)

        def self_attention(normed_one, first, cos, sin, bias):
            first = of(first, came_direct)
            mixed = project_heads(normed_one, first, 3 * local, (cos, sin), 512)
            attended, self_totals = attend_forward(
                mixed, mixed, mixed, 0, pairs, 2 * pairs, bias, pairs, rows
            )
            return mixed, attended, self_totals, branch((attended, first, 3))

        mixed, attended, self_totals, near = stage(
            self_attention, normed_one, full["first"], *tables, bias
        )
        near = tick(near, "cross up_a down_", [start_up_b])

        def add_and_norm(streams, near, gain):
            def work(i, kept, got, far):
                return add_norm(streams[i], kept, got, far, gain, i)

            return exchange(near, work)

        after_self, normed_two = stage(add_and_norm, (hidden, hidden), near, gain_second)
        normed_two = tick(normed_two, "cross up_a up_b")

        links.finish("cross")
        cross_w = [x.reshape(-1, cross_rows, 2 * local) for x in full["cross"]]

        def unpack_memory(cross_w):
            return join([x[:, shard:].reshape(-1, 2 * local) for x in cross_w])

        def cross_attention(normed_two, cross_w):
            memory = dot(memory_input, unpack_memory(cross_w))
            cross_memory = jnp.pad(low(memory), ((0, pad_tokens), (0, 0)))
            weight = of(cross_w, far_places)
            cross_queries = project(normed_two, weight, local, 0)
            cross_attended, cross_totals = attend_forward(
                cross_queries, cross_memory, cross_memory, 0, 0, pairs, cond_bias, pairs, rows
            )
            near = branch((cross_attended, weight, 1))
            return cross_queries, cross_memory, cross_attended, cross_totals, near

        cross_queries, cross_memory, cross_attended, cross_totals, near = stage(
            cross_attention, normed_two, cross_w
        )
        near = tick(near, "up_b down")
        after_cross, normed_three = stage(add_and_norm, after_self, near, gain_third)
        normed_three = tick(normed_three, "up_a down")
        links.finish("up_a")
        gate_value = stage(
            lambda x, w: project(x, of(w, far_places), ff, 0, kind=F32), normed_three, full["up_a"]
        )
        gate_value = tick(gate_value, "up_b")
        links.finish("up_b")
        upward, hidden_units = stage(
            lambda x, w, gate: hidden_forward(x, of(w, far_places), gate),
            normed_three,
            full["up_b"],
            gate_value,
        )
        hidden_units = tick(hidden_units, "down")
        links.finish("down")
        near = stage(lambda x, w: branch((x, of(w, pair_places), 0)), hidden_units, full["down"])

        def final_rows(streams, near, target_low, valid_rows):
            factor = valid_rows * (2.0 * length / token_count)

            def work(i, kept, got, far):
                final, grad, grad_low, loss = final_part(
                    streams[i], kept, got, far, target_low, valid_rows, factor, i
                )
                return (final, jnp.sum(loss), grad), grad_low

            return exchange(near, work)

        valid_rows = wide(take(valid_mask[0][:, None], me))
        finals, grad_final_low = stage(final_rows, after_cross, near, target_low, valid_rows)
        final_low = join([final for final, _, _ in finals])
        losses = sum(loss for _, loss, _ in finals)
        grad_final = [grad for _, _, grad in finals]
        grads = {}

        def half_of(x, y, at):
            return weight_half([(x, y)], at)

        def halves_of(x, y):
            return half_of(x, y, 0), half_of(x, y, 1)

        def reducing(name, halves):
            return name, functools.partial(reduce_halve, out=grads, name=name), list(halves)

        others = {}

        def reducing_far(name, far):
            return (
                name,
                functools.partial(reduce_halve, out=grads, name=name, own=name),
                [far],
            )

        grad_final_low = tick(
            grad_final_low,
            "",
            [
                reducing_far("down", half_of(grad_final_low, hidden_units, 1)),
                (
                    "output",
                    functools.partial(output_chain, out=others, name="output"),
                    [final_low],
                ),
            ],
        )

        def hidden_back(grad_final_low, gate_value, upward, down_w, up_a, up_b):
            grad_gate, grad_up = hidden_backward(
                grad_final_low, of(down_w, pair_places), gate_value, upward
            )
            near = branch(
                (grad_gate, of(up_a, far_places), 0), (grad_up, of(up_b, far_places), 0)
            )
            return grad_gate, grad_up, near

        grad_gate, grad_up, near = stage(
            hidden_back,
            grad_final_low,
            gate_value,
            upward,
            full["down"],
            full["up_a"],
            full["up_b"],
        )

        def back_rows(near, uppers, streams, gain, beside):
            def work(i, kept, got, far):
                total, small, gain_sum = norm_back(uppers[i], kept, got, far, streams[i], gain, i)
                return (total, gain_sum), small

            outs, rows_low, first, second = exchange(near, work, beside)
            return [out for out, _ in outs], sum(x for _, x in outs), rows_low, first, second

        near = tick(
            near, "output", [reducing_far("up_a", half_of(normed_three, grad_gate, 1))]
        )

        def back_three(near, normed_three, grad_gate, grad_up):
            own = half_of(normed_three, grad_up, 0)
            return (
                *back_rows(
                    near,
                    grad_final,
                    after_cross,
                    gain_third,
                    (
                        (
                            half_of(grad_final_low, hidden_units, 0),
                            half_of(normed_three, grad_gate, 0),
                        ),
                        half_of(normed_three, grad_up, 1),
                    ),
                ),
                own,
            )

        grad_after_cross, gain_three_sum, grad_cross_low, owns, far, own = stage(
            back_three, near, normed_three, grad_gate, grad_up
        )
        later["down"], later["up_a"] = owns
        grad_up_b = (own, far)
        grad_cross_low = tick(grad_cross_low, "down output", [reducing("up_b", grad_up_b)])

        def cross_back(grad_cross_low, cross_w):
            weight = of(cross_w, far_places)
            grad_cross_attended = project(grad_cross_low, weight, local, 1)
            grad_cross_queries, grad_keys, grad_values = attend_backward(
                cross_queries,
                cross_memory,
                cross_memory,
                0,
                0,
                pairs,
                cond_bias,
                cross_totals,
                grad_cross_attended,
                None,
                pairs,
                rows,
            )
            near = branch((grad_cross_queries, weight, 0))
            return grad_cross_queries, grad_keys, grad_values, near

        grad_cross_queries, grad_keys, grad_values, near = stage(
            cross_back, grad_cross_low, cross_w
        )

        near = tick(near, "up_a")

        def arrange_out(x, out_type):
            return arrange(x, row_at, col_at, side, own_rows, shard, out_type, True)

        def back_two(
            near, grad_cross_queries, grad_keys, grad_values, grad_cross_low, rows_output
        ):
            grad_memory_low = jnp.concatenate(
                [grad_keys[:cond_tokens], grad_values[:cond_tokens]], axis=1
            )
            cond_part = lax.dot_general(
                dot_nt(grad_memory_low, unpack_memory(cross_w)),
                wide(cond_place),
                (((1,), (1,)), ((), ())),
                precision=lax.Precision.HIGHEST,
            )
            products = ((normed_two, grad_cross_queries), (grad_cross_low, cross_attended))
            if n_dp == 8:
                packed = tuple(
                    weight_half(products, at, (memory_input, grad_memory_low), n_dp // 2)
                    for at in range(2)
                )
            else:
                packed = []
                for at in range(2):
                    memory = half_of(memory_input, grad_memory_low, at)
                    memory = memory.reshape(n_dp // 2, cond_shard, 2, local)
                    memory = memory.transpose(0, 2, 1, 3).reshape(-1, local)
                    packed.append(
                        jnp.concatenate([half_of(x, y, at) for x, y in products] + [memory], axis=1)
                    )
                packed = tuple(packed)
            cond_part = cond_part.reshape(-1, width)
            block_output = arrange_out(rows_output, BF16)
            return back_rows(
                near,
                grad_after_cross,
                after_self,
                gain_second,
                ((packed[0], cond_part), (packed[1], block_output)),
            )

        grad_after_self, gain_two_sum, grad_self_low, (pack_near, cond_part), (pack_far, block_output) = (
            stage(
                back_two,
                near,
                grad_cross_queries,
                grad_keys,
                grad_values,
                grad_cross_low,
                others["output"],
            )
        )
        grad_cross = (pack_near, pack_far)
        grad_self_low = tick(grad_self_low, "up_a down up_b", [reducing("cross", grad_cross)])

        def self_back(grad_self_low, first, cond_part):
            grad_attended = project(grad_self_low, of(first, came_direct), local, 3)
            grad_parts = attend_backward(
                mixed,
                mixed,
                mixed,
                0,
                pairs,
                2 * pairs,
                bias,
                self_totals,
                grad_attended,
                tables,
                pairs,
                rows,
            )
            return list(grad_parts), first_half(grad_parts, 1), sum_tensor(cond_part)

        def first_half(grad_parts, at):
            products = [(normed_one, part) for part in grad_parts] + [(grad_self_low, attended)]
            return weight_half(products, at)

        grad_mixed, grad_first, cond_sum = stage(
            self_back, grad_self_low, full["first"], cond_part
        )
        grad_mixed = tick(
            grad_mixed,
            "up_a down up_b cross",
            [("first", functools.partial(reduce_direct, out=grads, name="first"), [grad_first])],
        )

        def self_branch(grad_mixed, first):
            near = branch(*((part, of(first, came_direct), i) for i, part in enumerate(grad_mixed)))
            return near, first_half(grad_mixed, 0)

        near, later["first"] = stage(self_branch, grad_mixed, full["first"])
        near = tick(near, "first cross up_b")

        def small_sums(gain_one_sum):
            sums = jnp.stack([gain_one_sum, gain_two_sum, gain_three_sum]).reshape(3, n_dp, shard)
            sums = jnp.concatenate(
                [sums.transpose(1, 0, 2).reshape(n_dp, 3 * shard), jnp.full((n_dp, shard), losses)],
                axis=1,
            )
            for bit in near_first:
                half = sums.shape[0] // 2
                sums = sums[:half] + swap_dp(sums[half:], bit)
            return sum_tensor(sums)[0]

        links.finish("up_a", "up_b")

        def back_one(near, up_a, up_b):
            _, gain_one_sum, rows_hidden, grad_gate_up, _ = back_rows(
                near,
                grad_after_self,
                (hidden, hidden),
                gain_first,
                (jnp.stack([up_a, up_b], axis=1), gain_two_sum),
            )
            return rows_hidden, gain_one_sum, grad_gate_up

        rows_hidden, gain_one_sum, grad_gate_up = stage(
            back_one, near, grads["up_a"], grads["up_b"]
        )
        rows_hidden, gain_one_sum = tick(
            (rows_hidden, gain_one_sum), "first cross"
        )

        def last(rows_hidden, gain_one_sum):
            return small_sums(gain_one_sum), arrange_out(rows_hidden, F32)

        sums, grad_hidden = stage(last, rows_hidden, gain_one_sum)
        sums, grad_hidden = tick((sums, grad_hidden), "first")
        links.finish(*list(links.flying))

        grad_conditioning = cond_sum.reshape(cond_tokens, cond_width)
        mean_loss = sums[3 * shard] / (token_count * width)

        return (
            mean_loss,
            block_output[None],
            grad_hidden[None],
            grad_conditioning[None],
            sums[:shard],
            sums[shard : 2 * shard],
            sums[2 * shard : 3 * shard],
            grads["first"][:, : 3 * local].reshape(shard, 3, local),
            grads["first"][:, 3 * local :].T,
            grads["cross"][:, :local],
            jnp.stack(
                [grads["cross"][:cond_shard, 2 * local :], grads["cross"][cond_shard:, 2 * local :]],
                axis=1,
            ),
            grads["cross"][:, local : 2 * local].T,
            grad_gate_up,
            grads["down"].T,
        )

    return body


def solution(mesh):
    return jax.shard_map(
        build(mesh.shape["dp"], mesh.shape["tensor"]),
        mesh=mesh,
        in_specs=(
            P("dp", None, None),
            P("dp", None, None),
            P("dp", None),
            P("dp", None, None),
            P("dp"),
            P("dp"),
            P("dp"),
            P("dp", None, "tensor"),
            P("tensor", "dp"),
            P("dp", "tensor"),
            P("dp", None, "tensor"),
            P("tensor", "dp"),
            P("dp", None, "tensor"),
            P("tensor", "dp"),
        ),
        out_specs=(
            P(),
            P("dp", None, None),
            P("dp", None, None),
            P("dp", None, None),
            P("dp"),
            P("dp"),
            P("dp"),
            P("dp", None, "tensor"),
            P("tensor", "dp"),
            P("dp", "tensor"),
            P("dp", None, "tensor"),
            P("tensor", "dp"),
            P("dp", None, "tensor"),
            P("tensor", "dp"),
        ),
        check_vma=False,
    )
```
